32 devices in a mesh: space: 8 (over z, y), samp: 4 (over x, core).
Axes of the slice: x: 2, y: 2, z: 4, core: 2. Of those that a mesh axis runs over, the one named last changes fastest.
Arguments:
- volume: bfloat16 [4, 32, 32, 256], P(None, 'space', 'samp'), may hold values from -6 to 6
- filters_one: bfloat16 [1728], P('samp'), may hold values from -0.625 to 0.625
- filters_two: bfloat16 [13824], P('space'), may hold values from -0.3125 to 0.3125
- cotangent: bfloat16 [32, 32, 32, 256], P(None, 'space', 'samp'), may hold values from -6 to 6
Outputs:
- activation: bfloat16 [32, 32, 32, 256], P(None, 'space', 'samp')
- grad_one: float32 [1728], P('samp')
- grad_two: float32 [13824], P('space')
The draws below stay inside these ranges and needn't reach their ends.
All inputs are finite; a program needn't handle non-finite values.
Results may differ from the reference program's by a relative error of at most 0.0044.
The reference program's roundings to bfloat16 on the way count: a program that leaves them out, or rounds other values in their place, can miss the bound.
Values may be sent and summed in bfloat16 or wider, within the bound.
A program may use at most 64 MiB of HBM per device.

```python
import math
import jax
import jax.numpy as jnp
from jax import lax

CIN = 4
C1 = 16
C2 = 32
CZ = 256
NX = 32
NY = 32


def shard_levels(key, shape, cuts, least, top_value):
    factor_of = 1.0
    for position, blocks in cuts:
        heights = jax.random.uniform(jax.random.fold_in(jax.random.fold_in(key, 6), position), (blocks,), jnp.float32, least / len(cuts), top_value / len(cuts))
        factor_of = factor_of * jnp.repeat(jnp.exp(heights), shape[position] // blocks).reshape((-1,) + (1,) * (len(shape) - 1 - position))
    return factor_of


def noise(stream_key, dims, spread, bound, shards=(), dtype=jnp.bfloat16):
    values = jax.random.normal(stream_key, dims, jnp.float32) * spread
    if len(shards) > 0:
        values = shard_levels(stream_key, dims, shards, -0.22, 0.18) * values
    return jnp.clip(values, min=-bound, max=bound).astype(dtype)


def setup_inputs(seed: int = 0) -> dict:
    arg_keys = jax.random.split(jax.random.key(seed), 5)
    volume = noise(arg_keys[0], (CIN, NX, NY, CZ), 1.0, 6.0, ((1, 8), (2, 4)))
    filters_one = noise(arg_keys[1], (27 * CIN * C1,), (27 * CIN) ** -0.5, 0.625, ((0, 4),))
    filters_two = noise(arg_keys[2], (27 * C1 * C2,), (27 * C1) ** -0.5, 0.3125, ((0, 8),))
    cotangent = noise(arg_keys[3], (C2, NX, NY, CZ), 1.0, 6.0, ((1, 8), (2, 4)))
    return {"volume": volume, "filters_one": filters_one, "filters_two": filters_two, "cotangent": cotangent}


SLOPE = 0.3

def conv_valid(padded, kernel):
    result = lax.conv_general_dilated(padded[None], kernel, (1, 1, 1), 'VALID', dimension_numbers=('NCDHW', 'OIDHW', 'NCDHW'), preferred_element_type=jnp.float32)
    return result[0]

def kernel_grad(grad_out, padded):
    chans_out = grad_out.shape[0]
    chans_in = padded.shape[0]
    size_x, size_y, size_z = (grad_out.shape[1], grad_out.shape[2], grad_out.shape[3])
    flat_out = grad_out.reshape(chans_out, -1)
    pieces = []
    for shift_x in range(3):
        for shift_y in range(3):
            for shift_z in range(3):
                window = padded[:, shift_x:shift_x + size_x, shift_y:shift_y + size_y, shift_z:shift_z + size_z].reshape(chans_in, -1)
                pieces.append(lax.dot_general(flat_out, window, (((1,), (1,)), ((), ())), preferred_element_type=jnp.float32))
    return jnp.stack(pieces, axis=-1).reshape(-1)

def leaky(values):
    return jnp.where(values > 0, values, SLOPE * values)

def slope_of(values):
    return jnp.where(values > 0, jnp.float32(1.0), jnp.float32(SLOPE))

def pad_all(field):
    return jnp.pad(field, ((0, 0), (1, 1), (1, 1), (1, 1)))

def reference(volume, filters_one, filters_two, cotangent):
    kernel_one = filters_one.reshape(C1, CIN, 3, 3, 3)
    kernel_two = filters_two.reshape(C2, C1, 3, 3, 3)
    volume_pad = pad_all(volume)
    pre_one = conv_valid(volume_pad, kernel_one)
    hidden = leaky(pre_one).astype(jnp.bfloat16)
    hidden_pad = pad_all(hidden)
    pre_two = conv_valid(hidden_pad, kernel_two)
    activation = leaky(pre_two).astype(jnp.bfloat16)
    back_two = (cotangent.astype(jnp.float32) * slope_of(pre_two)).astype(jnp.bfloat16)
    flipped = jnp.flip(kernel_two, (2, 3, 4)).transpose(1, 0, 2, 3, 4)
    dhidden = conv_valid(pad_all(back_two), flipped)
    back_one = (dhidden * slope_of(pre_one)).astype(jnp.bfloat16)
    scale = 1.0 / math.sqrt(float(NX * NY * CZ))
    grad_two = kernel_grad(back_two, hidden_pad) * scale
    grad_one = kernel_grad(back_one, volume_pad) * scale
    return (activation, grad_one, grad_two)
```

```python
import functools
import math

import jax
import jax.numpy as jnp
from jax import lax
from jax.experimental import pallas as pl
from jax.experimental.pallas import tpu as pltpu
from jax.sharding import PartitionSpec as P

CIN = 4
C1 = 16
C2 = 32
SLOPE = 0.3
MESH = pl.DeviceIdType.MESH
F32 = jnp.float32
BF16 = jnp.bfloat16
DIRS = [(dx, dy) for dx in (-1, 0, 1) for dy in (-1, 0, 1) if (dx, dy) != (0, 0)]


def spans(delta, size, width):
    if delta == 1:
        return (size - width, width), (0, width)
    if delta == -1:
        return (0, width), (size + width, width)
    return (0, size), (width, size)


def leaky(values):
    return jnp.where(values > 0, values, SLOPE * values)


def tap_sum(t, rows, lane, last):
    low = jnp.where(lane == 0, 0.0, pltpu.roll(t[:rows], 1, axis=1))
    high = jnp.where(lane == last, 0.0, pltpu.roll(t[2 * rows :], last, axis=1))
    return t[rows : 2 * rows] + low + high


def tap_spread(b, lane, last):
    low = jnp.where(lane == last, 0.0, pltpu.roll(b, last, axis=1))
    high = jnp.where(lane == 0, 0.0, pltpu.roll(b, 1, axis=1))
    return jnp.concatenate([low, b, high], axis=0)


def dot(a, b):
    return lax.dot_general(a, b, (((1,), (0,)), ((), ())), preferred_element_type=F32)


def dot_nt(a, b):
    return lax.dot_general(a, b, (((1,), (1,)), ((), ())), preferred_element_type=F32)


def one_hot(rows, source):
    row = lax.broadcasted_iota(jnp.int32, (rows, source.shape[1]), 0)
    return jnp.where(row == source, 1.0, 0.0).astype(BF16)


def one_hot_rows(chans, size_y):
    r = lax.broadcasted_iota(jnp.int32, (chans * size_y, chans * size_y), 0)
    q = lax.broadcasted_iota(jnp.int32, (chans * size_y, chans * size_y), 1)
    return jnp.where(q == (r % chans) * size_y + r // chans, 1.0, 0.0).astype(BF16)


def build_selectors(q1, q2, q3):
    lane = lax.broadcasted_iota(jnp.int32, (1, 256), 1)
    kx, ky, i = lane >> 6, (lane >> 2) & 15, lane & 3
    source1 = jnp.where((kx < 3) & (ky < 3), i * 27 + kx * 9 + ky * 3, -9)
    kx, ky, i = lane >> 6, (lane >> 4) & 3, lane & 15
    source2 = jnp.where((kx < 3) & (ky < 3), i * 27 + kx * 9 + ky * 3, -9)
    for kz in range(3):
        q1[kz] = one_hot(27 * CIN, source1 + kz)
        q2[kz] = one_hot(27 * C1, source2 + kz)
    lane = lax.broadcasted_iota(jnp.int32, (1, 128), 1)
    kz, i = lane >> 4, lane & 15
    for kx in range(3):
        for ky in range(3):
            source3 = jnp.where(kz < 3, i * 27 + (2 - kx) * 9 + (2 - ky) * 3 + 2 - kz, -9)
            q3[3 * kx + ky] = one_hot(27 * C1, source3)


def gather_rows(all_ref, rows_ref, wide_ref):
    owners, count, unit = all_ref.shape
    for j in range(owners):
        rows_ref[count * j : count * (j + 1)] = all_ref[j].astype(F32)
    split = wide_ref.shape[1] // unit
    if split == 1:
        return rows_ref[...].astype(BF16)
    for k in range(split):
        wide_ref[:, unit * k : unit * (k + 1)] = rows_ref[pl.ds(k, wide_ref.shape[0], stride=split)]
    return wide_ref[...].astype(BF16)


def scatter_rows(value, rows_ref, wide_ref, out_ref):
    owners, count, unit = out_ref.shape
    split = value.shape[1] // unit
    if split == 1:
        rows_ref[...] = value
    else:
        wide_ref[...] = value
        for k in range(split):
            rows_ref[pl.ds(k, value.shape[0], stride=split)] = wide_ref[:, unit * k : unit * (k + 1)]
    for j in range(owners):
        out_ref[j] = rows_ref[count * j : count * (j + 1)]


def flat_order(grad, q, chans):
    result = 0.0
    for kz in range(3):
        g = grad[chans * kz : chans * (kz + 1)]
        high = g.astype(BF16)
        rest = g - high.astype(F32)
        mid = rest.astype(BF16)
        low = (rest - mid.astype(F32)).astype(BF16)
        r = dot_nt(jnp.concatenate([high, mid, low], axis=0), q[kz])
        result = result + (r[:chans] + r[chans : 2 * chans] + r[2 * chans :])
    return result


def fused_kernel(
    n_space, n_samp, scale, v_ref, c_ref, f1_ref, f2_ref, act_ref, o1_ref, o2_ref,
    vp, cp, all1, all2,
    turn, a1, a2, a3, hid, back, pre, t1, perm, acc1, acc2, act,
    q1, q2, q3, rows1, wide1, rows2, wide2, tall3, vf, vrows,
    grad1, grad2, part1, part2, full2, mine2,
    send_v, recv_v, send_1, recv_1, send_2, recv_2,
    send_a1, recv_a1, send_a2, recv_a2, send_b2, recv_b2,
):
    s = lax.axis_index("space")
    m = lax.axis_index("samp")
    size_x, size_y, size_z = v_ref.shape[1:]

    vp[...] = jnp.zeros_like(vp)

    def there(dx, dy):
        return (s + dx >= 0) & (s + dx < n_space) & (m + dy >= 0) & (m + dy < n_samp)

    barrier = pltpu.get_barrier_semaphore()
    peers = n_samp - 1 + n_space - 1
    for dx, dy in DIRS:
        if dx == 0 or dy == 0:
            continue
        peers = peers + jnp.where(there(dx, dy), 1, 0)

        @pl.when(there(dx, dy))
        def _():
            pl.semaphore_signal(barrier, inc=1, device_id=(s + dx, m + dy), device_id_type=MESH)
    for k in range(1, n_samp):
        pl.semaphore_signal(barrier, inc=1, device_id=(s, lax.rem(m + k, n_samp)), device_id_type=MESH)

    def greet(k, carry):
        pl.semaphore_signal(barrier, inc=1, device_id=(lax.rem(s + k, n_space), m), device_id_type=MESH)
        return carry

    lax.fori_loop(1, n_space, greet, 0)

    turn_v = one_hot_rows(CIN, size_y)

    def centre(x, carry):
        value = v_ref[:, x].astype(F32).reshape(CIN * size_y, size_z).astype(BF16)
        value = dot(turn_v, value)
        for y in range(size_y):
            vp[x + 2, y + 2] = value[CIN * y : CIN * (y + 1)].astype(BF16)
        return carry

    lax.fori_loop(0, size_x, centre, 0)
    pl.semaphore_wait(barrier, peers)

    def copy_1(k):
        return pltpu.make_async_remote_copy(
            src_ref=f1_ref, dst_ref=all1.at[m], send_sem=send_1.at[k], recv_sem=recv_1.at[k],
            device_id=(s, lax.rem(m + k, n_samp)), device_id_type=MESH)

    def copy_2(k):
        return pltpu.make_async_remote_copy(
            src_ref=f2_ref, dst_ref=all2.at[s], send_sem=send_2.at[k], recv_sem=recv_2.at[k],
            device_id=(lax.rem(s + k, n_space), m), device_id_type=MESH)

    def halo(src, dst, width, send, recv, slot, dx, dy):
        (sx, nx), (tx, _) = spans(dx, size_x, width)
        (sy, ny), (ty, _) = spans(dy, size_y, width)
        return pltpu.make_async_remote_copy(
            src_ref=src.at[pl.ds(sx + width, nx), pl.ds(sy + width, ny)], dst_ref=dst.at[pl.ds(tx, nx), pl.ds(ty, ny)],
            send_sem=send.at[slot], recv_sem=recv.at[slot],
            device_id=(jnp.clip(s + dx, 0, n_space - 1), jnp.clip(m + dy, 0, n_samp - 1)),
            device_id_type=MESH)

    vol = [halo(vp, vp, 2, send_v, recv_v, j, dx, dy) for j, (dx, dy) in enumerate(DIRS)]
    for k in range(1, n_samp):
        copy_1(k).start()

    def start_2(k, carry):
        copy_2(k).start()
        return carry

    lax.fori_loop(1, n_space, start_2, 0)
    for copy, (dx, dy) in zip(vol, DIRS):
        @pl.when(there(dx, dy))
        def _():
            copy.start()

    all1[m] = f1_ref[...]
    all2[s] = f2_ref[...]
    last = size_z - 1
    high_y = size_y + 2

    def lanes(rows):
        return lax.broadcasted_iota(jnp.int32, (rows, size_z), 1)

    lane1 = lanes(C1)
    lane2 = lanes(C2)
    build_selectors(q1, q2, q3)
    turn[...] = one_hot_rows(C2, size_y)

    def turn_c(x, carry):
        value = c_ref[:, x].astype(F32).reshape(C2 * size_y, size_z).astype(BF16)
        cp[x] = dot(turn[...], value).astype(BF16).reshape(size_y, C2, size_z)
        return carry

    lax.fori_loop(0, size_x, turn_c, 0)

    def clear(x, carry):
        back[x] = jnp.zeros(back.shape[1:], back.dtype)
        return carry

    lax.fori_loop(0, back.shape[0], clear, 0)
    r = lax.broadcasted_iota(jnp.int32, (C2 * size_y, C2 * size_y), 0)
    q = lax.broadcasted_iota(jnp.int32, (C2 * size_y, C2 * size_y), 1)
    from_row = (r % size_y) * C2 + r // size_y
    perm[...] = jnp.where(q == from_row, 1.0, 0.0).astype(BF16)
    acc1[...] = jnp.zeros_like(acc1)
    acc2[...] = jnp.zeros_like(acc2)
    tall3[...] = jnp.zeros_like(tall3)

    def over_space(body):
        def step(k, carry):
            body(k)
            return carry

        lax.fori_loop(1, n_space, step, 0)

    def arrive(group):
        for copy, (dx, dy) in zip(group, DIRS):
            @pl.when(there(-dx, -dy))
            def _():
                copy.wait_recv()

            @pl.when(there(dx, dy))
            def _():
                copy.wait_send()

    for k in range(1, n_samp):
        copy_1(k).wait()
    over_space(lambda k: copy_2(k).wait())
    m1 = gather_rows(all1, rows1, wide1)
    m2 = gather_rows(all2, rows2, wide2)
    base1 = jnp.concatenate([dot(m1, q1[kz]) for kz in range(3)], axis=0)
    base2 = jnp.concatenate([dot(m2, q2[kz]) for kz in range(3)], axis=0)
    for kx in range(3):
        for ky in range(3):
            first = 128 * kx + C2 * ky
            tall3[first : first + C2] = dot(m2, q3[3 * kx + ky])
    base3 = tall3[...].T[:48]
    for y in range(high_y):
        row = base1 if y == 0 else pltpu.roll(base1, 4 * y, axis=1)
        a1[48 * y : 48 * y + 48] = row[:, :192].astype(BF16)
    a2[:96] = base2[:, :192].astype(BF16)
    a2[96:] = pltpu.roll(base2, 16, axis=1)[:, :192].astype(BF16)
    a3[:48] = base3.astype(BF16)
    a3[48:] = pltpu.roll(base3, 32, axis=1).astype(BF16)

    arrive(vol)

    def lift(x, carry):
        for y in range(vp.shape[1]):
            vf[CIN * y : CIN * (y + 1)] = vp[x, y].astype(F32)
        vrows[x] = vf[...].astype(BF16)
        return carry

    lax.fori_loop(0, vp.shape[0], lift, 0)

    def vwin(x):
        return jnp.concatenate([vrows[x], vrows[x + 1], vrows[x + 2]], axis=0)

    def layer1(x, carry):
        gx = s * size_x + x - 1
        ok_x = (gx >= 0) & (gx < n_space * size_x)
        t1[...] = dot(a1[...], vwin(x))
        for y in range(high_y):
            gy = m * size_y + y - 1
            ok = ok_x & (gy >= 0) & (gy < n_samp * size_y)
            p = tap_sum(t1[48 * y : 48 * y + 48], C1, lane1, last)
            pre[x, 16 * y : 16 * y + 16] = p
            h = leaky(p) * jnp.where(ok, 1.0, 0.0)
            hid[x, 16 * y : 16 * y + 16] = h.astype(BF16)
        return carry

    lax.fori_loop(0, size_x + 2, layer1, 0)

    def hwin(x, y):
        return jnp.concatenate([hid[x + k, 16 * y : 16 * y + 64] for k in range(3)], axis=0)

    def pre_two(t, half):
        return tap_sum(t[96 * half : 96 * half + 96], C2, lane2, last)

    def back_two(x, y, p):
        b = (cp[x, y].astype(F32) * jnp.where(p > 0, 1.0, SLOPE)).astype(BF16)
        back[x + 2, C2 * (y + 2) : C2 * (y + 3)] = b
        return b

    def layer2(x, carry):
        moved, windows = [], []
        for y in range(0, size_y, 2):
            win = hwin(x, y)
            t = dot(a2[...], win)
            both = []
            for half in range(2):
                p = pre_two(t, half)
                act[C2 * (y + half) : C2 * (y + half + 1)] = leaky(p).astype(BF16)
                b = back_two(x, y + half, p)
                both.append(tap_spread(b.astype(F32), lane2, last).astype(BF16))
            moved.append(jnp.concatenate(both, axis=0))
            windows.append(win)
        acc2[...] += dot_nt(jnp.concatenate(moved, axis=1), jnp.concatenate(windows, axis=1))
        value = dot(perm[...], act[...])
        act_ref[:, x] = value.reshape(C2, size_y, size_z).astype(BF16)
        return carry

    lax.fori_loop(0, size_x, layer2, 0)

    def wide(values, rows):
        return jnp.concatenate([values, jnp.zeros((rows, 64), F32)], axis=1)

    def samp_peer(k):
        return lax.rem(m + k, n_samp)

    def space_peer(k):
        return lax.rem(s + k, n_space)

    def first_2(k):
        return pltpu.make_async_remote_copy(
            src_ref=grad2.at[space_peer(k)], dst_ref=part2.at[s], send_sem=send_a2.at[k],
            recv_sem=recv_a2.at[k], device_id=(space_peer(k), m), device_id_type=MESH)

    def second_2(k):
        return pltpu.make_async_remote_copy(
            src_ref=mine2, dst_ref=full2.at[m], send_sem=send_b2.at[k],
            recv_sem=recv_b2.at[k], device_id=(s, samp_peer(k)), device_id_type=MESH)

    total2 = wide(acc2[:96], 96) + pltpu.roll(wide(acc2[96:], 96), 256 - 16, axis=1)
    scatter_rows(flat_order(total2, q2, C2), rows2, wide2, grad2)
    over_space(lambda k: first_2(k).start())
    part2[s] = grad2[s]

    def finish(x, carry):
        gx = s * size_x + x - 1
        ok_x = (gx >= 0) & (gx < n_space * size_x)
        pieces = []
        for y in range(0, high_y, 2):
            win = jnp.concatenate([back[x + k, C2 * y : C2 * y + 128] for k in range(3)], axis=0)
            t = dot(a3[...], win)
            for half in range(2):
                gy = m * size_y + y + half - 1
                ok = ok_x & (gy >= 0) & (gy < n_samp * size_y)
                d = tap_sum(t[48 * half : 48 * half + 48], C1, lane1, last)
                p = pre[x, 16 * (y + half) : 16 * (y + half) + 16]
                slope = jnp.where(p > 0, 1.0, SLOPE) * jnp.where(ok, 1.0, 0.0)
                b1 = (d * slope).astype(BF16).astype(F32)
                pieces.append(tap_spread(b1, lane1, last).astype(BF16))
        acc1[...] += dot_nt(jnp.concatenate(pieces, axis=0), vwin(x))
        return carry

    lax.fori_loop(0, size_x + 2, finish, 0)

    total1 = jnp.zeros((48, 256), F32)
    for y in range(high_y):
        total1 = total1 + pltpu.roll(wide(acc1[48 * y : 48 * y + 48], 48), (256 - 4 * y) % 256, axis=1)
    scatter_rows(flat_order(total1, q1, C1), rows1, wide1, grad1)

    everyone = n_space * n_samp
    me = s * n_samp + m

    def to_all(k, carry):
        peer = lax.rem(me + k, everyone)
        ps, pm = peer // n_samp, lax.rem(peer, n_samp)
        pltpu.make_async_remote_copy(
            src_ref=grad1.at[pm], dst_ref=part1.at[me], send_sem=send_a1, recv_sem=recv_a1,
            device_id=(ps, pm), device_id_type=MESH).start()
        return carry

    lax.fori_loop(1, everyone, to_all, 0)
    part1[me] = grad1[m]
    over_space(lambda k: first_2(k).wait())
    mine2[...] = jnp.sum(part2[...], axis=0)
    for k in range(1, n_samp):
        second_2(k).start()
    full2[m] = mine2[...]
    for k in range(1, n_samp):
        second_2(k).wait()
    o2_ref[...] = jnp.sum(full2[...], axis=0) * scale
    others = part1.at[pl.ds(0, everyone - 1)]
    pltpu.make_async_copy(others, others, send_a1).wait()
    pltpu.make_async_copy(others, others, recv_a1).wait()
    o1_ref[...] = jnp.sum(part1[...], axis=0) * scale


VMEM = pl.BlockSpec(memory_space=pltpu.VMEM)


def on_device(n_space, n_samp, volume, filters_one, filters_two, cotangent):
    _, size_x, size_y, size_z = volume.shape
    len1 = filters_one.shape[0]
    len2 = filters_two.shape[0]
    unit1 = math.gcd(len1, 27 * CIN)
    unit2 = math.gcd(len2, 27 * C1)
    piece1 = (len1 // unit1, unit1)
    piece2 = (len2 // unit2, unit2)
    high_y = size_y + 2
    scale = 1.0 / math.sqrt(float(size_x * n_space * size_y * n_samp * size_z))
    samp, space = pltpu.SemaphoreType.DMA((n_samp,)), pltpu.SemaphoreType.DMA((n_space,))
    sides = pltpu.SemaphoreType.DMA((8,))
    activation, out1, out2 = pl.pallas_call(
        functools.partial(fused_kernel, n_space, n_samp, scale),
        out_shape=[
            jax.ShapeDtypeStruct((C2, size_x, size_y, size_z), BF16),
            jax.ShapeDtypeStruct(piece1, F32),
            jax.ShapeDtypeStruct(piece2, F32),
        ],
        in_specs=[VMEM] * 4,
        out_specs=[VMEM] * 3,
        scratch_shapes=[
            pltpu.VMEM((size_x + 4, size_y + 8, CIN, size_z), BF16),
            pltpu.VMEM((size_x, size_y, C2, size_z), BF16),
            pltpu.VMEM((n_samp, *piece1), BF16),
            pltpu.VMEM((n_space, *piece2), BF16),
            pltpu.VMEM((C2 * size_y, C2 * size_y), BF16),
            pltpu.VMEM((48 * high_y, 192), BF16),
            pltpu.VMEM((192, 192), BF16),
            pltpu.VMEM((96, 384), BF16),
            pltpu.VMEM((size_x + 2, 16 * high_y, size_z), BF16),
            pltpu.VMEM((size_x + 4, C2 * (size_y + 4), size_z), BF16),
            pltpu.VMEM((size_x + 2, 16 * high_y, size_z), F32),
            pltpu.VMEM((48 * high_y, size_z), F32),
            pltpu.VMEM((C2 * size_y, C2 * size_y), BF16),
            pltpu.VMEM((48 * high_y, 192), F32),
            pltpu.VMEM((192, 192), F32),
            pltpu.VMEM((C2 * size_y, size_z), BF16),
            pltpu.VMEM((3, 27 * CIN, 256), BF16),
            pltpu.VMEM((3, 27 * C1, 256), BF16),
            pltpu.VMEM((9, 27 * C1, 128), BF16),
            pltpu.VMEM((n_samp * piece1[0], piece1[1]), F32),
            pltpu.VMEM((C1, 27 * CIN), F32),
            pltpu.VMEM((n_space * piece2[0], piece2[1]), F32),
            pltpu.VMEM((C2, 27 * C1), F32),
            pltpu.VMEM((384, 128), F32),
            pltpu.VMEM((CIN * (size_y + 8), size_z), F32),
            pltpu.VMEM((size_x + 4, CIN * (size_y + 8), size_z), BF16),
            pltpu.VMEM((n_samp, *piece1), F32),
            pltpu.VMEM((n_space, *piece2), F32),
            pltpu.VMEM((n_space * n_samp, *piece1), F32),
            pltpu.VMEM((n_space, *piece2), F32),
            pltpu.VMEM((n_samp, *piece2), F32),
            pltpu.VMEM(piece2, F32),
            sides, sides, samp, samp, space, space,
            pltpu.SemaphoreType.DMA, pltpu.SemaphoreType.DMA, space, space, samp, samp,
        ],
        compiler_params=pltpu.CompilerParams(
            collective_id=0, has_side_effects=True, vmem_limit_bytes=48 * 2**20),
    )(volume, cotangent,
      filters_one.reshape(piece1), filters_two.reshape(piece2))
    return activation, out1.reshape(len1), out2.reshape(len2)


def solution(mesh):
    in_specs = (
        P(None, "space", "samp", None),
        P("samp"),
        P("space"),
        P(None, "space", "samp", None),
    )
    out_specs = (P(None, "space", "samp", None), P("samp"), P("space"))
    return jax.shard_map(
        functools.partial(on_device, mesh.shape["space"], mesh.shape["samp"]),
        mesh=mesh, in_specs=in_specs, out_specs=out_specs, check_vma=False,
    )
```

```python
import functools
import math

import jax
import jax.numpy as jnp
from jax import lax
from jax.experimental import pallas as pl
from jax.experimental.pallas import tpu as pltpu
from jax.sharding import PartitionSpec as P

CIN = 4
C1 = 16
C2 = 32
SLOPE = 0.3
MESH = pl.DeviceIdType.MESH
F32 = jnp.float32
BF16 = jnp.bfloat16
DIRS = [(dx, dy) for dx in (-1, 0, 1) for dy in (-1, 0, 1) if (dx, dy) != (0, 0)]


def spans(delta, size, width):
    if delta == 1:
        return (size - width, width), (0, width)
    if delta == -1:
        return (0, width), (size + width, width)
    return (0, size), (width, size)


def leaky(values):
    return jnp.where(values > 0, values, SLOPE * values)


def tap_sum(t, rows, lane, last):
    low = jnp.where(lane == 0, 0.0, pltpu.roll(t[:rows], 1, axis=1))
    high = jnp.where(lane == last, 0.0, pltpu.roll(t[2 * rows :], last, axis=1))
    return t[rows : 2 * rows] + low + high


def tap_spread(b, lane, last):
    low = jnp.where(lane == last, 0.0, pltpu.roll(b, last, axis=1))
    high = jnp.where(lane == 0, 0.0, pltpu.roll(b, 1, axis=1))
    return jnp.concatenate([low, b, high], axis=0)


def dot(a, b):
    return lax.dot_general(a, b, (((1,), (0,)), ((), ())), preferred_element_type=F32)


def dot_nt(a, b):
    return lax.dot_general(a, b, (((1,), (1,)), ((), ())), preferred_element_type=F32)


def one_hot(rows, source):
    row = lax.broadcasted_iota(jnp.int32, (rows, source.shape[1]), 0)
    return jnp.where(row == source, 1.0, 0.0).astype(BF16)


def one_hot_rows(chans, size_y):
    r = lax.broadcasted_iota(jnp.int32, (chans * size_y, chans * size_y), 0)
    q = lax.broadcasted_iota(jnp.int32, (chans * size_y, chans * size_y), 1)
    return jnp.where(q == (r % chans) * size_y + r // chans, 1.0, 0.0).astype(BF16)


def build_selectors(q1, q2, q3):
    lane = lax.broadcasted_iota(jnp.int32, (1, 256), 1)
    kx, ky, i = lane >> 6, (lane >> 2) & 15, lane & 3
    source1 = jnp.where((kx < 3) & (ky < 3), i * 27 + kx * 9 + ky * 3, -9)
    kx, ky, i = lane >> 6, (lane >> 4) & 3, lane & 15
    source2 = jnp.where((kx < 3) & (ky < 3), i * 27 + kx * 9 + ky * 3, -9)
    for kz in range(3):
        q1[kz] = one_hot(27 * CIN, source1 + kz)
        q2[kz] = one_hot(27 * C1, source2 + kz)
    lane = lax.broadcasted_iota(jnp.int32, (1, 128), 1)
    kz, i = lane >> 4, lane & 15
    for kx in range(3):
        for ky in range(3):
            source3 = jnp.where(kz < 3, i * 27 + (2 - kx) * 9 + (2 - ky) * 3 + 2 - kz, -9)
            q3[3 * kx + ky] = one_hot(27 * C1, source3)


def split_rows(flat_ref, rows_ref):
    rows, unit = rows_ref.shape
    flat = flat_ref[...].astype(F32).reshape(1, rows * unit)
    rows_ref[...] = jnp.concatenate(
        [flat[:, unit * k : unit * (k + 1)] for k in range(rows)], axis=0).astype(BF16)


def flatten(rows):
    return jnp.concatenate([rows[k : k + 1] for k in range(rows.shape[0])], axis=1).reshape(rows.size)


def gather_rows(all_ref, rows_ref, wide_ref):
    owners, count, unit = all_ref.shape
    for j in range(owners):
        rows_ref[count * j : count * (j + 1)] = all_ref[j].astype(F32)
    split = wide_ref.shape[1] // unit
    if split == 1:
        return rows_ref[...].astype(BF16)
    for k in range(split):
        wide_ref[:, unit * k : unit * (k + 1)] = rows_ref[pl.ds(k, wide_ref.shape[0], stride=split)]
    return wide_ref[...].astype(BF16)


def scatter_rows(value, rows_ref, wide_ref, out_ref):
    owners, count, unit = out_ref.shape
    split = value.shape[1] // unit
    if split == 1:
        rows_ref[...] = value
    else:
        wide_ref[...] = value
        for k in range(split):
            rows_ref[pl.ds(k, value.shape[0], stride=split)] = wide_ref[:, unit * k : unit * (k + 1)]
    for j in range(owners):
        out_ref[j] = rows_ref[count * j : count * (j + 1)]


def flat_order(grad, q, chans):
    result = 0.0
    for kz in range(3):
        g = grad[chans * kz : chans * (kz + 1)]
        high = g.astype(BF16)
        rest = g - high.astype(F32)
        mid = rest.astype(BF16)
        low = (rest - mid.astype(F32)).astype(BF16)
        r = dot_nt(jnp.concatenate([high, mid, low], axis=0), q[kz])
        result = result + (r[:chans] + r[chans : 2 * chans] + r[2 * chans :])
    return result


def fused_kernel(
    n_space, n_samp, scale, v_hbm, c_hbm, f1_hbm, f2_hbm, act_ref, o1_ref, o2_ref,
    v_ref, c_ref, f1_flat, f2_flat, f1_ref, f2_ref, load,
    vp, cp, all1, all2,
    turn, a1, a2, a3, hid, back, pre, t1, perm, acc1, acc2, act,
    q1, q2, q3, rows1, wide1, rows2, wide2, tall3, vf, vrows,
    grad1, grad2, part1, part2, full2, mine2,
    send_v, recv_v, send_1, recv_1, send_2, recv_2,
    send_a1, recv_a1, send_a2, recv_a2, send_b2, recv_b2,
):
    s = lax.axis_index("space")
    m = lax.axis_index("samp")
    size_x, size_y, size_z = v_ref.shape[1:]

    loads = [
        pltpu.make_async_copy(src, dst, load.at[j])
        for j, (src, dst) in enumerate(
            ((f2_hbm, f2_flat), (f1_hbm, f1_flat), (v_hbm, v_ref), (c_hbm, c_ref)))
    ]
    for copy in loads:
        copy.start()
    vp[...] = jnp.zeros_like(vp)

    def there(dx, dy):
        return (s + dx >= 0) & (s + dx < n_space) & (m + dy >= 0) & (m + dy < n_samp)

    barrier = pltpu.get_barrier_semaphore()
    peers = n_samp - 1 + n_space - 1
    for dx, dy in DIRS:
        if dx == 0 or dy == 0:
            continue
        peers = peers + jnp.where(there(dx, dy), 1, 0)

        @pl.when(there(dx, dy))
        def _():
            pl.semaphore_signal(barrier, inc=1, device_id=(s + dx, m + dy), device_id_type=MESH)
    for k in range(1, n_samp):
        pl.semaphore_signal(barrier, inc=1, device_id=(s, lax.rem(m + k, n_samp)), device_id_type=MESH)

    def greet(k, carry):
        pl.semaphore_signal(barrier, inc=1, device_id=(lax.rem(s + k, n_space), m), device_id_type=MESH)
        return carry

    lax.fori_loop(1, n_space, greet, 0)

    loads[0].wait()
    split_rows(f2_flat, f2_ref)
    loads[1].wait()
    split_rows(f1_flat, f1_ref)
    turn_v = one_hot_rows(CIN, size_y)
    loads[2].wait()

    def centre(x, carry):
        value = v_ref[:, x].astype(F32).reshape(CIN * size_y, size_z).astype(BF16)
        value = dot(turn_v, value)
        for y in range(size_y):
            vp[x + 2, y + 2] = value[CIN * y : CIN * (y + 1)].astype(BF16)
        return carry

    lax.fori_loop(0, size_x, centre, 0)
    pl.semaphore_wait(barrier, peers)

    def copy_1(k):
        return pltpu.make_async_remote_copy(
            src_ref=f1_ref, dst_ref=all1.at[m], send_sem=send_1.at[k], recv_sem=recv_1.at[k],
            device_id=(s, lax.rem(m + k, n_samp)), device_id_type=MESH)

    def copy_2(k):
        return pltpu.make_async_remote_copy(
            src_ref=f2_ref, dst_ref=all2.at[s], send_sem=send_2.at[k], recv_sem=recv_2.at[k],
            device_id=(lax.rem(s + k, n_space), m), device_id_type=MESH)

    def halo(src, dst, width, send, recv, slot, dx, dy):
        (sx, nx), (tx, _) = spans(dx, size_x, width)
        (sy, ny), (ty, _) = spans(dy, size_y, width)
        return pltpu.make_async_remote_copy(
            src_ref=src.at[pl.ds(sx + width, nx), pl.ds(sy + width, ny)], dst_ref=dst.at[pl.ds(tx, nx), pl.ds(ty, ny)],
            send_sem=send.at[slot], recv_sem=recv.at[slot],
            device_id=(jnp.clip(s + dx, 0, n_space - 1), jnp.clip(m + dy, 0, n_samp - 1)),
            device_id_type=MESH)

    vol = [halo(vp, vp, 2, send_v, recv_v, j, dx, dy) for j, (dx, dy) in enumerate(DIRS)]
    for k in range(1, n_samp):
        copy_1(k).start()

    def start_2(k, carry):
        copy_2(k).start()
        return carry

    lax.fori_loop(1, n_space, start_2, 0)
    for copy, (dx, dy) in zip(vol, DIRS):
        @pl.when(there(dx, dy))
        def _():
            copy.start()

    all1[m] = f1_ref[...]
    all2[s] = f2_ref[...]
    last = size_z - 1
    high_y = size_y + 2

    def lanes(rows):
        return lax.broadcasted_iota(jnp.int32, (rows, size_z), 1)

    lane1 = lanes(C1)
    lane2 = lanes(C2)
    build_selectors(q1, q2, q3)
    turn[...] = one_hot_rows(C2, size_y)
    loads[3].wait()

    def turn_c(x, carry):
        value = c_ref[:, x].astype(F32).reshape(C2 * size_y, size_z).astype(BF16)
        cp[x] = dot(turn[...], value).astype(BF16).reshape(size_y, C2, size_z)
        return carry

    lax.fori_loop(0, size_x, turn_c, 0)

    def clear(x, carry):
        back[x] = jnp.zeros(back.shape[1:], back.dtype)
        return carry

    lax.fori_loop(0, back.shape[0], clear, 0)
    r = lax.broadcasted_iota(jnp.int32, (C2 * size_y, C2 * size_y), 0)
    q = lax.broadcasted_iota(jnp.int32, (C2 * size_y, C2 * size_y), 1)
    from_row = (r % size_y) * C2 + r // size_y
    perm[...] = jnp.where(q == from_row, 1.0, 0.0).astype(BF16)
    acc1[...] = jnp.zeros_like(acc1)
    acc2[...] = jnp.zeros_like(acc2)
    tall3[...] = jnp.zeros_like(tall3)

    def over_space(body):
        def step(k, carry):
            body(k)
            return carry

        lax.fori_loop(1, n_space, step, 0)

    def arrive(group):
        for copy, (dx, dy) in zip(group, DIRS):
            @pl.when(there(-dx, -dy))
            def _():
                copy.wait_recv()

            @pl.when(there(dx, dy))
            def _():
                copy.wait_send()

    for k in range(1, n_samp):
        copy_1(k).wait()
    over_space(lambda k: copy_2(k).wait())
    m1 = gather_rows(all1, rows1, wide1)
    m2 = gather_rows(all2, rows2, wide2)
    base1 = jnp.concatenate([dot(m1, q1[kz]) for kz in range(3)], axis=0)
    base2 = jnp.concatenate([dot(m2, q2[kz]) for kz in range(3)], axis=0)
    for kx in range(3):
        for ky in range(3):
            first = 128 * kx + C2 * ky
            tall3[first : first + C2] = dot(m2, q3[3 * kx + ky])
    base3 = tall3[...].T[:48]
    for y in range(high_y):
        row = base1 if y == 0 else pltpu.roll(base1, 4 * y, axis=1)
        a1[48 * y : 48 * y + 48] = row[:, :192].astype(BF16)
    a2[:96] = base2[:, :192].astype(BF16)
    a2[96:] = pltpu.roll(base2, 16, axis=1)[:, :192].astype(BF16)
    a3[:48] = base3.astype(BF16)
    a3[48:] = pltpu.roll(base3, 32, axis=1).astype(BF16)

    arrive(vol)

    def lift(x, carry):
        for y in range(vp.shape[1]):
            vf[CIN * y : CIN * (y + 1)] = vp[x, y].astype(F32)
        vrows[x] = vf[...].astype(BF16)
        return carry

    lax.fori_loop(0, vp.shape[0], lift, 0)

    def vwin(x):
        return jnp.concatenate([vrows[x], vrows[x + 1], vrows[x + 2]], axis=0)

    def layer1(x, carry):
        gx = s * size_x + x - 1
        ok_x = (gx >= 0) & (gx < n_space * size_x)
        t1[...] = dot(a1[...], vwin(x))
        for y in range(high_y):
            gy = m * size_y + y - 1
            ok = ok_x & (gy >= 0) & (gy < n_samp * size_y)
            p = tap_sum(t1[48 * y : 48 * y + 48], C1, lane1, last)
            pre[x, 16 * y : 16 * y + 16] = p
            h = leaky(p) * jnp.where(ok, 1.0, 0.0)
            hid[x, 16 * y : 16 * y + 16] = h.astype(BF16)
        return carry

    lax.fori_loop(0, size_x + 2, layer1, 0)

    def hwin(x, y):
        return jnp.concatenate([hid[x + k, 16 * y : 16 * y + 64] for k in range(3)], axis=0)

    def pre_two(t, half):
        return tap_sum(t[96 * half : 96 * half + 96], C2, lane2, last)

    def back_two(x, y, p):
        b = (cp[x, y].astype(F32) * jnp.where(p > 0, 1.0, SLOPE)).astype(BF16)
        back[x + 2, C2 * (y + 2) : C2 * (y + 3)] = b
        return b

    def layer2(x, carry):
        moved, windows = [], []
        for y in range(0, size_y, 2):
            win = hwin(x, y)
            t = dot(a2[...], win)
            both = []
            for half in range(2):
                p = pre_two(t, half)
                act[C2 * (y + half) : C2 * (y + half + 1)] = leaky(p).astype(BF16)
                b = back_two(x, y + half, p)
                both.append(tap_spread(b.astype(F32), lane2, last).astype(BF16))
            moved.append(jnp.concatenate(both, axis=0))
            windows.append(win)
        acc2[...] += dot_nt(jnp.concatenate(moved, axis=1), jnp.concatenate(windows, axis=1))
        value = dot(perm[...], act[...])
        act_ref[:, x] = value.reshape(C2, size_y, size_z).astype(BF16)
        return carry

    lax.fori_loop(0, size_x, layer2, 0)

    def wide(values, rows):
        return jnp.concatenate([values, jnp.zeros((rows, 64), F32)], axis=1)

    def samp_peer(k):
        return lax.rem(m + k, n_samp)

    def space_peer(k):
        return lax.rem(s + k, n_space)

    def first_2(k):
        return pltpu.make_async_remote_copy(
            src_ref=grad2.at[space_peer(k)], dst_ref=part2.at[s], send_sem=send_a2.at[k],
            recv_sem=recv_a2.at[k], device_id=(space_peer(k), m), device_id_type=MESH)

    def second_2(k):
        return pltpu.make_async_remote_copy(
            src_ref=mine2, dst_ref=full2.at[m], send_sem=send_b2.at[k],
            recv_sem=recv_b2.at[k], device_id=(s, samp_peer(k)), device_id_type=MESH)

    total2 = wide(acc2[:96], 96) + pltpu.roll(wide(acc2[96:], 96), 256 - 16, axis=1)
    scatter_rows(flat_order(total2, q2, C2), rows2, wide2, grad2)
    over_space(lambda k: first_2(k).start())
    part2[s] = grad2[s]

    def finish(x, carry):
        gx = s * size_x + x - 1
        ok_x = (gx >= 0) & (gx < n_space * size_x)
        pieces = []
        for y in range(0, high_y, 2):
            win = jnp.concatenate([back[x + k, C2 * y : C2 * y + 128] for k in range(3)], axis=0)
            t = dot(a3[...], win)
            for half in range(2):
                gy = m * size_y + y + half - 1
                ok = ok_x & (gy >= 0) & (gy < n_samp * size_y)
                d = tap_sum(t[48 * half : 48 * half + 48], C1, lane1, last)
                p = pre[x, 16 * (y + half) : 16 * (y + half) + 16]
                slope = jnp.where(p > 0, 1.0, SLOPE) * jnp.where(ok, 1.0, 0.0)
                b1 = (d * slope).astype(BF16).astype(F32)
                pieces.append(tap_spread(b1, lane1, last).astype(BF16))
        acc1[...] += dot_nt(jnp.concatenate(pieces, axis=0), vwin(x))
        return carry

    lax.fori_loop(0, size_x + 2, finish, 0)

    total1 = jnp.zeros((48, 256), F32)
    for y in range(high_y):
        total1 = total1 + pltpu.roll(wide(acc1[48 * y : 48 * y + 48], 48), (256 - 4 * y) % 256, axis=1)
    scatter_rows(flat_order(total1, q1, C1), rows1, wide1, grad1)

    everyone = n_space * n_samp
    me = s * n_samp + m

    def to_all(k, carry):
        peer = lax.rem(me + k, everyone)
        ps, pm = peer // n_samp, lax.rem(peer, n_samp)
        pltpu.make_async_remote_copy(
            src_ref=grad1.at[pm], dst_ref=part1.at[me], send_sem=send_a1, recv_sem=recv_a1,
            device_id=(ps, pm), device_id_type=MESH).start()
        return carry

    lax.fori_loop(1, everyone, to_all, 0)
    part1[me] = grad1[m]
    over_space(lambda k: first_2(k).wait())
    mine2[...] = jnp.sum(part2[...], axis=0)
    for k in range(1, n_samp):
        second_2(k).start()
    full2[m] = mine2[...]
    for k in range(1, n_samp):
        second_2(k).wait()
    o2_ref[...] = flatten(jnp.sum(full2[...], axis=0) * scale)
    others = part1.at[pl.ds(0, everyone - 1)]
    pltpu.make_async_copy(others, others, send_a1).wait()
    pltpu.make_async_copy(others, others, recv_a1).wait()
    o1_ref[...] = flatten(jnp.sum(part1[...], axis=0) * scale)


def store_kernel(act, o1, o2, act_out, o1_out, o2_out, done):
    copies = [
        pltpu.make_async_copy(src, dst, done.at[j])
        for j, (src, dst) in enumerate(((act, act_out), (o1, o1_out), (o2, o2_out)))
    ]
    for copy in copies:
        copy.start()
    for copy in copies:
        copy.wait()


VMEM = pl.BlockSpec(memory_space=pltpu.VMEM)
HBM = pl.BlockSpec(memory_space=pltpu.HBM)


def on_device(n_space, n_samp, volume, filters_one, filters_two, cotangent):
    _, size_x, size_y, size_z = volume.shape
    len1 = filters_one.shape[0]
    len2 = filters_two.shape[0]
    unit1 = math.gcd(len1, 27 * CIN)
    unit2 = math.gcd(len2, 27 * C1)
    piece1 = (len1 // unit1, unit1)
    piece2 = (len2 // unit2, unit2)
    high_y = size_y + 2
    scale = 1.0 / math.sqrt(float(size_x * n_space * size_y * n_samp * size_z))
    samp, space = pltpu.SemaphoreType.DMA((n_samp,)), pltpu.SemaphoreType.DMA((n_space,))
    sides = pltpu.SemaphoreType.DMA((8,))
    activation, out1, out2 = pl.pallas_call(
        functools.partial(fused_kernel, n_space, n_samp, scale),
        out_shape=[
            jax.ShapeDtypeStruct((C2, size_x, size_y, size_z), BF16),
            jax.ShapeDtypeStruct((len1,), F32),
            jax.ShapeDtypeStruct((len2,), F32),
        ],
        in_specs=[HBM] * 4,
        out_specs=[VMEM] * 3,
        scratch_shapes=[
            pltpu.VMEM(volume.shape, BF16),
            pltpu.VMEM(cotangent.shape, BF16),
            pltpu.VMEM((len1,), BF16),
            pltpu.VMEM((len2,), BF16),
            pltpu.VMEM(piece1, BF16),
            pltpu.VMEM(piece2, BF16),
            pltpu.SemaphoreType.DMA((4,)),
            pltpu.VMEM((size_x + 4, size_y + 8, CIN, size_z), BF16),
            pltpu.VMEM((size_x, size_y, C2, size_z), BF16),
            pltpu.VMEM((n_samp, *piece1), BF16),
            pltpu.VMEM((n_space, *piece2), BF16),
            pltpu.VMEM((C2 * size_y, C2 * size_y), BF16),
            pltpu.VMEM((48 * high_y, 192), BF16),
            pltpu.VMEM((192, 192), BF16),
            pltpu.VMEM((96, 384), BF16),
            pltpu.VMEM((size_x + 2, 16 * high_y, size_z), BF16),
            pltpu.VMEM((size_x + 4, C2 * (size_y + 4), size_z), BF16),
            pltpu.VMEM((size_x + 2, 16 * high_y, size_z), F32),
            pltpu.VMEM((48 * high_y, size_z), F32),
            pltpu.VMEM((C2 * size_y, C2 * size_y), BF16),
            pltpu.VMEM((48 * high_y, 192), F32),
            pltpu.VMEM((192, 192), F32),
            pltpu.VMEM((C2 * size_y, size_z), BF16),
            pltpu.VMEM((3, 27 * CIN, 256), BF16),
            pltpu.VMEM((3, 27 * C1, 256), BF16),
            pltpu.VMEM((9, 27 * C1, 128), BF16),
            pltpu.VMEM((n_samp * piece1[0], piece1[1]), F32),
            pltpu.VMEM((C1, 27 * CIN), F32),
            pltpu.VMEM((n_space * piece2[0], piece2[1]), F32),
            pltpu.VMEM((C2, 27 * C1), F32),
            pltpu.VMEM((384, 128), F32),
            pltpu.VMEM((CIN * (size_y + 8), size_z), F32),
            pltpu.VMEM((size_x + 4, CIN * (size_y + 8), size_z), BF16),
            pltpu.VMEM((n_samp, *piece1), F32),
            pltpu.VMEM((n_space, *piece2), F32),
            pltpu.VMEM((n_space * n_samp, *piece1), F32),
            pltpu.VMEM((n_space, *piece2), F32),
            pltpu.VMEM((n_samp, *piece2), F32),
            pltpu.VMEM(piece2, F32),
            sides, sides, samp, samp, space, space,
            pltpu.SemaphoreType.DMA, pltpu.SemaphoreType.DMA, space, space, samp, samp,
        ],
        compiler_params=pltpu.CompilerParams(
            collective_id=0, has_side_effects=True, vmem_limit_bytes=48 * 2**20),
    )(*(pltpu.with_memory_space_constraint(x, pltpu.HBM)
        for x in (volume, cotangent, filters_one, filters_two)))
    return pl.pallas_call(
        store_kernel,
        out_shape=[jax.ShapeDtypeStruct(x.shape, x.dtype) for x in (activation, out1, out2)],
        in_specs=[VMEM] * 3,
        out_specs=[HBM] * 3,
        scratch_shapes=[pltpu.SemaphoreType.DMA((3,))],
        compiler_params=pltpu.CompilerParams(vmem_limit_bytes=2**20),
    )(activation, out1, out2)


def solution(mesh):
    in_specs = (
        P(None, "space", "samp", None),
        P("samp"),
        P("space"),
        P(None, "space", "samp", None),
    )
    out_specs = (P(None, "space", "samp", None), P("samp"), P("space"))
    return jax.shard_map(
        functools.partial(on_device, mesh.shape["space"], mesh.shape["samp"]),
        mesh=mesh, in_specs=in_specs, out_specs=out_specs, check_vma=False,
    )
```

```python
import functools
import math

import jax
import jax.numpy as jnp
from jax import lax
from jax.experimental import pallas as pl
from jax.experimental.pallas import tpu as pltpu
from jax.sharding import PartitionSpec as P

CIN = 4
C1 = 16
C2 = 32
SLOPE = 0.3
MESH = pl.DeviceIdType.MESH
F32 = jnp.float32
BF16 = jnp.bfloat16
DIRS = [(dx, dy) for dx in (-1, 0, 1) for dy in (-1, 0, 1) if (dx, dy) != (0, 0)]


def spans(delta, size, width):
    if delta == 1:
        return (size - width, width), (0, width)
    if delta == -1:
        return (0, width), (size + width, width)
    return (0, size), (width, size)


def leaky(values):
    return jnp.where(values > 0, values, SLOPE * values)


def shifted(values, lane, last):
    before = jnp.where(lane == 0, 0.0, pltpu.roll(values, 1, axis=1))
    after = jnp.where(lane == last, 0.0, pltpu.roll(values, last, axis=1))
    return before, after


def dot(a, b):
    return lax.dot_general(a, b, (((1,), (0,)), ((), ())), preferred_element_type=F32)


def dot_nt(a, b):
    return lax.dot_general(a, b, (((1,), (1,)), ((), ())), preferred_element_type=F32)


def one_hot(rows, source):
    row = lax.broadcasted_iota(jnp.int32, (rows, source.shape[1]), 0)
    return jnp.where(row == source, 1.0, 0.0).astype(BF16)


def one_hot_rows(chans, size_y):
    r = lax.broadcasted_iota(jnp.int32, (chans * size_y, chans * size_y), 0)
    q = lax.broadcasted_iota(jnp.int32, (chans * size_y, chans * size_y), 1)
    return jnp.where(q == (r % chans) * size_y + r // chans, 1.0, 0.0).astype(BF16)


def build_selectors(s1, s2, q2, width1, width2):
    lane = lax.broadcasted_iota(jnp.int32, (1, s1.shape[1]), 1)
    group, rest = lax.div(lane, width1), lax.rem(lane, width1)
    kz, kx, ky, i = lax.div(group, 3), lax.rem(group, 3), lax.div(rest, CIN), lax.rem(rest, CIN)
    s1[...] = one_hot(27 * CIN, jnp.where((group < 9) & (ky < 3), i * 27 + kx * 9 + ky * 3 + kz, -9))
    lane = lax.broadcasted_iota(jnp.int32, (1, s2.shape[1]), 1)
    group, rest = lax.div(lane, width2), lax.rem(lane, width2)
    kz, kx, ky, i = lax.div(group, 3), lax.rem(group, 3), lax.div(rest, C1), lax.rem(rest, C1)
    s2[...] = one_hot(27 * C1, jnp.where((group < 9) & (ky < 3), i * 27 + kx * 9 + ky * 3 + kz, -9))
    lane = lax.broadcasted_iota(jnp.int32, (1, 256), 1)
    kx, ky, i = lane >> 6, (lane >> 4) & 3, lane & 15
    source = jnp.where((kx < 3) & (ky < 3), i * 27 + kx * 9 + ky * 3, -9)
    for kz in range(3):
        q2[kz] = one_hot(27 * C1, source + kz)


def split_rows(flat_ref, rows_ref):
    rows, unit = rows_ref.shape
    flat = flat_ref[...].astype(F32).reshape(1, rows * unit)
    rows_ref[...] = jnp.concatenate(
        [flat[:, unit * k : unit * (k + 1)] for k in range(rows)], axis=0).astype(BF16)


def flatten(rows):
    return jnp.concatenate([rows[k : k + 1] for k in range(rows.shape[0])], axis=1).reshape(rows.size)


def gather_rows(all_ref, rows_ref, wide_ref):
    owners, count, unit = all_ref.shape
    for j in range(owners):
        rows_ref[count * j : count * (j + 1)] = all_ref[j].astype(F32)
    split = wide_ref.shape[1] // unit
    if split == 1:
        return rows_ref[...].astype(BF16)
    for k in range(split):
        wide_ref[:, unit * k : unit * (k + 1)] = rows_ref[pl.ds(k, wide_ref.shape[0], stride=split)]
    return wide_ref[...].astype(BF16)


def scatter_rows(value, rows_ref, wide_ref, out_ref):
    owners, count, unit = out_ref.shape
    split = value.shape[1] // unit
    if split == 1:
        rows_ref[...] = value
    else:
        wide_ref[...] = value
        for k in range(split):
            rows_ref[pl.ds(k, value.shape[0], stride=split)] = wide_ref[:, unit * k : unit * (k + 1)]
    for j in range(owners):
        out_ref[j] = rows_ref[count * j : count * (j + 1)]


def split3(g):
    high = g.astype(BF16)
    rest = g - high.astype(F32)
    mid = rest.astype(BF16)
    low = (rest - mid.astype(F32)).astype(BF16)
    return jnp.concatenate([high, mid, low], axis=0)


def pick(g, selector):
    rows = g.shape[0]
    r = dot_nt(split3(g), selector)
    return r[:rows] + r[rows : 2 * rows] + r[2 * rows :]


def fused_kernel(
    n_space, n_samp, scale, v_hbm, c_hbm, f1_hbm, f2_hbm, act_ref, o1_ref, o2_ref,
    v_ref, c_ref, f1_flat, f2_flat, f1_ref, f2_ref, load,
    vp, cp, all1, all2,
    turn, a1, a2, a3, hid, back, slope1, perm, acc1, acc2, act,
    s1, s2, q2, rows1, wide1, rows2, wide2, vf, vrows,
    grad1, grad2, part1, part2, full2, mine2,
    send_v, recv_v, send_1, recv_1, send_2, recv_2,
    send_a1, recv_a1, send_a2, recv_a2, send_b2, recv_b2,
):
    s = lax.axis_index("space")
    m = lax.axis_index("samp")
    size_x, size_y, size_z = v_ref.shape[1:]

    loads = [
        pltpu.make_async_copy(src, dst, load.at[j])
        for j, (src, dst) in enumerate(
            ((f2_hbm, f2_flat), (f1_hbm, f1_flat), (v_hbm, v_ref), (c_hbm, c_ref)))
    ]
    for copy in loads:
        copy.start()
    vp[...] = jnp.zeros_like(vp)

    def there(dx, dy):
        return (s + dx >= 0) & (s + dx < n_space) & (m + dy >= 0) & (m + dy < n_samp)

    barrier = pltpu.get_barrier_semaphore()
    peers = n_samp - 1 + n_space - 1
    for dx, dy in DIRS:
        if dx == 0 or dy == 0:
            continue
        peers = peers + jnp.where(there(dx, dy), 1, 0)

        @pl.when(there(dx, dy))
        def _():
            pl.semaphore_signal(barrier, inc=1, device_id=(s + dx, m + dy), device_id_type=MESH)
    for k in range(1, n_samp):
        pl.semaphore_signal(barrier, inc=1, device_id=(s, lax.rem(m + k, n_samp)), device_id_type=MESH)

    def greet(k, carry):
        pl.semaphore_signal(barrier, inc=1, device_id=(lax.rem(s + k, n_space), m), device_id_type=MESH)
        return carry

    lax.fori_loop(1, n_space, greet, 0)

    loads[0].wait()
    split_rows(f2_flat, f2_ref)
    loads[1].wait()
    split_rows(f1_flat, f1_ref)
    turn_v = one_hot_rows(CIN, size_y)
    loads[2].wait()

    def centre(x, carry):
        value = v_ref[:, x].astype(F32).reshape(CIN * size_y, size_z).astype(BF16)
        value = dot(turn_v, value)
        for y in range(size_y):
            vp[x + 2, y + 2] = value[CIN * y : CIN * (y + 1)].astype(BF16)
        return carry

    lax.fori_loop(0, size_x, centre, 0)
    pl.semaphore_wait(barrier, peers)

    def copy_1(k):
        return pltpu.make_async_remote_copy(
            src_ref=f1_ref, dst_ref=all1.at[m], send_sem=send_1.at[k], recv_sem=recv_1.at[k],
            device_id=(s, lax.rem(m + k, n_samp)), device_id_type=MESH)

    def copy_2(k):
        return pltpu.make_async_remote_copy(
            src_ref=f2_ref, dst_ref=all2.at[s], send_sem=send_2.at[k], recv_sem=recv_2.at[k],
            device_id=(lax.rem(s + k, n_space), m), device_id_type=MESH)

    def halo(src, dst, width, send, recv, slot, dx, dy):
        (sx, nx), (tx, _) = spans(dx, size_x, width)
        (sy, ny), (ty, _) = spans(dy, size_y, width)
        return pltpu.make_async_remote_copy(
            src_ref=src.at[pl.ds(sx + width, nx), pl.ds(sy + width, ny)], dst_ref=dst.at[pl.ds(tx, nx), pl.ds(ty, ny)],
            send_sem=send.at[slot], recv_sem=recv.at[slot],
            device_id=(jnp.clip(s + dx, 0, n_space - 1), jnp.clip(m + dy, 0, n_samp - 1)),
            device_id_type=MESH)

    vol = [halo(vp, vp, 2, send_v, recv_v, j, dx, dy) for j, (dx, dy) in enumerate(DIRS)]
    for k in range(1, n_samp):
        copy_1(k).start()

    def start_2(k, carry):
        copy_2(k).start()
        return carry

    lax.fori_loop(1, n_space, start_2, 0)
    for copy, (dx, dy) in zip(vol, DIRS):
        @pl.when(there(dx, dy))
        def _():
            copy.start()

    all1[m] = f1_ref[...]
    all2[s] = f2_ref[...]
    last = size_z - 1
    high_y = size_y + 2

    def lanes(rows):
        return lax.broadcasted_iota(jnp.int32, (rows, size_z), 1)

    width1 = CIN * (size_y + 4)
    width2 = C1 * 6
    build_selectors(s1, s2, q2, width1, width2)
    turn[...] = one_hot_rows(C2, size_y)
    loads[3].wait()

    def turn_c(x, carry):
        value = c_ref[:, x].astype(F32).reshape(C2 * size_y, size_z).astype(BF16)
        cp[x] = dot(turn[...], value).astype(BF16)
        return carry

    lax.fori_loop(0, size_x, turn_c, 0)

    r = lax.broadcasted_iota(jnp.int32, (C2 * size_y, C2 * size_y), 0)
    q = lax.broadcasted_iota(jnp.int32, (C2 * size_y, C2 * size_y), 1)
    from_row = (r % size_y) * C2 + r // size_y
    perm[...] = jnp.where(q == from_row, 1.0, 0.0).astype(BF16)
    acc1[...] = jnp.zeros_like(acc1)
    acc2[...] = jnp.zeros_like(acc2)

    def over_space(body):
        def step(k, carry):
            body(k)
            return carry

        lax.fori_loop(1, n_space, step, 0)

    def arrive(group):
        for copy, (dx, dy) in zip(group, DIRS):
            @pl.when(there(-dx, -dy))
            def _():
                copy.wait_recv()

            @pl.when(there(dx, dy))
            def _():
                copy.wait_send()

    for k in range(1, n_samp):
        copy_1(k).wait()
    base1 = dot(gather_rows(all1, rows1, wide1), s1[...])
    for y in range(high_y):
        row = base1 if y == 0 else pltpu.roll(base1, CIN * y, axis=1)
        a1[C1 * y : C1 * (y + 1)] = row[:, : 9 * width1].astype(BF16)

    arrive(vol)
    lane_v = lanes(width1)
    lane_h = lanes(C1 * high_y)
    lane_b = lanes(C2 * 4)

    for x in range(size_x + 4):
        for y in range(vp.shape[1]):
            vf[x, CIN * y : CIN * (y + 1)] = vp[x, y].astype(F32)
    for x in range(size_x + 4):
        value = vf[x]
        before, after = shifted(value, lane_v, last)
        vrows[0, x] = before.astype(BF16)
        vrows[1, x] = value.astype(BF16)
        vrows[2, x] = after.astype(BF16)

    def vwin(x):
        return jnp.concatenate([vrows[kz, x + kx] for kz in range(3) for kx in range(3)], axis=0)

    first_row = jnp.where(m > 0, 1.0, 0.0)
    last_row = jnp.where(m < n_samp - 1, 1.0, 0.0)

    for x in range(size_x + 2):
        p = dot(a1[...], vwin(x))
        slope = jnp.where(p > 0, 1.0, SLOPE)
        if x == 0:
            slope = slope * jnp.where(s > 0, 1.0, 0.0)
        if x == size_x + 1:
            slope = slope * jnp.where(s < n_space - 1, 1.0, 0.0)
        slope = jnp.concatenate(
            [slope[:C1] * first_row, slope[C1 : C1 * (high_y - 1)], slope[C1 * (high_y - 1) :] * last_row], axis=0)
        slope1[x] = slope
        h = p * slope
        before, after = shifted(h, lane_h, last)
        hid[0, x] = before.astype(BF16)
        hid[1, x] = h.astype(BF16)
        hid[2, x] = after.astype(BF16)

    over_space(lambda k: copy_2(k).wait())
    base2 = dot(gather_rows(all2, rows2, wide2), s2[...])
    for y in range(4):
        row = base2 if y == 0 else pltpu.roll(base2, C1 * y, axis=1)
        a2[C2 * y : C2 * (y + 1)] = row[:, : 9 * width2].astype(BF16)
    tall = jnp.concatenate([base2, jnp.zeros((128 - C2, base2.shape[1]), F32)], axis=0).T
    lane_t = lax.broadcasted_iota(jnp.int32, (C1, 128), 1)
    for kx in range(3):
        for kz in range(3):
            tile = 0.0
            for y in range(3):
                first = width2 * (3 * kz + kx) + C1 * (2 - y)
                piece = tall[first : first + C1]
                tile = tile + (piece if y == 0 else pltpu.roll(piece, C2 * y, axis=1))
            column = C2 * size_y * (3 * kx + kz)
            zero = jnp.zeros((C1, 128), BF16)
            for r in range(4):
                turned = tile if r == 0 else pltpu.roll(tile, C2 * r, axis=1)
                main = jnp.where(lane_t >= C2 * r, turned, 0.0).astype(BF16)
                over = jnp.where(lane_t < C2 * r, turned, 0.0).astype(BF16)
                for y in range(high_y):
                    q = (y - 2) // 4
                    if (y - 2) % 4 != r:
                        continue
                    low, high = ((over, zero), (main, over), (zero, main))[q + 1]
                    a3[C1 * y : C1 * (y + 1), column : column + 128] = low
                    a3[C1 * y : C1 * (y + 1), column + 128 : column + 256] = high

    def layer2(x, carry):
        for half in range(size_y // 4):
            rows = slice(128 * half, 128 * half + 128)
            win = jnp.concatenate(
                [hid[kz, x + kx, 64 * half : 64 * half + width2] for kz in range(3) for kx in range(3)], axis=0)
            p = dot(a2[...], win)
            slope = jnp.where(p > 0, 1.0, SLOPE)
            act[rows] = (p * slope).astype(BF16)
            b = (cp[x, rows].astype(F32) * slope).astype(BF16)
            before, after = shifted(b.astype(F32), lane_b, last)
            back[0, x, rows] = after.astype(BF16)
            back[1, x, rows] = b
            back[2, x, rows] = before.astype(BF16)
        value = dot(perm[...], act[...])
        act_ref[:, x] = value.reshape(C2, size_y, size_z).astype(BF16)
        return carry

    lax.fori_loop(0, size_x, layer2, 0)

    def kernel_grad2(x, carry):
        moved, windows = [], []
        for y in range(0, size_y, 2):
            moved.append(jnp.concatenate([back[kz, x, C2 * y : C2 * y + 64] for kz in range(3)], axis=0))
            windows.append(jnp.concatenate([hid[1, x + kx, C1 * y : C1 * y + 64] for kx in range(3)], axis=0))
        acc2[...] += dot_nt(jnp.concatenate(moved, axis=1), jnp.concatenate(windows, axis=1))
        return carry

    lax.fori_loop(0, size_x, kernel_grad2, 0)

    def samp_peer(k):
        return lax.rem(m + k, n_samp)

    def space_peer(k):
        return lax.rem(s + k, n_space)

    def first_2(k):
        return pltpu.make_async_remote_copy(
            src_ref=grad2.at[space_peer(k)], dst_ref=part2.at[s], send_sem=send_a2.at[k],
            recv_sem=recv_a2.at[k], device_id=(space_peer(k), m), device_id_type=MESH)

    def second_2(k):
        return pltpu.make_async_remote_copy(
            src_ref=mine2, dst_ref=full2.at[m], send_sem=send_b2.at[k],
            recv_sem=recv_b2.at[k], device_id=(s, samp_peer(k)), device_id_type=MESH)

    result = 0.0
    for kz in range(3):
        low = jnp.concatenate([acc2[64 * kz : 64 * kz + C2], jnp.zeros((C2, 64), F32)], axis=1)
        high = jnp.concatenate([acc2[64 * kz + C2 : 64 * kz + 64], jnp.zeros((C2, 64), F32)], axis=1)
        result = result + pick(low + pltpu.roll(high, 256 - C1, axis=1), q2[kz])
    scatter_rows(result, rows2, wide2, grad2)
    over_space(lambda k: first_2(k).start())
    part2[s] = grad2[s]

    group = 3 * C2 * size_y
    for x in range(size_x + 2):
        taps = [kx for kx in range(3) if 0 <= x - kx < size_x]
        weights = a3[:, group * taps[0] : group * (taps[-1] + 1)]
        win = jnp.concatenate([back[kz, x - kx] for kx in taps for kz in range(3)], axis=0)
        b1 = (dot(weights, win) * slope1[x]).astype(BF16)
        acc1[:, : 9 * width1] += dot_nt(b1, vwin(x))

    total1 = acc1[:C1]
    for y in range(1, high_y):
        total1 = total1 + pltpu.roll(acc1[C1 * y : C1 * (y + 1)], acc1.shape[1] - CIN * y, axis=1)
    scatter_rows(pick(total1, s1[...]), rows1, wide1, grad1)

    everyone = n_space * n_samp
    me = s * n_samp + m

    def to_all(k, carry):
        peer = lax.rem(me + k, everyone)
        ps, pm = peer // n_samp, lax.rem(peer, n_samp)
        pltpu.make_async_remote_copy(
            src_ref=grad1.at[pm], dst_ref=part1.at[me], send_sem=send_a1, recv_sem=recv_a1,
            device_id=(ps, pm), device_id_type=MESH).start()
        return carry

    lax.fori_loop(1, everyone, to_all, 0)
    part1[me] = grad1[m]
    over_space(lambda k: first_2(k).wait())
    mine2[...] = jnp.sum(part2[...], axis=0)
    for k in range(1, n_samp):
        second_2(k).start()
    full2[m] = mine2[...]
    for k in range(1, n_samp):
        second_2(k).wait()
    o2_ref[...] = flatten(jnp.sum(full2[...], axis=0) * scale)
    others = part1.at[pl.ds(0, everyone - 1)]
    pltpu.make_async_copy(others, others, send_a1).wait()
    pltpu.make_async_copy(others, others, recv_a1).wait()
    o1_ref[...] = flatten(jnp.sum(part1[...], axis=0) * scale)


def store_kernel(act, o1, o2, act_out, o1_out, o2_out, done):
    copies = [
        pltpu.make_async_copy(src, dst, done.at[j])
        for j, (src, dst) in enumerate(((act, act_out), (o1, o1_out), (o2, o2_out)))
    ]
    for copy in copies:
        copy.start()
    for copy in copies:
        copy.wait()


VMEM = pl.BlockSpec(memory_space=pltpu.VMEM)
HBM = pl.BlockSpec(memory_space=pltpu.HBM)


def on_device(n_space, n_samp, volume, filters_one, filters_two, cotangent):
    _, size_x, size_y, size_z = volume.shape
    len1 = filters_one.shape[0]
    len2 = filters_two.shape[0]
    unit1 = math.gcd(len1, 27 * CIN)
    unit2 = math.gcd(len2, 27 * C1)
    piece1 = (len1 // unit1, unit1)
    piece2 = (len2 // unit2, unit2)
    high_y = size_y + 2
    width1 = CIN * (size_y + 4)
    scale = 1.0 / math.sqrt(float(size_x * n_space * size_y * n_samp * size_z))
    samp, space = pltpu.SemaphoreType.DMA((n_samp,)), pltpu.SemaphoreType.DMA((n_space,))
    sides = pltpu.SemaphoreType.DMA((8,))
    activation, out1, out2 = pl.pallas_call(
        functools.partial(fused_kernel, n_space, n_samp, scale),
        out_shape=[
            jax.ShapeDtypeStruct((C2, size_x, size_y, size_z), BF16),
            jax.ShapeDtypeStruct((len1,), F32),
            jax.ShapeDtypeStruct((len2,), F32),
        ],
        in_specs=[HBM] * 4,
        out_specs=[VMEM] * 3,
        scratch_shapes=[
            pltpu.VMEM(volume.shape, BF16),
            pltpu.VMEM(cotangent.shape, BF16),
            pltpu.VMEM((len1,), BF16),
            pltpu.VMEM((len2,), BF16),
            pltpu.VMEM(piece1, BF16),
            pltpu.VMEM(piece2, BF16),
            pltpu.SemaphoreType.DMA((4,)),
            pltpu.VMEM((size_x + 4, size_y + 4, CIN, size_z), BF16),
            pltpu.VMEM((size_x, C2 * size_y, size_z), BF16),
            pltpu.VMEM((n_samp, *piece1), BF16),
            pltpu.VMEM((n_space, *piece2), BF16),
            pltpu.VMEM((C2 * size_y, C2 * size_y), BF16),
            pltpu.VMEM((C1 * high_y, 9 * width1), BF16),
            pltpu.VMEM((C2 * 4, 9 * C1 * 6), BF16),
            pltpu.VMEM((C1 * high_y, 9 * C2 * size_y), BF16),
            pltpu.VMEM((3, size_x + 2, C1 * high_y, size_z), BF16),
            pltpu.VMEM((3, size_x, C2 * size_y, size_z), BF16),
            pltpu.VMEM((size_x + 2, C1 * high_y, size_z), F32),
            pltpu.VMEM((C2 * size_y, C2 * size_y), BF16),
            pltpu.VMEM((C1 * high_y, 512), F32),
            pltpu.VMEM((192, 192), F32),
            pltpu.VMEM((C2 * size_y, size_z), BF16),
            pltpu.VMEM((27 * CIN, 512), BF16),
            pltpu.VMEM((27 * C1, 896), BF16),
            pltpu.VMEM((3, 27 * C1, 256), BF16),
            pltpu.VMEM((n_samp * piece1[0], piece1[1]), F32),
            pltpu.VMEM((C1, 27 * CIN), F32),
            pltpu.VMEM((n_space * piece2[0], piece2[1]), F32),
            pltpu.VMEM((C2, 27 * C1), F32),
            pltpu.VMEM((size_x + 4, width1, size_z), F32),
            pltpu.VMEM((3, size_x + 4, width1, size_z), BF16),
            pltpu.VMEM((n_samp, *piece1), F32),
            pltpu.VMEM((n_space, *piece2), F32),
            pltpu.VMEM((n_space * n_samp, *piece1), F32),
            pltpu.VMEM((n_space, *piece2), F32),
            pltpu.VMEM((n_samp, *piece2), F32),
            pltpu.VMEM(piece2, F32),
            sides, sides, samp, samp, space, space,
            pltpu.SemaphoreType.DMA, pltpu.SemaphoreType.DMA, space, space, samp, samp,
        ],
        compiler_params=pltpu.CompilerParams(
            collective_id=0, has_side_effects=True, vmem_limit_bytes=48 * 2**20),
    )(*(pltpu.with_memory_space_constraint(x, pltpu.HBM)
        for x in (volume, cotangent, filters_one, filters_two)))
    return pl.pallas_call(
        store_kernel,
        out_shape=[jax.ShapeDtypeStruct(x.shape, x.dtype) for x in (activation, out1, out2)],
        in_specs=[VMEM] * 3,
        out_specs=[HBM] * 3,
        scratch_shapes=[pltpu.SemaphoreType.DMA((3,))],
        compiler_params=pltpu.CompilerParams(vmem_limit_bytes=2**20),
    )(activation, out1, out2)


def solution(mesh):
    in_specs = (
        P(None, "space", "samp", None),
        P("samp"),
        P("space"),
        P(None, "space", "samp", None),
    )
    out_specs = (P(None, "space", "samp", None), P("samp"), P("space"))
    return jax.shard_map(
        functools.partial(on_device, mesh.shape["space"], mesh.shape["samp"]),
        mesh=mesh, in_specs=in_specs, out_specs=out_specs, check_vma=False,
    )
```

```python
import functools
import math

import jax
import jax.numpy as jnp
from jax import lax
from jax.experimental import pallas as pl
from jax.experimental.pallas import tpu as pltpu
from jax.sharding import PartitionSpec as P

CIN = 4
C1 = 16
C2 = 32
SLOPE = 0.3
MESH = pl.DeviceIdType.MESH
F32 = jnp.float32
BF16 = jnp.bfloat16
DIRS = [(dx, dy) for dx in (-1, 0, 1) for dy in (-1, 0, 1) if (dx, dy) != (0, 0)]


def spans(delta, size, width):
    if delta == 1:
        return (size - width, width), (0, width)
    if delta == -1:
        return (0, width), (size + width, width)
    return (0, size), (width, size)


def leaky(values):
    return jnp.where(values > 0, values, SLOPE * values)


def shifted(values, lane, last):
    before = jnp.where(lane == 0, 0.0, pltpu.roll(values, 1, axis=1))
    after = jnp.where(lane == last, 0.0, pltpu.roll(values, last, axis=1))
    return before, after


def dot(a, b):
    return lax.dot_general(a, b, (((1,), (0,)), ((), ())), preferred_element_type=F32)


def dot_nt(a, b):
    return lax.dot_general(a, b, (((1,), (1,)), ((), ())), preferred_element_type=F32)


def one_hot(rows, source):
    row = lax.broadcasted_iota(jnp.int32, (rows, source.shape[1]), 0)
    return jnp.where(row == source, 1.0, 0.0).astype(BF16)


def one_hot_rows(chans, size_y):
    r = lax.broadcasted_iota(jnp.int32, (chans * size_y, chans * size_y), 0)
    q = lax.broadcasted_iota(jnp.int32, (chans * size_y, chans * size_y), 1)
    return jnp.where(q == (r % chans) * size_y + r // chans, 1.0, 0.0).astype(BF16)


def build_selectors(s1, s2, q2, width1, width2):
    lane = lax.broadcasted_iota(jnp.int32, (1, s1.shape[1]), 1)
    group, rest = lax.div(lane, width1), lax.rem(lane, width1)
    kz, kx, ky, i = lax.div(group, 3), lax.rem(group, 3), lax.div(rest, CIN), lax.rem(rest, CIN)
    s1[...] = one_hot(27 * CIN, jnp.where((group < 9) & (ky < 3), i * 27 + kx * 9 + ky * 3 + kz, -9))
    lane = lax.broadcasted_iota(jnp.int32, (1, s2.shape[1]), 1)
    group, rest = lax.div(lane, width2), lax.rem(lane, width2)
    kz, kx, ky, i = lax.div(group, 3), lax.rem(group, 3), lax.div(rest, C1), lax.rem(rest, C1)
    s2[...] = one_hot(27 * C1, jnp.where((group < 9) & (ky < 3), i * 27 + kx * 9 + ky * 3 + kz, -9))
    lane = lax.broadcasted_iota(jnp.int32, (1, 256), 1)
    kx, ky, i = lane >> 6, (lane >> 4) & 3, lane & 15
    source = jnp.where((kx < 3) & (ky < 3), i * 27 + kx * 9 + ky * 3, -9)
    for kz in range(3):
        q2[kz] = one_hot(27 * C1, source + kz)


def split_rows(flat_ref, rows_ref):
    rows, unit = rows_ref.shape
    flat = flat_ref[...].astype(F32).reshape(1, rows * unit)
    rows_ref[...] = jnp.concatenate(
        [flat[:, unit * k : unit * (k + 1)] for k in range(rows)], axis=0).astype(BF16)


def flatten(rows):
    return jnp.concatenate([rows[k : k + 1] for k in range(rows.shape[0])], axis=1).reshape(rows.size)


def gather_rows(all_ref, rows_ref, wide_ref):
    owners, count, unit = all_ref.shape
    for j in range(owners):
        rows_ref[count * j : count * (j + 1)] = all_ref[j].astype(F32)
    split = wide_ref.shape[1] // unit
    if split == 1:
        return rows_ref[...].astype(BF16)
    for k in range(split):
        wide_ref[:, unit * k : unit * (k + 1)] = rows_ref[pl.ds(k, wide_ref.shape[0], stride=split)]
    return wide_ref[...].astype(BF16)


def scatter_rows(value, rows_ref, wide_ref, out_ref):
    owners, count, unit = out_ref.shape
    split = value.shape[1] // unit
    if split == 1:
        rows_ref[...] = value
    else:
        wide_ref[...] = value
        for k in range(split):
            rows_ref[pl.ds(k, value.shape[0], stride=split)] = wide_ref[:, unit * k : unit * (k + 1)]
    for j in range(owners):
        out_ref[j] = rows_ref[count * j : count * (j + 1)]


def split3(g):
    high = g.astype(BF16)
    rest = g - high.astype(F32)
    mid = rest.astype(BF16)
    low = (rest - mid.astype(F32)).astype(BF16)
    return jnp.concatenate([high, mid, low], axis=0)


def pick(g, selector):
    rows = g.shape[0]
    r = dot_nt(split3(g), selector)
    return r[:rows] + r[rows : 2 * rows] + r[2 * rows :]


def fused_kernel(
    n_space, n_samp, scale, v_hbm, c_hbm, f1_hbm, f2_hbm, act_ref, o1_ref, o2_ref,
    v_ref, c_ref, f1_flat, f2_flat, f1_ref, f2_ref, load,
    vp, cp, all1, all2,
    turn, a1, a2, a3, dhid, hid, back, slope1, perm, acc1, acc2, act,
    s1, s2, q2, rows1, wide1, rows2, wide2, vf, vrows,
    grad1, grad2, part1, part2, full2, mine2,
    send_v, recv_v, send_1, recv_1, send_2, recv_2,
    send_a1, recv_a1, send_a2, recv_a2, send_b2, recv_b2,
):
    s = lax.axis_index("space")
    m = lax.axis_index("samp")
    size_x, size_y, size_z = v_ref.shape[1:]
    other = m + 1 - 2 * lax.rem(m, 2)
    chips = n_samp // 2
    turn_sign = 1 - 2 * ((2 * s) // n_space)

    def far(k):
        return lax.rem(2 * n_space + s - turn_sign * k, n_space)

    def across(j):
        return lax.rem(other + 2 * j, n_samp)

    def each_other_far(body):
        if n_space <= 16:
            for k in range(1, n_space):
                body(far(k))
            return

        def step(k, carry):
            body(far(k))
            return carry

        lax.fori_loop(1, n_space, step, 0)

    loads = [
        pltpu.make_async_copy(src, dst, load.at[j])
        for j, (src, dst) in enumerate(
            ((f2_hbm, f2_flat), (f1_hbm, f1_flat), (v_hbm, v_ref), (c_hbm, c_ref)))
    ]
    for copy in loads:
        copy.start()
    vp[...] = jnp.zeros_like(vp)

    def there(dx, dy):
        return (s + dx >= 0) & (s + dx < n_space) & (m + dy >= 0) & (m + dy < n_samp)

    barrier = pltpu.get_barrier_semaphore()
    peers = n_samp - 1 + n_space - 1
    @each_other_far
    def _(peer):
        pl.semaphore_signal(barrier, inc=1, device_id=(peer, other), device_id_type=MESH)

    for k in range(1, n_samp):
        pl.semaphore_signal(barrier, inc=1, device_id=(s, lax.rem(m + k, n_samp)), device_id_type=MESH)

    for dx, dy in DIRS:
        if dx == 0:
            continue
        peers = peers + jnp.where(there(dx, dy), 1, 0)

        @pl.when(there(dx, dy))
        def _():
            pl.semaphore_signal(barrier, inc=1, device_id=(s + dx, m + dy), device_id_type=MESH)

    loads[0].wait()
    split_rows(f2_flat, f2_ref)
    loads[1].wait()
    split_rows(f1_flat, f1_ref)
    turn_v = one_hot_rows(CIN, size_y)
    loads[2].wait()

    def centre(x, carry):
        value = v_ref[:, x].astype(F32).reshape(CIN * size_y, size_z).astype(BF16)
        value = dot(turn_v, value)
        for y in range(size_y):
            vp[x + 2, y + 2] = value[CIN * y : CIN * (y + 1)].astype(BF16)
        return carry

    lax.fori_loop(0, size_x, centre, 0)
    pl.semaphore_wait(barrier, peers)

    def copy_1(k):
        return pltpu.make_async_remote_copy(
            src_ref=f1_ref, dst_ref=all1.at[m], send_sem=send_1.at[k], recv_sem=recv_1.at[k],
            device_id=(s, lax.rem(m + k, n_samp)), device_id_type=MESH)

    def copy_2(peer):
        return pltpu.make_async_remote_copy(
            src_ref=f2_ref, dst_ref=all2.at[s], send_sem=send_2, recv_sem=recv_2.at[s],
            device_id=(peer, other), device_id_type=MESH)

    def await_2(peer):
        pltpu.make_async_copy(all2.at[peer], all2.at[peer], send_2).wait()
        pltpu.make_async_copy(all2.at[peer], all2.at[peer], recv_2.at[peer]).wait()

    def halo(src, dst, width, send, recv, slot, dx, dy):
        (sx, nx), (tx, _) = spans(dx, size_x, width)
        (sy, ny), (ty, _) = spans(dy, size_y, width)
        return pltpu.make_async_remote_copy(
            src_ref=src.at[pl.ds(sx + width, nx), pl.ds(sy + width, ny)], dst_ref=dst.at[pl.ds(tx, nx), pl.ds(ty, ny)],
            send_sem=send.at[slot], recv_sem=recv.at[slot],
            device_id=(jnp.clip(s + dx, 0, n_space - 1), jnp.clip(m + dy, 0, n_samp - 1)),
            device_id_type=MESH)

    vol = [halo(vp, vp, 2, send_v, recv_v, j, dx, dy) for j, (dx, dy) in enumerate(DIRS)]
    @each_other_far
    def _(peer):
        copy_2(peer).start()

    for k in range(1, n_samp):
        copy_1(k).start()
    for copy, (dx, dy) in zip(vol, DIRS):
        @pl.when(there(dx, dy))
        def _():
            copy.start()

    all1[m] = f1_ref[...]
    all2[s] = f2_ref[...]
    last = size_z - 1
    high_y = size_y + 2

    def lanes(rows):
        return lax.broadcasted_iota(jnp.int32, (rows, size_z), 1)

    width1 = CIN * (size_y + 4)
    width2 = C1 * 6
    build_selectors(s1, s2, q2, width1, width2)
    turn[...] = one_hot_rows(C2, size_y)
    loads[3].wait()

    def turn_c(x, carry):
        value = c_ref[:, x].astype(F32).reshape(C2 * size_y, size_z).astype(BF16)
        cp[x] = dot(turn[...], value).astype(BF16)
        return carry

    lax.fori_loop(0, size_x, turn_c, 0)

    r = lax.broadcasted_iota(jnp.int32, (C2 * size_y, C2 * size_y), 0)
    q = lax.broadcasted_iota(jnp.int32, (C2 * size_y, C2 * size_y), 1)
    from_row = (r % size_y) * C2 + r // size_y
    perm[...] = jnp.where(q == from_row, 1.0, 0.0).astype(BF16)
    acc1[...] = jnp.zeros_like(acc1)
    acc2[...] = jnp.zeros_like(acc2)

    def arrive(group):
        for copy, (dx, dy) in zip(group, DIRS):
            @pl.when(there(-dx, -dy))
            def _():
                copy.wait_recv()

            @pl.when(there(dx, dy))
            def _():
                copy.wait_send()

    for k in range(1, n_samp):
        copy_1(k).wait()
    base1 = dot(gather_rows(all1, rows1, wide1), s1[...])
    for y in range(high_y):
        row = base1 if y == 0 else pltpu.roll(base1, CIN * y, axis=1)
        a1[C1 * y : C1 * (y + 1)] = row[:, : 9 * width1].astype(BF16)

    arrive(vol)
    lane_v = lanes(width1)
    lane_h = lanes(C1 * high_y)
    lane_b = lanes(C2 * 4)

    for x in range(size_x + 4):
        for y in range(vp.shape[1]):
            vf[x, CIN * y : CIN * (y + 1)] = vp[x, y].astype(F32)
    for x in range(size_x + 4):
        value = vf[x]
        before, after = shifted(value, lane_v, last)
        vrows[0, x] = before.astype(BF16)
        vrows[1, x] = value.astype(BF16)
        vrows[2, x] = after.astype(BF16)

    def vwin(x):
        return jnp.concatenate([vrows[kz, x + kx] for kz in range(3) for kx in range(3)], axis=0)

    first_row = jnp.where(m > 0, 1.0, 0.0)
    last_row = jnp.where(m < n_samp - 1, 1.0, 0.0)

    for x in range(size_x + 2):
        p = dot(a1[...], vwin(x))
        slope = jnp.where(p > 0, 1.0, SLOPE)
        if x == 0:
            slope = slope * jnp.where(s > 0, 1.0, 0.0)
        if x == size_x + 1:
            slope = slope * jnp.where(s < n_space - 1, 1.0, 0.0)
        slope = jnp.concatenate(
            [slope[:C1] * first_row, slope[C1 : C1 * (high_y - 1)], slope[C1 * (high_y - 1) :] * last_row], axis=0)
        slope1[x] = slope
        h = p * slope
        before, after = shifted(h, lane_h, last)
        hid[0, x] = before.astype(BF16)
        hid[1, x] = h.astype(BF16)
        hid[2, x] = after.astype(BF16)

    each_other_far(await_2)
    base2 = dot(gather_rows(all2, rows2, wide2), s2[...])
    for y in range(4):
        row = base2 if y == 0 else pltpu.roll(base2, C1 * y, axis=1)
        a2[C2 * y : C2 * (y + 1)] = row[:, : 9 * width2].astype(BF16)
    tall = jnp.concatenate([base2, jnp.zeros((128 - C2, base2.shape[1]), F32)], axis=0).T
    lane_t = lax.broadcasted_iota(jnp.int32, (C1, 128), 1)
    for kx in range(3):
        for kz in range(3):
            tile = 0.0
            for y in range(3):
                first = width2 * (3 * kz + kx) + C1 * (2 - y)
                piece = tall[first : first + C1]
                tile = tile + (piece if y == 0 else pltpu.roll(piece, C2 * y, axis=1))
            column = C2 * size_y * kz
            start = C1 * high_y * kx
            zero = jnp.zeros((C1, 128), BF16)
            for r in range(4):
                turned = tile if r == 0 else pltpu.roll(tile, C2 * r, axis=1)
                main = jnp.where(lane_t >= C2 * r, turned, 0.0).astype(BF16)
                over = jnp.where(lane_t < C2 * r, turned, 0.0).astype(BF16)
                for y in range(high_y):
                    q = (y - 2) // 4
                    if (y - 2) % 4 != r:
                        continue
                    low, high = ((over, zero), (main, over), (zero, main))[q + 1]
                    a3[start + C1 * y : start + C1 * (y + 1), column : column + 128] = low
                    a3[start + C1 * y : start + C1 * (y + 1), column + 128 : column + 256] = high

    for x in range(size_x):
        for half in range(size_y // 4):
            rows = slice(128 * half, 128 * half + 128)
            win = jnp.concatenate(
                [hid[kz, x + kx, 64 * half : 64 * half + width2] for kz in range(3) for kx in range(3)], axis=0)
            p = dot(a2[...], win)
            slope = jnp.where(p > 0, 1.0, SLOPE)
            act[x, rows] = (p * slope).astype(BF16)
            b = (cp[x, rows].astype(F32) * slope).astype(BF16)
            before, after = shifted(b.astype(F32), lane_b, last)
            back[0, x, rows] = after.astype(BF16)
            back[1, x, rows] = b
            back[2, x, rows] = before.astype(BF16)

    for x in range(size_x):
        moved, windows = [], []
        for y in range(0, size_y, 2):
            moved.append(jnp.concatenate([back[kz, x, C2 * y : C2 * y + 64] for kz in range(3)], axis=0))
            windows.append(jnp.concatenate([hid[1, x + kx, C1 * y : C1 * y + 64] for kx in range(3)], axis=0))
        acc2[...] += dot_nt(jnp.concatenate(moved, axis=1), jnp.concatenate(windows, axis=1))

    result = 0.0
    for kz in range(3):
        low = jnp.concatenate([acc2[64 * kz : 64 * kz + C2], jnp.zeros((C2, 64), F32)], axis=1)
        high = jnp.concatenate([acc2[64 * kz + C2 : 64 * kz + 64], jnp.zeros((C2, 64), F32)], axis=1)
        result = result + pick(low + pltpu.roll(high, 256 - C1, axis=1), q2[kz])
    scatter_rows(result, rows2, wide2, grad2)

    def spread_2(peer):
        for j in range(chips):
            pltpu.make_async_remote_copy(
                src_ref=grad2.at[peer], dst_ref=part2.at[s * chips + m // 2], send_sem=send_a2, recv_sem=recv_a2,
                device_id=(peer, across(chips - 1 - j)), device_id_type=MESH).start()

    each_other_far(spread_2)
    spread_2(s)

    rows = C1 * high_y
    for x in range(size_x):
        win = jnp.concatenate([back[kz, x] for kz in range(3)], axis=0)
        d = dot(a3[...], win)
        for kx in range(3):
            share = d[rows * kx : rows * (kx + 1)]
            if x == 0 or kx == 2:
                dhid[x + kx] = share
            else:
                dhid[x + kx] += share
    for x in range(size_x + 2):
        b1 = (dhid[x] * slope1[x]).astype(BF16)
        acc1[:, : 9 * width1] += dot_nt(b1, vwin(x))

    total1 = acc1[:C1]
    for y in range(1, high_y):
        total1 = total1 + pltpu.roll(acc1[C1 * y : C1 * (y + 1)], acc1.shape[1] - CIN * y, axis=1)
    scatter_rows(pick(total1, s1[...]), rows1, wide1, grad1)

    everyone = n_space * n_samp
    me = s * n_samp + m

    def to_one(ps, pm):
        pltpu.make_async_remote_copy(
            src_ref=grad1.at[pm], dst_ref=part1.at[me], send_sem=send_a1, recv_sem=recv_a1,
            device_id=(ps, pm), device_id_type=MESH).start()

    @each_other_far
    def _(peer):
        for j in range(n_samp):
            to_one(peer, lax.rem(m + n_samp - 1 - j, n_samp))

    for k in range(1, n_samp):
        to_one(s, lax.rem(m + k, n_samp))

    def send_act(x, carry):
        value = dot(perm[...], act[x])
        act_ref[:, x] = value.reshape(C2, size_y, size_z).astype(BF16)
        return carry

    lax.fori_loop(0, size_x, send_act, 0)
    part1[me] = grad1[m]
    pltpu.make_async_copy(part2, part2, send_a2).wait()
    pltpu.make_async_copy(part2, part2, recv_a2).wait()
    mine2[...] = jnp.sum(part2[...], axis=0)
    swap = pltpu.make_async_remote_copy(
        src_ref=mine2, dst_ref=full2, send_sem=send_b2, recv_sem=recv_b2,
        device_id=(s, other), device_id_type=MESH)
    swap.start()
    swap.wait()
    o2_ref[...] = flatten((mine2[...] + full2[...]) * scale)
    others = part1.at[pl.ds(0, everyone - 1)]
    pltpu.make_async_copy(others, others, send_a1).wait()
    pltpu.make_async_copy(others, others, recv_a1).wait()
    o1_ref[...] = flatten(jnp.sum(part1[...], axis=0) * scale)


def store_kernel(act, o1, o2, act_out, o1_out, o2_out, done):
    copies = [
        pltpu.make_async_copy(src, dst, done.at[j])
        for j, (src, dst) in enumerate(((act, act_out), (o1, o1_out), (o2, o2_out)))
    ]
    for copy in copies:
        copy.start()
    for copy in copies:
        copy.wait()


VMEM = pl.BlockSpec(memory_space=pltpu.VMEM)
HBM = pl.BlockSpec(memory_space=pltpu.HBM)


def on_device(n_space, n_samp, volume, filters_one, filters_two, cotangent):
    _, size_x, size_y, size_z = volume.shape
    len1 = filters_one.shape[0]
    len2 = filters_two.shape[0]
    unit1 = math.gcd(len1, 27 * CIN)
    unit2 = math.gcd(len2, 27 * C1)
    piece1 = (len1 // unit1, unit1)
    piece2 = (len2 // unit2, unit2)
    high_y = size_y + 2
    width1 = CIN * (size_y + 4)
    scale = 1.0 / math.sqrt(float(size_x * n_space * size_y * n_samp * size_z))
    samp, space = pltpu.SemaphoreType.DMA((n_samp,)), pltpu.SemaphoreType.DMA((n_space,))
    sides, one = pltpu.SemaphoreType.DMA((8,)), pltpu.SemaphoreType.DMA
    activation, out1, out2 = pl.pallas_call(
        functools.partial(fused_kernel, n_space, n_samp, scale),
        out_shape=[
            jax.ShapeDtypeStruct((C2, size_x, size_y, size_z), BF16),
            jax.ShapeDtypeStruct((len1,), F32),
            jax.ShapeDtypeStruct((len2,), F32),
        ],
        in_specs=[HBM] * 4,
        out_specs=[VMEM] * 3,
        scratch_shapes=[
            pltpu.VMEM(volume.shape, BF16),
            pltpu.VMEM(cotangent.shape, BF16),
            pltpu.VMEM((len1,), BF16),
            pltpu.VMEM((len2,), BF16),
            pltpu.VMEM(piece1, BF16),
            pltpu.VMEM(piece2, BF16),
            pltpu.SemaphoreType.DMA((4,)),
            pltpu.VMEM((size_x + 4, size_y + 4, CIN, size_z), BF16),
            pltpu.VMEM((size_x, C2 * size_y, size_z), BF16),
            pltpu.VMEM((n_samp, *piece1), BF16),
            pltpu.VMEM((n_space, *piece2), BF16),
            pltpu.VMEM((C2 * size_y, C2 * size_y), BF16),
            pltpu.VMEM((C1 * high_y, 9 * width1), BF16),
            pltpu.VMEM((C2 * 4, 9 * C1 * 6), BF16),
            pltpu.VMEM((3 * C1 * high_y, 3 * C2 * size_y), BF16),
            pltpu.VMEM((size_x + 2, C1 * high_y, size_z), F32),
            pltpu.VMEM((3, size_x + 2, C1 * high_y, size_z), BF16),
            pltpu.VMEM((3, size_x, C2 * size_y, size_z), BF16),
            pltpu.VMEM((size_x + 2, C1 * high_y, size_z), F32),
            pltpu.VMEM((C2 * size_y, C2 * size_y), BF16),
            pltpu.VMEM((C1 * high_y, 512), F32),
            pltpu.VMEM((192, 192), F32),
            pltpu.VMEM((size_x, C2 * size_y, size_z), BF16),
            pltpu.VMEM((27 * CIN, 512), BF16),
            pltpu.VMEM((27 * C1, 896), BF16),
            pltpu.VMEM((3, 27 * C1, 256), BF16),
            pltpu.VMEM((n_samp * piece1[0], piece1[1]), F32),
            pltpu.VMEM((C1, 27 * CIN), F32),
            pltpu.VMEM((n_space * piece2[0], piece2[1]), F32),
            pltpu.VMEM((C2, 27 * C1), F32),
            pltpu.VMEM((size_x + 4, width1, size_z), F32),
            pltpu.VMEM((3, size_x + 4, width1, size_z), BF16),
            pltpu.VMEM((n_samp, *piece1), F32),
            pltpu.VMEM((n_space, *piece2), F32),
            pltpu.VMEM((n_space * n_samp, *piece1), F32),
            pltpu.VMEM((n_space * (n_samp // 2), *piece2), F32),
            pltpu.VMEM(piece2, F32),
            pltpu.VMEM(piece2, F32),
            sides, sides, samp, samp, one, space,
            one, one, one, one, one, one,
        ],
        compiler_params=pltpu.CompilerParams(
            collective_id=0, has_side_effects=True, vmem_limit_bytes=48 * 2**20),
    )(*(pltpu.with_memory_space_constraint(x, pltpu.HBM)
        for x in (volume, cotangent, filters_one, filters_two)))
    return pl.pallas_call(
        store_kernel,
        out_shape=[jax.ShapeDtypeStruct(x.shape, x.dtype) for x in (activation, out1, out2)],
        in_specs=[VMEM] * 3,
        out_specs=[HBM] * 3,
        scratch_shapes=[pltpu.SemaphoreType.DMA((3,))],
        compiler_params=pltpu.CompilerParams(vmem_limit_bytes=2**20),
    )(activation, out1, out2)


def solution(mesh):
    in_specs = (
        P(None, "space", "samp", None),
        P("samp"),
        P("space"),
        P(None, "space", "samp", None),
    )
    out_specs = (P(None, "space", "samp", None), P("samp"), P("space"))
    return jax.shard_map(
        functools.partial(on_device, mesh.shape["space"], mesh.shape["samp"]),
        mesh=mesh, in_specs=in_specs, out_specs=out_specs, check_vma=False,
    )
```

```python
import functools
import math

import jax
import jax.numpy as jnp
from jax import lax
from jax.experimental import pallas as pl
from jax.experimental.pallas import tpu as pltpu
from jax.sharding import PartitionSpec as P

CIN = 4
C1 = 16
C2 = 32
SLOPE = 0.3
MESH = pl.DeviceIdType.MESH
F32 = jnp.float32
BF16 = jnp.bfloat16
DIRS = [(dx, dy) for dx in (-1, 0, 1) for dy in (-1, 0, 1) if (dx, dy) != (0, 0)]


def spans(delta, size, width):
    if delta == 1:
        return (size - width, width), (0, width)
    if delta == -1:
        return (0, width), (size + width, width)
    return (0, size), (width, size)


def leaky(values):
    return jnp.where(values > 0, values, SLOPE * values)


def shifted(values, lane, last):
    before = jnp.where(lane == 0, 0.0, pltpu.roll(values, 1, axis=1))
    after = jnp.where(lane == last, 0.0, pltpu.roll(values, last, axis=1))
    return before, after


def dot(a, b):
    return lax.dot_general(a, b, (((1,), (0,)), ((), ())), preferred_element_type=F32)


def dot_nt(a, b):
    return lax.dot_general(a, b, (((1,), (1,)), ((), ())), preferred_element_type=F32)


def one_hot(rows, source):
    row = lax.broadcasted_iota(jnp.int32, (rows, source.shape[1]), 0)
    return jnp.where(row == source, 1.0, 0.0).astype(BF16)


def one_hot_rows(chans, size_y):
    r = lax.broadcasted_iota(jnp.int32, (chans * size_y, chans * size_y), 0)
    q = lax.broadcasted_iota(jnp.int32, (chans * size_y, chans * size_y), 1)
    return jnp.where(q == (r % chans) * size_y + r // chans, 1.0, 0.0).astype(BF16)


def build_selectors(s1, s2, q2, width1, width2):
    lane = lax.broadcasted_iota(jnp.int32, (1, s1.shape[1]), 1)
    group, rest = lax.div(lane, width1), lax.rem(lane, width1)
    kz, kx, ky, i = lax.div(group, 3), lax.rem(group, 3), lax.div(rest, CIN), lax.rem(rest, CIN)
    s1[...] = one_hot(27 * CIN, jnp.where((group < 9) & (ky < 3), i * 27 + kx * 9 + ky * 3 + kz, -9))
    lane = lax.broadcasted_iota(jnp.int32, (1, s2.shape[1]), 1)
    group, rest = lax.div(lane, width2), lax.rem(lane, width2)
    kz, kx, ky, i = lax.div(group, 3), lax.rem(group, 3), lax.div(rest, C1), lax.rem(rest, C1)
    s2[...] = one_hot(27 * C1, jnp.where((group < 9) & (ky < 3), i * 27 + kx * 9 + ky * 3 + kz, -9))
    lane = lax.broadcasted_iota(jnp.int32, (1, 256), 1)
    kx, ky, i = lane >> 6, (lane >> 4) & 3, lane & 15
    source = jnp.where((kx < 3) & (ky < 3), i * 27 + kx * 9 + ky * 3, -9)
    for kz in range(3):
        q2[kz] = one_hot(27 * C1, source + kz)


def split_rows(flat_ref, rows_ref):
    rows, unit = rows_ref.shape
    flat = flat_ref[...].astype(F32).reshape(1, rows * unit)
    rows_ref[...] = jnp.concatenate(
        [flat[:, unit * k : unit * (k + 1)] for k in range(rows)], axis=0).astype(BF16)


def flatten(rows):
    return jnp.concatenate([rows[k : k + 1] for k in range(rows.shape[0])], axis=1).reshape(rows.size)


def gather_rows(all_ref, rows_ref, wide_ref):
    owners, count, unit = all_ref.shape
    for j in range(owners):
        rows_ref[count * j : count * (j + 1)] = all_ref[j].astype(F32)
    split = wide_ref.shape[1] // unit
    if split == 1:
        return rows_ref[...].astype(BF16)
    for k in range(split):
        wide_ref[:, unit * k : unit * (k + 1)] = rows_ref[pl.ds(k, wide_ref.shape[0], stride=split)]
    return wide_ref[...].astype(BF16)


def scatter_rows(value, rows_ref, wide_ref, out_ref):
    owners, count, unit = out_ref.shape
    split = value.shape[1] // unit
    if split == 1:
        rows_ref[...] = value
    else:
        wide_ref[...] = value
        for k in range(split):
            rows_ref[pl.ds(k, value.shape[0], stride=split)] = wide_ref[:, unit * k : unit * (k + 1)]
    for j in range(owners):
        out_ref[j] = rows_ref[count * j : count * (j + 1)]


def split3(g):
    high = g.astype(BF16)
    rest = g - high.astype(F32)
    mid = rest.astype(BF16)
    low = (rest - mid.astype(F32)).astype(BF16)
    return jnp.concatenate([high, mid, low], axis=0)


def pick(g, selector):
    rows = g.shape[0]
    r = dot_nt(split3(g), selector)
    return r[:rows] + r[rows : 2 * rows] + r[2 * rows :]


def fused_kernel(
    n_space, n_samp, scale, v_hbm, c_hbm, f1_hbm, f2_hbm, act_ref, o1_ref, o2_ref,
    v_ref, c_ref, f1_flat, f2_flat, f1_ref, f2_ref, load,
    vp, cp, all1, all2,
    turn, a1, a2, a3, dhid, hid, back, slope1, perm, acc1, acc2, act,
    s1, s2, q2, rows1, wide1, rows2, wide2, vf, vrows,
    grad1, grad2, part1, part2, full2, mine2,
    send_v, recv_v, send_1, recv_1, send_2, recv_2,
    send_a1, recv_a1, send_a2, recv_a2, send_b2, recv_b2,
):
    s = lax.axis_index("space")
    m = lax.axis_index("samp")
    size_x, size_y, size_z = v_ref.shape[1:]
    other = m + 1 - 2 * lax.rem(m, 2)
    chips = n_samp // 2
    turn_sign = 1 - 2 * ((2 * s) // n_space)

    def far(k):
        return lax.rem(2 * n_space + s - turn_sign * k, n_space)

    def across(j):
        return lax.rem(other + 2 * j, n_samp)

    def each_other_far(body):
        if n_space <= 16:
            for k in range(1, n_space):
                body(far(k))
            return

        def step(k, carry):
            body(far(k))
            return carry

        lax.fori_loop(1, n_space, step, 0)

    def there(dx, dy):
        return (s + dx >= 0) & (s + dx < n_space) & (m + dy >= 0) & (m + dy < n_samp)

    barrier = pltpu.get_barrier_semaphore()
    peers = n_samp - 1 + n_space - 1
    @each_other_far
    def _(peer):
        pl.semaphore_signal(barrier, inc=1, device_id=(peer, other), device_id_type=MESH)

    for k in range(1, n_samp):
        pl.semaphore_signal(barrier, inc=1, device_id=(s, lax.rem(m + k, n_samp)), device_id_type=MESH)

    for dx, dy in DIRS:
        if dx == 0:
            continue
        peers = peers + jnp.where(there(dx, dy), 1, 0)

        @pl.when(there(dx, dy))
        def _():
            pl.semaphore_signal(barrier, inc=1, device_id=(s + dx, m + dy), device_id_type=MESH)

    loads = [
        pltpu.make_async_copy(src, dst, load.at[j])
        for j, (src, dst) in enumerate(
            ((f2_hbm, f2_flat), (f1_hbm, f1_flat), (v_hbm, v_ref), (c_hbm, c_ref)))
    ]
    for copy in loads:
        copy.start()
    for dx, dy in DIRS:
        (_, nx), (tx, _) = spans(-dx, size_x, 2)
        (_, ny), (ty, _) = spans(-dy, size_y, 2)

        @pl.when(jnp.logical_not(there(dx, dy)))
        def _():
            vp[tx : tx + nx, ty : ty + ny] = jnp.zeros((nx, ny, CIN, size_z), BF16)

    loads[0].wait()
    split_rows(f2_flat, f2_ref)
    loads[1].wait()
    split_rows(f1_flat, f1_ref)
    turn_v = one_hot_rows(CIN, size_y)
    loads[2].wait()

    def centre(x, carry):
        value = v_ref[:, x].astype(F32).reshape(CIN * size_y, size_z).astype(BF16)
        value = dot(turn_v, value)
        for y in range(size_y):
            vp[x + 2, y + 2] = value[CIN * y : CIN * (y + 1)].astype(BF16)
        return carry

    lax.fori_loop(0, size_x, centre, 0)
    pl.semaphore_wait(barrier, peers)

    def copy_1(k):
        return pltpu.make_async_remote_copy(
            src_ref=f1_ref, dst_ref=all1.at[m], send_sem=send_1.at[k], recv_sem=recv_1.at[k],
            device_id=(s, lax.rem(m + k, n_samp)), device_id_type=MESH)

    def copy_2(peer):
        return pltpu.make_async_remote_copy(
            src_ref=f2_ref, dst_ref=all2.at[s], send_sem=send_2, recv_sem=recv_2.at[s],
            device_id=(peer, other), device_id_type=MESH)

    def await_2(peer):
        pltpu.make_async_copy(all2.at[peer], all2.at[peer], send_2).wait()
        pltpu.make_async_copy(all2.at[peer], all2.at[peer], recv_2.at[peer]).wait()

    def halo(src, dst, width, send, recv, slot, dx, dy):
        (sx, nx), (tx, _) = spans(dx, size_x, width)
        (sy, ny), (ty, _) = spans(dy, size_y, width)
        return pltpu.make_async_remote_copy(
            src_ref=src.at[pl.ds(sx + width, nx), pl.ds(sy + width, ny)], dst_ref=dst.at[pl.ds(tx, nx), pl.ds(ty, ny)],
            send_sem=send.at[slot], recv_sem=recv.at[slot],
            device_id=(jnp.clip(s + dx, 0, n_space - 1), jnp.clip(m + dy, 0, n_samp - 1)),
            device_id_type=MESH)

    vol = [halo(vp, vp, 2, send_v, recv_v, j, dx, dy) for j, (dx, dy) in enumerate(DIRS)]
    @each_other_far
    def _(peer):
        copy_2(peer).start()

    for k in range(1, n_samp):
        copy_1(k).start()
    for copy, (dx, dy) in zip(vol, DIRS):
        @pl.when(there(dx, dy))
        def _():
            copy.start()

    all1[m] = f1_ref[...]
    all2[s] = f2_ref[...]
    last = size_z - 1
    high_y = size_y + 2

    def lanes(rows):
        return lax.broadcasted_iota(jnp.int32, (rows, size_z), 1)

    width1 = CIN * (size_y + 4)
    width2 = C1 * 6
    build_selectors(s1, s2, q2, width1, width2)
    turn[...] = one_hot_rows(C2, size_y)
    loads[3].wait()

    def turn_c(x, carry):
        value = c_ref[:, x].astype(F32).reshape(C2 * size_y, size_z).astype(BF16)
        cp[x] = dot(turn[...], value).astype(BF16)
        return carry

    lax.fori_loop(0, size_x, turn_c, 0)

    r = lax.broadcasted_iota(jnp.int32, (C2 * size_y, C2 * size_y), 0)
    q = lax.broadcasted_iota(jnp.int32, (C2 * size_y, C2 * size_y), 1)
    from_row = (r % size_y) * C2 + r // size_y
    perm[...] = jnp.where(q == from_row, 1.0, 0.0).astype(BF16)
    acc1[...] = jnp.zeros_like(acc1)
    acc2[...] = jnp.zeros_like(acc2)

    def arrive(group):
        for copy, (dx, dy) in zip(group, DIRS):
            @pl.when(there(-dx, -dy))
            def _():
                copy.wait_recv()

            @pl.when(there(dx, dy))
            def _():
                copy.wait_send()

    for k in range(1, n_samp):
        copy_1(k).wait()
    base1 = dot(gather_rows(all1, rows1, wide1), s1[...])
    for y in range(high_y):
        row = base1 if y == 0 else pltpu.roll(base1, CIN * y, axis=1)
        a1[C1 * y : C1 * (y + 1)] = row[:, : 9 * width1].astype(BF16)

    arrive(vol)
    lane_v = lanes(width1)
    lane_h = lanes(C1 * high_y)
    lane_b = lanes(C2 * 4)

    for x in range(size_x + 4):
        for y in range(vp.shape[1]):
            vf[x, CIN * y : CIN * (y + 1)] = vp[x, y].astype(F32)
    for x in range(size_x + 4):
        value = vf[x]
        before, after = shifted(value, lane_v, last)
        vrows[0, x] = before.astype(BF16)
        vrows[1, x] = value.astype(BF16)
        vrows[2, x] = after.astype(BF16)

    def vwin(x):
        return jnp.concatenate([vrows[kz, x + kx] for kz in range(3) for kx in range(3)], axis=0)

    first_row = jnp.where(m > 0, 1.0, 0.0)
    last_row = jnp.where(m < n_samp - 1, 1.0, 0.0)

    for x in range(size_x + 2):
        p = dot(a1[...], vwin(x))
        slope = jnp.where(p > 0, 1.0, SLOPE)
        if x == 0:
            slope = slope * jnp.where(s > 0, 1.0, 0.0)
        if x == size_x + 1:
            slope = slope * jnp.where(s < n_space - 1, 1.0, 0.0)
        slope = jnp.concatenate(
            [slope[:C1] * first_row, slope[C1 : C1 * (high_y - 1)], slope[C1 * (high_y - 1) :] * last_row], axis=0)
        slope1[x] = slope
        h = p * slope
        before, after = shifted(h, lane_h, last)
        hid[0, x] = before.astype(BF16)
        hid[1, x] = h.astype(BF16)
        hid[2, x] = after.astype(BF16)

    each_other_far(await_2)
    base2 = dot(gather_rows(all2, rows2, wide2), s2[...])
    for y in range(4):
        row = base2 if y == 0 else pltpu.roll(base2, C1 * y, axis=1)
        a2[C2 * y : C2 * (y + 1)] = row[:, : 9 * width2].astype(BF16)
    tall = jnp.concatenate([base2, jnp.zeros((128 - C2, base2.shape[1]), F32)], axis=0).T
    lane_t = lax.broadcasted_iota(jnp.int32, (C1, 128), 1)
    for kx in range(3):
        for kz in range(3):
            tile = 0.0
            for y in range(3):
                first = width2 * (3 * kz + kx) + C1 * (2 - y)
                piece = tall[first : first + C1]
                tile = tile + (piece if y == 0 else pltpu.roll(piece, C2 * y, axis=1))
            turns = [tile] + [pltpu.roll(tile, C2 * r, axis=1) for r in range(1, 4)]
            for y in range(6):
                turned = turns[(y + 2) % 4]
                if y < 2:
                    turned = jnp.where(lane_t < C2 * (y + 2), turned, 0.0)
                elif y > 3:
                    turned = jnp.where(lane_t >= C2 * (y - 2), turned, 0.0)
                first = C1 * (6 * kx + y)
                a3[first : first + C1, 128 * kz : 128 * kz + 128] = turned.astype(BF16)

    for x in range(size_x):
        for half in range(size_y // 4):
            rows = slice(128 * half, 128 * half + 128)
            win = jnp.concatenate(
                [hid[kz, x + kx, 64 * half : 64 * half + width2] for kz in range(3) for kx in range(3)], axis=0)
            p = dot(a2[...], win)
            slope = jnp.where(p > 0, 1.0, SLOPE)
            act[x, rows] = (p * slope).astype(BF16)
            b = (cp[x, rows].astype(F32) * slope).astype(BF16)
            before, after = shifted(b.astype(F32), lane_b, last)
            back[0, x, rows] = after.astype(BF16)
            back[1, x, rows] = b
            back[2, x, rows] = before.astype(BF16)

    for x in range(size_x):
        moved, windows = [], []
        for y in range(0, size_y, 2):
            moved.append(jnp.concatenate([back[kz, x, C2 * y : C2 * y + 64] for kz in range(3)], axis=0))
            windows.append(jnp.concatenate([hid[1, x + kx, C1 * y : C1 * y + 64] for kx in range(3)], axis=0))
        acc2[...] += dot_nt(jnp.concatenate(moved, axis=1), jnp.concatenate(windows, axis=1))

    result = 0.0
    for kz in range(3):
        low = jnp.concatenate([acc2[64 * kz : 64 * kz + C2], jnp.zeros((C2, 64), F32)], axis=1)
        high = jnp.concatenate([acc2[64 * kz + C2 : 64 * kz + 64], jnp.zeros((C2, 64), F32)], axis=1)
        result = result + pick(low + pltpu.roll(high, 256 - C1, axis=1), q2[kz])
    scatter_rows(result, rows2, wide2, grad2)

    def spread_2(peer):
        pltpu.make_async_remote_copy(
            src_ref=grad2.at[peer], dst_ref=part2.at[s], send_sem=send_a2, recv_sem=recv_a2,
            device_id=(peer, other), device_id_type=MESH).start()

    each_other_far(spread_2)
    spread_2(s)

    span = C1 * 6
    for x in range(size_x):
        halves = []
        for half in range(size_y // 4):
            win = jnp.concatenate([back[kz, x, 128 * half : 128 * half + 128] for kz in range(3)], axis=0)
            halves.append(dot(a3[...], win))
        for kx in range(3):
            low, high = (d[span * kx : span * (kx + 1)] for d in halves)
            share = jnp.concatenate([low[:64], low[64:] + high[:32], high[32:]], axis=0)
            if x == 0 or kx == 2:
                dhid[x + kx] = share
            else:
                dhid[x + kx] += share
    for x in range(size_x + 2):
        b1 = (dhid[x] * slope1[x]).astype(BF16)
        acc1[:, : 9 * width1] += dot_nt(b1, vwin(x))

    total1 = acc1[:C1]
    for y in range(1, high_y):
        total1 = total1 + pltpu.roll(acc1[C1 * y : C1 * (y + 1)], acc1.shape[1] - CIN * y, axis=1)
    scatter_rows(pick(total1, s1[...]), rows1, wide1, grad1)

    everyone = n_space * n_samp
    me = s * n_samp + m

    def to_one(ps, pm):
        pltpu.make_async_remote_copy(
            src_ref=grad1.at[pm], dst_ref=part1.at[me], send_sem=send_a1, recv_sem=recv_a1,
            device_id=(ps, pm), device_id_type=MESH).start()

    @each_other_far
    def _(peer):
        for j in range(n_samp):
            to_one(peer, lax.rem(m + n_samp - 1 - j, n_samp))

    for k in range(1, n_samp):
        to_one(s, lax.rem(m + k, n_samp))

    def send_act(x, carry):
        value = dot(perm[...], act[x])
        act_ref[:, x] = value.reshape(C2, size_y, size_z).astype(BF16)
        return carry

    lax.fori_loop(0, size_x, send_act, 0)
    part1[me] = grad1[m]
    pltpu.make_async_copy(part2, part2, send_a2).wait()
    pltpu.make_async_copy(part2, part2, recv_a2).wait()
    mine2[...] = jnp.sum(part2[...], axis=0)
    for k in range(n_samp - 1, 0, -1):
        pltpu.make_async_remote_copy(
            src_ref=mine2, dst_ref=full2.at[m], send_sem=send_b2, recv_sem=recv_b2,
            device_id=(s, lax.rem(m + k, n_samp)), device_id_type=MESH).start()
    full2[m] = mine2[...]
    rest = full2.at[pl.ds(0, n_samp - 1)]
    pltpu.make_async_copy(rest, rest, send_b2).wait()
    pltpu.make_async_copy(rest, rest, recv_b2).wait()
    o2_ref[...] = flatten(jnp.sum(full2[...], axis=0) * scale)
    others = part1.at[pl.ds(0, everyone - 1)]
    pltpu.make_async_copy(others, others, send_a1).wait()
    pltpu.make_async_copy(others, others, recv_a1).wait()
    o1_ref[...] = flatten(jnp.sum(part1[...], axis=0) * scale)


def store_kernel(act, o1, o2, act_out, o1_out, o2_out, done):
    pieces = done.shape[0] - 2
    step = C2 // pieces
    pairs = [(o1, o1_out), (o2, o2_out)]
    for j in range(pieces):
        pairs.append((act.at[pl.ds(step * j, step)], act_out.at[pl.ds(step * j, step)]))
    copies = [pltpu.make_async_copy(src, dst, done.at[j]) for j, (src, dst) in enumerate(pairs)]
    for copy in copies:
        copy.start()
    for copy in copies:
        copy.wait()


VMEM = pl.BlockSpec(memory_space=pltpu.VMEM)
HBM = pl.BlockSpec(memory_space=pltpu.HBM)


def on_device(n_space, n_samp, volume, filters_one, filters_two, cotangent):
    _, size_x, size_y, size_z = volume.shape
    len1 = filters_one.shape[0]
    len2 = filters_two.shape[0]
    unit1 = math.gcd(len1, 27 * CIN)
    unit2 = math.gcd(len2, 27 * C1)
    piece1 = (len1 // unit1, unit1)
    piece2 = (len2 // unit2, unit2)
    high_y = size_y + 2
    width1 = CIN * (size_y + 4)
    scale = 1.0 / math.sqrt(float(size_x * n_space * size_y * n_samp * size_z))
    samp, space = pltpu.SemaphoreType.DMA((n_samp,)), pltpu.SemaphoreType.DMA((n_space,))
    sides, one = pltpu.SemaphoreType.DMA((8,)), pltpu.SemaphoreType.DMA
    activation, out1, out2 = pl.pallas_call(
        functools.partial(fused_kernel, n_space, n_samp, scale),
        out_shape=[
            jax.ShapeDtypeStruct((C2, size_x, size_y, size_z), BF16),
            jax.ShapeDtypeStruct((len1,), F32),
            jax.ShapeDtypeStruct((len2,), F32),
        ],
        in_specs=[HBM] * 4,
        out_specs=[VMEM] * 3,
        scratch_shapes=[
            pltpu.VMEM(volume.shape, BF16),
            pltpu.VMEM(cotangent.shape, BF16),
            pltpu.VMEM((len1,), BF16),
            pltpu.VMEM((len2,), BF16),
            pltpu.VMEM(piece1, BF16),
            pltpu.VMEM(piece2, BF16),
            pltpu.SemaphoreType.DMA((4,)),
            pltpu.VMEM((size_x + 4, size_y + 4, CIN, size_z), BF16),
            pltpu.VMEM((size_x, C2 * size_y, size_z), BF16),
            pltpu.VMEM((n_samp, *piece1), BF16),
            pltpu.VMEM((n_space, *piece2), BF16),
            pltpu.VMEM((C2 * size_y, C2 * size_y), BF16),
            pltpu.VMEM((C1 * high_y, 9 * width1), BF16),
            pltpu.VMEM((C2 * 4, 9 * C1 * 6), BF16),
            pltpu.VMEM((18 * C1, 12 * C2), BF16),
            pltpu.VMEM((size_x + 2, C1 * high_y, size_z), F32),
            pltpu.VMEM((3, size_x + 2, C1 * high_y, size_z), BF16),
            pltpu.VMEM((3, size_x, C2 * size_y, size_z), BF16),
            pltpu.VMEM((size_x + 2, C1 * high_y, size_z), F32),
            pltpu.VMEM((C2 * size_y, C2 * size_y), BF16),
            pltpu.VMEM((C1 * high_y, 512), F32),
            pltpu.VMEM((192, 192), F32),
            pltpu.VMEM((size_x, C2 * size_y, size_z), BF16),
            pltpu.VMEM((27 * CIN, 512), BF16),
            pltpu.VMEM((27 * C1, 896), BF16),
            pltpu.VMEM((3, 27 * C1, 256), BF16),
            pltpu.VMEM((n_samp * piece1[0], piece1[1]), F32),
            pltpu.VMEM((C1, 27 * CIN), F32),
            pltpu.VMEM((n_space * piece2[0], piece2[1]), F32),
            pltpu.VMEM((C2, 27 * C1), F32),
            pltpu.VMEM((size_x + 4, width1, size_z), F32),
            pltpu.VMEM((3, size_x + 4, width1, size_z), BF16),
            pltpu.VMEM((n_samp, *piece1), F32),
            pltpu.VMEM((n_space, *piece2), F32),
            pltpu.VMEM((n_space * n_samp, *piece1), F32),
            pltpu.VMEM((n_space, *piece2), F32),
            pltpu.VMEM((n_samp, *piece2), F32),
            pltpu.VMEM(piece2, F32),
            sides, sides, samp, samp, one, space,
            one, one, one, one, one, one,
        ],
        compiler_params=pltpu.CompilerParams(
            collective_id=0, has_side_effects=True, vmem_limit_bytes=48 * 2**20),
    )(*(pltpu.with_memory_space_constraint(x, pltpu.HBM)
        for x in (volume, cotangent, filters_one, filters_two)))
    return pl.pallas_call(
        store_kernel,
        out_shape=[jax.ShapeDtypeStruct(x.shape, x.dtype) for x in (activation, out1, out2)],
        in_specs=[VMEM] * 3,
        out_specs=[HBM] * 3,
        scratch_shapes=[pltpu.SemaphoreType.DMA((6,))],
        compiler_params=pltpu.CompilerParams(vmem_limit_bytes=2**20),
    )(activation, out1, out2)


def solution(mesh):
    in_specs = (
        P(None, "space", "samp", None),
        P("samp"),
        P("space"),
        P(None, "space", "samp", None),
    )
    out_specs = (P(None, "space", "samp", None), P("samp"), P("space"))
    return jax.shard_map(
        functools.partial(on_device, mesh.shape["space"], mesh.shape["samp"]),
        mesh=mesh, in_specs=in_specs, out_specs=out_specs, check_vma=False,
    )
```

```python
import functools
import math

import jax
import jax.numpy as jnp
from jax import lax
from jax.experimental import pallas as pl
from jax.experimental.pallas import tpu as pltpu
from jax.sharding import PartitionSpec as P

CIN = 4
C1 = 16
C2 = 32
SLOPE = 0.3
MESH = pl.DeviceIdType.MESH
F32 = jnp.float32
BF16 = jnp.bfloat16
DIRS = [(dx, dy) for dx in (-1, 0, 1) for dy in (-1, 0, 1) if (dx, dy) != (0, 0)]


def spans(delta, size, width):
    if delta == 1:
        return (size - width, width), (0, width)
    if delta == -1:
        return (0, width), (size + width, width)
    return (0, size), (width, size)


def leaky(values):
    return jnp.where(values > 0, values, SLOPE * values)


def shifted(values, lane, last):
    before = jnp.where(lane == 0, 0.0, pltpu.roll(values, 1, axis=1))
    after = jnp.where(lane == last, 0.0, pltpu.roll(values, last, axis=1))
    return before, after


def dot(a, b):
    return lax.dot_general(a, b, (((1,), (0,)), ((), ())), preferred_element_type=F32)


def dot_nt(a, b):
    return lax.dot_general(a, b, (((1,), (1,)), ((), ())), preferred_element_type=F32)


def one_hot(rows, source):
    row = lax.broadcasted_iota(jnp.int32, (rows, source.shape[1]), 0)
    return jnp.where(row == source, 1.0, 0.0).astype(BF16)


def one_hot_rows(chans, size_y):
    r = lax.broadcasted_iota(jnp.int32, (chans * size_y, chans * size_y), 0)
    q = lax.broadcasted_iota(jnp.int32, (chans * size_y, chans * size_y), 1)
    return jnp.where(q == (r % chans) * size_y + r // chans, 1.0, 0.0).astype(BF16)


def build_selectors(s1, q2, width1):
    lane = lax.broadcasted_iota(jnp.int32, (1, s1.shape[1]), 1)
    group, rest = lax.div(lane, width1), lax.rem(lane, width1)
    kz, kx, ky, i = lax.div(group, 3), lax.rem(group, 3), lax.div(rest, CIN), lax.rem(rest, CIN)
    s1[...] = one_hot(27 * CIN, jnp.where((group < 9) & (ky < 3), i * 27 + kx * 9 + ky * 3 + kz, -9))
    lane = lax.broadcasted_iota(jnp.int32, (1, 256), 1)
    kx, ky, i = lane >> 6, (lane >> 4) & 3, lane & 15
    source = jnp.where((kx < 3) & (ky < 3), i * 27 + kx * 9 + ky * 3, -9)
    for kz in range(3):
        q2[:, 256 * kz : 256 * kz + 256] = one_hot(27 * C1, source + kz)


def build_order(s2):
    lane = lax.broadcasted_iota(jnp.int32, (1, s2.shape[1]), 1)
    tap, i = lane >> 4, lane & 15
    ky, kz, kx = lax.div(tap, 9), lax.rem(lax.div(tap, 3), 3), lax.rem(tap, 3)
    s2[...] = one_hot(27 * C1, jnp.where(tap < 27, i * 27 + kx * 9 + ky * 3 + kz, -9))


def split_rows(flat_ref, rows_ref):
    rows, unit = rows_ref.shape
    flat = flat_ref[...].astype(F32).reshape(1, rows * unit)
    rows_ref[...] = jnp.concatenate(
        [flat[:, unit * k : unit * (k + 1)] for k in range(rows)], axis=0).astype(BF16)


def flatten(rows):
    return jnp.concatenate([rows[k : k + 1] for k in range(rows.shape[0])], axis=1).reshape(rows.size)


def gather_rows(all_ref, rows_ref, wide_ref):
    owners, count, unit = all_ref.shape
    for j in range(owners):
        rows_ref[count * j : count * (j + 1)] = all_ref[j].astype(F32)
    split = wide_ref.shape[1] // unit
    if split == 1:
        return rows_ref[...].astype(BF16)
    for k in range(split):
        wide_ref[:, unit * k : unit * (k + 1)] = rows_ref[pl.ds(k, wide_ref.shape[0], stride=split)]
    return wide_ref[...].astype(BF16)


def scatter_rows(value, rows_ref, wide_ref, out_ref):
    owners, count, unit = out_ref.shape
    split = value.shape[1] // unit
    if split == 1:
        rows_ref[...] = value
    else:
        wide_ref[...] = value
        for k in range(split):
            rows_ref[pl.ds(k, value.shape[0], stride=split)] = wide_ref[:, unit * k : unit * (k + 1)]
    for j in range(owners):
        out_ref[j] = rows_ref[count * j : count * (j + 1)]


def split3(g):
    high = g.astype(BF16)
    rest = g - high.astype(F32)
    mid = rest.astype(BF16)
    low = (rest - mid.astype(F32)).astype(BF16)
    return jnp.concatenate([high, mid, low], axis=0)


def pick(g, selector):
    rows = g.shape[0]
    r = dot_nt(split3(g), selector)
    return r[:rows] + r[rows : 2 * rows] + r[2 * rows :]


def fused_kernel(
    n_space, n_samp, v_hbm, c_hbm, f1_hbm, f2_hbm, act_ref, o1_ref, o2_ref,
    v_ref, c_ref, f1_flat, f2_flat, f1_ref, f2_ref, load,
    vp, cp, all1, all2,
    turn, a1, a2, a3, dhid, hid, back, slope1, perm, acc1, acc2, act,
    s1, s2, q2, rows1, wide1, rows2, wide2, vf, vrows,
    grad1, grad2, part1, part2, full2, mine2,
    send_v, recv_v, send_1, recv_1, send_2, recv_2,
    send_a1, recv_a1, send_a2, recv_a2, send_b2, recv_b2,
):
    s = lax.axis_index("space")
    m = lax.axis_index("samp")
    size_x, size_y, size_z = v_ref.shape[1:]
    other = m + 1 - 2 * lax.rem(m, 2)
    chips = n_samp // 2
    turn_sign = 1 - 2 * ((2 * s) // n_space)

    def far(k):
        return lax.rem(2 * n_space + s - turn_sign * k, n_space)

    def across(j):
        return lax.rem(other + 2 * j, n_samp)

    def each_other_far(body):
        if n_space <= 16:
            for k in range(1, n_space):
                body(far(k))
            return

        def step(k, carry):
            body(far(k))
            return carry

        lax.fori_loop(1, n_space, step, 0)

    def there(dx, dy):
        return (s + dx >= 0) & (s + dx < n_space) & (m + dy >= 0) & (m + dy < n_samp)

    barrier = pltpu.get_barrier_semaphore()
    peers = n_samp - 1 + n_space - 1
    @each_other_far
    def _(peer):
        pl.semaphore_signal(barrier, inc=1, device_id=(peer, other), device_id_type=MESH)

    for k in range(1, n_samp):
        pl.semaphore_signal(barrier, inc=1, device_id=(s, lax.rem(m + k, n_samp)), device_id_type=MESH)

    for dx, dy in DIRS:
        if dx == 0:
            continue
        peers = peers + jnp.where(there(dx, dy), 1, 0)

        @pl.when(there(dx, dy))
        def _():
            pl.semaphore_signal(barrier, inc=1, device_id=(s + dx, m + dy), device_id_type=MESH)

    loads = [
        pltpu.make_async_copy(src, dst, load.at[j])
        for j, (src, dst) in enumerate(
            ((f2_hbm, f2_flat), (f1_hbm, f1_flat), (v_hbm, v_ref), (c_hbm, c_ref)))
    ]
    for copy in loads:
        copy.start()
    for dx, dy in DIRS:
        (_, nx), (tx, _) = spans(-dx, size_x, 2)
        (_, ny), (ty, _) = spans(-dy, size_y, 2)

        @pl.when(jnp.logical_not(there(dx, dy)))
        def _():
            vp[tx : tx + nx, ty : ty + ny] = jnp.zeros((nx, ny, CIN, size_z), BF16)

    loads[0].wait()
    split_rows(f2_flat, f2_ref)
    build_order(s2)
    ordered = f2_ref.shape[1] == 27 * C1
    if ordered:
        f2_ref[...] = dot(f2_ref[...], s2[...])[:, : 27 * C1].astype(BF16)
    loads[1].wait()
    split_rows(f1_flat, f1_ref)
    turn_v = one_hot_rows(CIN, size_y)
    loads[2].wait()

    def centre(x, carry):
        value = v_ref[:, x].astype(F32).reshape(CIN * size_y, size_z).astype(BF16)
        value = dot(turn_v, value)
        for y in range(size_y):
            vp[x + 2, y + 2] = value[CIN * y : CIN * (y + 1)].astype(BF16)
        return carry

    lax.fori_loop(0, size_x, centre, 0)
    pl.semaphore_wait(barrier, peers)

    def copy_1(k):
        return pltpu.make_async_remote_copy(
            src_ref=f1_ref, dst_ref=all1.at[m], send_sem=send_1.at[k], recv_sem=recv_1.at[k],
            device_id=(s, lax.rem(m + k, n_samp)), device_id_type=MESH)

    def copy_2(peer):
        return pltpu.make_async_remote_copy(
            src_ref=f2_ref, dst_ref=all2.at[s], send_sem=send_2, recv_sem=recv_2.at[s],
            device_id=(peer, other), device_id_type=MESH)

    def await_2(peer):
        pltpu.make_async_copy(all2.at[peer], all2.at[peer], send_2).wait()
        pltpu.make_async_copy(all2.at[peer], all2.at[peer], recv_2.at[peer]).wait()

    def halo(src, dst, width, send, recv, slot, dx, dy):
        (sx, nx), (tx, _) = spans(dx, size_x, width)
        (sy, ny), (ty, _) = spans(dy, size_y, width)
        return pltpu.make_async_remote_copy(
            src_ref=src.at[pl.ds(sx + width, nx), pl.ds(sy + width, ny)], dst_ref=dst.at[pl.ds(tx, nx), pl.ds(ty, ny)],
            send_sem=send.at[slot], recv_sem=recv.at[slot],
            device_id=(jnp.clip(s + dx, 0, n_space - 1), jnp.clip(m + dy, 0, n_samp - 1)),
            device_id_type=MESH)

    vol = [halo(vp, vp, 2, send_v, recv_v, j, dx, dy) for j, (dx, dy) in enumerate(DIRS)]
    @each_other_far
    def _(peer):
        copy_2(peer).start()

    for k in range(1, n_samp):
        copy_1(k).start()
    for copy, (dx, dy) in zip(vol, DIRS):
        @pl.when(there(dx, dy))
        def _():
            copy.start()

    all1[m] = f1_ref[...]
    all2[s] = f2_ref[...]
    last = size_z - 1
    high_y = size_y + 2

    def lanes(rows):
        return lax.broadcasted_iota(jnp.int32, (rows, size_z), 1)

    width1 = CIN * (size_y + 4)
    build_selectors(s1, q2, width1)
    turn[...] = one_hot_rows(C2, size_y)
    loads[3].wait()

    def turn_c(x, carry):
        value = c_ref[:, x].astype(F32).reshape(C2 * size_y, size_z).astype(BF16)
        cp[x] = dot(turn[...], value).astype(BF16)
        return carry

    lax.fori_loop(0, size_x, turn_c, 0)

    r = lax.broadcasted_iota(jnp.int32, (C2 * size_y, C2 * size_y), 0)
    q = lax.broadcasted_iota(jnp.int32, (C2 * size_y, C2 * size_y), 1)
    from_row = (r % size_y) * C2 + r // size_y
    perm[...] = jnp.where(q == from_row, 1.0, 0.0).astype(BF16)
    acc1[...] = jnp.zeros_like(acc1)
    acc2[...] = jnp.zeros_like(acc2)

    def arrive(group):
        for copy, (dx, dy) in zip(group, DIRS):
            @pl.when(there(-dx, -dy))
            def _():
                copy.wait_recv()

            @pl.when(there(dx, dy))
            def _():
                copy.wait_send()

    for k in range(1, n_samp):
        copy_1(k).wait()
    base1 = dot(gather_rows(all1, rows1, wide1), s1[...])
    for y in range(high_y):
        row = base1 if y == 0 else pltpu.roll(base1, CIN * y, axis=1)
        a1[C1 * y : C1 * (y + 1)] = row[:, : 9 * width1].astype(BF16)

    arrive(vol)
    lane_v = lanes(width1)
    lane_h = lanes(C1 * high_y)
    lane_b = lanes(C2 * 4)

    for x in range(size_x + 4):
        for y in range(vp.shape[1]):
            vf[x, CIN * y : CIN * (y + 1)] = vp[x, y].astype(F32)
    for x in range(size_x + 4):
        value = vf[x]
        before, after = shifted(value, lane_v, last)
        vrows[0, x] = before.astype(BF16)
        vrows[1, x] = value.astype(BF16)
        vrows[2, x] = after.astype(BF16)

    def vwin(x):
        return jnp.concatenate([vrows[kz, x + kx] for kz in range(3) for kx in range(3)], axis=0)

    first_row = jnp.where(m > 0, 1.0, 0.0)
    last_row = jnp.where(m < n_samp - 1, 1.0, 0.0)

    for x in range(size_x + 2):
        p = dot(a1[...], vwin(x))
        slope = jnp.where(p > 0, 1.0, SLOPE)
        if x == 0:
            slope = slope * jnp.where(s > 0, 1.0, 0.0)
        if x == size_x + 1:
            slope = slope * jnp.where(s < n_space - 1, 1.0, 0.0)
        slope = jnp.concatenate(
            [slope[:C1] * first_row, slope[C1 : C1 * (high_y - 1)], slope[C1 * (high_y - 1) :] * last_row], axis=0)
        slope1[x] = slope
        h = p * slope
        before, after = shifted(h, lane_h, last)
        hid[0, x] = before.astype(BF16)
        hid[1, x] = h.astype(BF16)
        hid[2, x] = after.astype(BF16)

    each_other_far(await_2)
    base2 = gather_rows(all2, rows2, wide2)
    base2 = base2.astype(F32) if ordered else dot(base2, s2[...])[:, : 27 * C1]
    base2 = jnp.concatenate([base2, jnp.zeros((C2, 896 - 27 * C1), F32)], axis=1)
    for y in range(4):
        row = base2 if y == 0 else pltpu.roll(base2, 9 * C1 * y, axis=1)
        a2[C2 * y : C2 * (y + 1)] = row[:, : 54 * C1].astype(BF16)

    for x in range(size_x):
        for half in range(size_y // 4):
            rows = slice(128 * half, 128 * half + 128)
            win = jnp.concatenate(
                [hid[kz, x + kx, 64 * half + C1 * y : 64 * half + C1 * (y + 1)]
                 for y in range(6) for kz in range(3) for kx in range(3)], axis=0)
            p = dot(a2[...], win)
            slope = jnp.where(p > 0, 1.0, SLOPE)
            act[x, rows] = (p * slope).astype(BF16)
            b = (cp[x, rows].astype(F32) * slope).astype(BF16)
            before, after = shifted(b.astype(F32), lane_b, last)
            back[0, x, rows] = after.astype(BF16)
            back[1, x, rows] = b
            back[2, x, rows] = before.astype(BF16)

    for x in range(size_x):
        moved, windows = [], []
        for y in range(0, size_y, 2):
            moved.append(jnp.concatenate([back[kz, x, C2 * y : C2 * y + 64] for kz in range(3)], axis=0))
            windows.append(jnp.concatenate([hid[1, x + kx, C1 * y : C1 * y + 64] for kx in range(3)], axis=0))
        acc2[...] += dot_nt(jnp.concatenate(moved, axis=1), jnp.concatenate(windows, axis=1))

    shares = []
    for kz in range(3):
        low = jnp.concatenate([acc2[64 * kz : 64 * kz + C2], jnp.zeros((C2, 64), F32)], axis=1)
        high = jnp.concatenate([acc2[64 * kz + C2 : 64 * kz + 64], jnp.zeros((C2, 64), F32)], axis=1)
        shares.append(low + pltpu.roll(high, 256 - C1, axis=1))
    scatter_rows(pick(jnp.concatenate(shares, axis=1), q2[...]), rows2, wide2, grad2)

    def spread_2(peer):
        pltpu.make_async_remote_copy(
            src_ref=grad2.at[peer], dst_ref=part2.at[s], send_sem=send_a2, recv_sem=recv_a2,
            device_id=(peer, other), device_id_type=MESH).start()

    each_other_far(spread_2)
    spread_2(s)

    tall = jnp.concatenate([base2[:, :512], jnp.zeros((128 - C2, 512), F32)], axis=0).T
    lane_t = lax.broadcasted_iota(jnp.int32, (C1, 128), 1)
    for kx in range(3):
        for kz in range(3):
            tile = 0.0
            for y in range(3):
                first = C1 * (9 * (2 - y) + 3 * kz + kx)
                piece = tall[first : first + C1]
                tile = tile + (piece if y == 0 else pltpu.roll(piece, C2 * y, axis=1))
            turns = [tile] + [pltpu.roll(tile, C2 * r, axis=1) for r in range(1, 4)]
            for y in range(6):
                turned = turns[(y + 2) % 4]
                if y < 2:
                    turned = jnp.where(lane_t < C2 * (y + 2), turned, 0.0)
                elif y > 3:
                    turned = jnp.where(lane_t >= C2 * (y - 2), turned, 0.0)
                first = C1 * (6 * kx + y)
                a3[first : first + C1, 128 * kz : 128 * kz + 128] = turned.astype(BF16)

    span = C1 * 6
    for x in range(size_x):
        halves = []
        for half in range(size_y // 4):
            win = jnp.concatenate([back[kz, x, 128 * half : 128 * half + 128] for kz in range(3)], axis=0)
            halves.append(dot(a3[...], win))
        for kx in range(3):
            low, high = (d[span * kx : span * (kx + 1)] for d in halves)
            share = jnp.concatenate([low[:64], low[64:] + high[:32], high[32:]], axis=0)
            if x == 0 or kx == 2:
                dhid[x + kx] = share
            else:
                dhid[x + kx] += share
    for x in range(size_x + 2):
        b1 = (dhid[x] * slope1[x]).astype(BF16)
        acc1[:, : 9 * width1] += dot_nt(b1, vwin(x))

    total1 = acc1[:C1]
    for y in range(1, high_y):
        total1 = total1 + pltpu.roll(acc1[C1 * y : C1 * (y + 1)], acc1.shape[1] - CIN * y, axis=1)
    scatter_rows(pick(total1, s1[...]), rows1, wide1, grad1)

    everyone = n_space * n_samp
    me = s * n_samp + m

    def to_one(ps, pm):
        pltpu.make_async_remote_copy(
            src_ref=grad1.at[pm], dst_ref=part1.at[me], send_sem=send_a1, recv_sem=recv_a1,
            device_id=(ps, pm), device_id_type=MESH).start()

    @each_other_far
    def _(peer):
        for j in range(n_samp):
            to_one(peer, lax.rem(m + n_samp - 1 - j, n_samp))

    for k in range(1, n_samp):
        to_one(s, lax.rem(m + k, n_samp))

    def send_act(x, carry):
        value = dot(perm[...], act[x])
        act_ref[:, x] = value.reshape(C2, size_y, size_z).astype(BF16)
        return carry

    lax.fori_loop(0, size_x, send_act, 0)
    part1[me] = grad1[m]
    pltpu.make_async_copy(part2, part2, send_a2).wait()
    pltpu.make_async_copy(part2, part2, recv_a2).wait()
    mine2[...] = jnp.sum(part2[...], axis=0)
    for k in range(n_samp - 1, 0, -1):
        pltpu.make_async_remote_copy(
            src_ref=mine2, dst_ref=full2.at[m], send_sem=send_b2, recv_sem=recv_b2,
            device_id=(s, lax.rem(m + k, n_samp)), device_id_type=MESH).start()
    full2[m] = mine2[...]
    rest = full2.at[pl.ds(0, n_samp - 1)]
    pltpu.make_async_copy(rest, rest, send_b2).wait()
    pltpu.make_async_copy(rest, rest, recv_b2).wait()
    o2_ref[...] = jnp.sum(full2[...], axis=0)
    others = part1.at[pl.ds(0, everyone - 1)]
    pltpu.make_async_copy(others, others, send_a1).wait()
    pltpu.make_async_copy(others, others, recv_a1).wait()
    o1_ref[...] = jnp.sum(part1[...], axis=0)


def store_kernel(scale, act, o1, o2, act_out, o1_out, o2_out, flat1, flat2, done):
    pieces = done.shape[0] - 2
    step = C2 // pieces
    copies = [
        pltpu.make_async_copy(act.at[pl.ds(step * j, step)], act_out.at[pl.ds(step * j, step)], done.at[j + 2])
        for j in range(pieces)
    ]
    copies.append(pltpu.make_async_copy(flat1, o1_out, done.at[0]))
    copies.append(pltpu.make_async_copy(flat2, o2_out, done.at[1]))
    for copy in copies[:pieces]:
        copy.start()
    flat2[...] = flatten(o2[...] * scale)
    copies[-1].start()
    flat1[...] = flatten(o1[...] * scale)
    copies[-2].start()
    for copy in copies:
        copy.wait()


VMEM = pl.BlockSpec(memory_space=pltpu.VMEM)
HBM = pl.BlockSpec(memory_space=pltpu.HBM)


def on_device(n_space, n_samp, volume, filters_one, filters_two, cotangent):
    _, size_x, size_y, size_z = volume.shape
    len1 = filters_one.shape[0]
    len2 = filters_two.shape[0]
    unit1 = math.gcd(len1, 27 * CIN)
    unit2 = math.gcd(len2, 27 * C1)
    piece1 = (len1 // unit1, unit1)
    piece2 = (len2 // unit2, unit2)
    high_y = size_y + 2
    width1 = CIN * (size_y + 4)
    scale = 1.0 / math.sqrt(float(size_x * n_space * size_y * n_samp * size_z))
    samp, space = pltpu.SemaphoreType.DMA((n_samp,)), pltpu.SemaphoreType.DMA((n_space,))
    sides, one = pltpu.SemaphoreType.DMA((8,)), pltpu.SemaphoreType.DMA
    activation, out1, out2 = pl.pallas_call(
        functools.partial(fused_kernel, n_space, n_samp),
        out_shape=[
            jax.ShapeDtypeStruct((C2, size_x, size_y, size_z), BF16),
            jax.ShapeDtypeStruct(piece1, F32),
            jax.ShapeDtypeStruct(piece2, F32),
        ],
        in_specs=[HBM] * 4,
        out_specs=[VMEM] * 3,
        scratch_shapes=[
            pltpu.VMEM(volume.shape, BF16),
            pltpu.VMEM(cotangent.shape, BF16),
            pltpu.VMEM((len1,), BF16),
            pltpu.VMEM((len2,), BF16),
            pltpu.VMEM(piece1, BF16),
            pltpu.VMEM(piece2, BF16),
            pltpu.SemaphoreType.DMA((4,)),
            pltpu.VMEM((size_x + 4, size_y + 4, CIN, size_z), BF16),
            pltpu.VMEM((size_x, C2 * size_y, size_z), BF16),
            pltpu.VMEM((n_samp, *piece1), BF16),
            pltpu.VMEM((n_space, *piece2), BF16),
            pltpu.VMEM((C2 * size_y, C2 * size_y), BF16),
            pltpu.VMEM((C1 * high_y, 9 * width1), BF16),
            pltpu.VMEM((C2 * 4, 9 * C1 * 6), BF16),
            pltpu.VMEM((18 * C1, 12 * C2), BF16),
            pltpu.VMEM((size_x + 2, C1 * high_y, size_z), F32),
            pltpu.VMEM((3, size_x + 2, C1 * high_y, size_z), BF16),
            pltpu.VMEM((3, size_x, C2 * size_y, size_z), BF16),
            pltpu.VMEM((size_x + 2, C1 * high_y, size_z), F32),
            pltpu.VMEM((C2 * size_y, C2 * size_y), BF16),
            pltpu.VMEM((C1 * high_y, 512), F32),
            pltpu.VMEM((192, 192), F32),
            pltpu.VMEM((size_x, C2 * size_y, size_z), BF16),
            pltpu.VMEM((27 * CIN, 512), BF16),
            pltpu.VMEM((27 * C1, 512), BF16),
            pltpu.VMEM((27 * C1, 768), BF16),
            pltpu.VMEM((n_samp * piece1[0], piece1[1]), F32),
            pltpu.VMEM((C1, 27 * CIN), F32),
            pltpu.VMEM((n_space * piece2[0], piece2[1]), F32),
            pltpu.VMEM((C2, 27 * C1), F32),
            pltpu.VMEM((size_x + 4, width1, size_z), F32),
            pltpu.VMEM((3, size_x + 4, width1, size_z), BF16),
            pltpu.VMEM((n_samp, *piece1), F32),
            pltpu.VMEM((n_space, *piece2), F32),
            pltpu.VMEM((n_space * n_samp, *piece1), F32),
            pltpu.VMEM((n_space, *piece2), F32),
            pltpu.VMEM((n_samp, *piece2), F32),
            pltpu.VMEM(piece2, F32),
            sides, sides, samp, samp, one, space,
            one, one, one, one, one, one,
        ],
        compiler_params=pltpu.CompilerParams(
            collective_id=0, has_side_effects=True, vmem_limit_bytes=48 * 2**20),
    )(*(pltpu.with_memory_space_constraint(x, pltpu.HBM)
        for x in (volume, cotangent, filters_one, filters_two)))
    return pl.pallas_call(
        functools.partial(store_kernel, scale),
        out_shape=[
            jax.ShapeDtypeStruct(activation.shape, BF16),
            jax.ShapeDtypeStruct((len1,), F32),
            jax.ShapeDtypeStruct((len2,), F32),
        ],
        in_specs=[VMEM] * 3,
        out_specs=[HBM] * 3,
        scratch_shapes=[pltpu.VMEM((len1,), F32), pltpu.VMEM((len2,), F32), pltpu.SemaphoreType.DMA((3,))],
        compiler_params=pltpu.CompilerParams(vmem_limit_bytes=2**20),
    )(activation, out1, out2)


def solution(mesh):
    in_specs = (
        P(None, "space", "samp", None),
        P("samp"),
        P("space"),
        P(None, "space", "samp", None),
    )
    out_specs = (P(None, "space", "samp", None), P("samp"), P("space"))
    return jax.shard_map(
        functools.partial(on_device, mesh.shape["space"], mesh.shape["samp"]),
        mesh=mesh, in_specs=in_specs, out_specs=out_specs, check_vma=False,
    )
```

```python
import functools
import math

import jax
import jax.numpy as jnp
from jax import lax
from jax.experimental import pallas as pl
from jax.experimental.pallas import tpu as pltpu
from jax.sharding import PartitionSpec as P

CIN = 4
C1 = 16
C2 = 32
SLOPE = 0.3
MESH = pl.DeviceIdType.MESH
F32 = jnp.float32
BF16 = jnp.bfloat16
DIRS = [(dx, dy) for dx in (-1, 0, 1) for dy in (-1, 0, 1) if (dx, dy) != (0, 0)]


def spans(delta, size, width):
    if delta == 1:
        return (size - width, width), (0, width)
    if delta == -1:
        return (0, width), (size + width, width)
    return (0, size), (width, size)


def leaky(values):
    return jnp.where(values > 0, values, SLOPE * values)


def shifted(values, lane, last):
    before = jnp.where(lane == 0, 0.0, pltpu.roll(values, 1, axis=1))
    after = jnp.where(lane == last, 0.0, pltpu.roll(values, last, axis=1))
    return before, after


def dot(a, b):
    return lax.dot_general(a, b, (((1,), (0,)), ((), ())), preferred_element_type=F32)


def dot_nt(a, b):
    return lax.dot_general(a, b, (((1,), (1,)), ((), ())), preferred_element_type=F32)


def one_hot(rows, source):
    row = lax.broadcasted_iota(jnp.int32, (rows, source.shape[1]), 0)
    return jnp.where(row == source, 1.0, 0.0).astype(BF16)


def one_hot_rows(chans, size_y):
    r = lax.broadcasted_iota(jnp.int32, (chans * size_y, chans * size_y), 0)
    q = lax.broadcasted_iota(jnp.int32, (chans * size_y, chans * size_y), 1)
    return jnp.where(q == (r % chans) * size_y + r // chans, 1.0, 0.0).astype(BF16)


def build_selectors(s1, q2, width1):
    lane = lax.broadcasted_iota(jnp.int32, (1, s1.shape[1]), 1)
    group, rest = lax.div(lane, width1), lax.rem(lane, width1)
    kz, kx, ky, i = lax.div(group, 3), lax.rem(group, 3), lax.div(rest, CIN), lax.rem(rest, CIN)
    s1[...] = one_hot(27 * CIN, jnp.where((group < 9) & (ky < 3), i * 27 + kx * 9 + ky * 3 + kz, -9))
    lane = lax.broadcasted_iota(jnp.int32, (1, 256), 1)
    kx, ky, i = lane >> 6, (lane >> 4) & 3, lane & 15
    source = jnp.where((kx < 3) & (ky < 3), i * 27 + kx * 9 + ky * 3, -9)
    for kz in range(3):
        q2[:, 256 * kz : 256 * kz + 256] = one_hot(27 * C1, source + kz)


def build_order(s2):
    lane = lax.broadcasted_iota(jnp.int32, (1, s2.shape[1]), 1)
    tap, i = lane >> 4, lane & 15
    ky, kz, kx = lax.div(tap, 9), lax.rem(lax.div(tap, 3), 3), lax.rem(tap, 3)
    s2[...] = one_hot(27 * C1, jnp.where(tap < 27, i * 27 + kx * 9 + ky * 3 + kz, -9))


def split_rows(flat_ref, rows_ref):
    rows, unit = rows_ref.shape
    flat = flat_ref[...].astype(F32).reshape(1, rows * unit)
    rows_ref[...] = jnp.concatenate(
        [flat[:, unit * k : unit * (k + 1)] for k in range(rows)], axis=0).astype(BF16)


def flatten(rows):
    return jnp.concatenate([rows[k : k + 1] for k in range(rows.shape[0])], axis=1).reshape(rows.size)


def gather_rows(all_ref, rows_ref, wide_ref):
    owners, count, unit = all_ref.shape
    for j in range(owners):
        rows_ref[count * j : count * (j + 1)] = all_ref[j].astype(F32)
    split = wide_ref.shape[1] // unit
    if split == 1:
        return rows_ref[...].astype(BF16)
    for k in range(split):
        wide_ref[:, unit * k : unit * (k + 1)] = rows_ref[pl.ds(k, wide_ref.shape[0], stride=split)]
    return wide_ref[...].astype(BF16)


def scatter_rows(value, rows_ref, wide_ref, out_ref):
    owners, count, unit = out_ref.shape
    split = value.shape[1] // unit
    if split == 1:
        rows_ref[...] = value
    else:
        wide_ref[...] = value
        for k in range(split):
            rows_ref[pl.ds(k, value.shape[0], stride=split)] = wide_ref[:, unit * k : unit * (k + 1)]
    for j in range(owners):
        out_ref[j] = rows_ref[count * j : count * (j + 1)]


def split3(g):
    high = g.astype(BF16)
    rest = g - high.astype(F32)
    mid = rest.astype(BF16)
    low = (rest - mid.astype(F32)).astype(BF16)
    return jnp.concatenate([high, mid, low], axis=0)


def pick(g, selector):
    rows = g.shape[0]
    r = dot_nt(split3(g), selector)
    return r[:rows] + r[rows : 2 * rows] + r[2 * rows :]


def fused_kernel(
    n_space, n_samp, v_hbm, c_hbm, f1_hbm, f2_hbm, act_ref, o1_ref, o2_ref,
    v_ref, c_ref, f1_flat, f2_flat, f1_ref, f2_ref, load,
    vp, cp, all1, all2,
    turn, a1, a2, a3, dhid, hid, back, slope1, perm, acc1, acc2, act,
    s1, s2, q2, rows1, wide1, rows2, wide2, vf, vrows,
    grad1, grad2, part1, part2, full2, mine2,
    send_v, recv_v, send_1, recv_1, send_2, recv_2,
    send_a1, recv_a1, send_a2, recv_a2, send_b2, recv_b2,
):
    s = lax.axis_index("space")
    m = lax.axis_index("samp")
    size_x, size_y, size_z = v_ref.shape[1:]
    other = m + 1 - 2 * lax.rem(m, 2)
    chips = n_samp // 2
    turn_sign = 1 - 2 * ((2 * s) // n_space)

    def far(k):
        return lax.rem(2 * n_space + s - turn_sign * k, n_space)

    def across(j):
        return lax.rem(other + 2 * j, n_samp)

    def each_other_far(body):
        if n_space <= 16:
            for k in range(1, n_space):
                body(far(k))
            return

        def step(k, carry):
            body(far(k))
            return carry

        lax.fori_loop(1, n_space, step, 0)

    def there(dx, dy):
        return (s + dx >= 0) & (s + dx < n_space) & (m + dy >= 0) & (m + dy < n_samp)

    barrier = pltpu.get_barrier_semaphore()
    peers = n_samp - 1 + n_space - 1
    @each_other_far
    def _(peer):
        pl.semaphore_signal(barrier, inc=1, device_id=(peer, other), device_id_type=MESH)

    for k in range(1, n_samp):
        pl.semaphore_signal(barrier, inc=1, device_id=(s, lax.rem(m + k, n_samp)), device_id_type=MESH)

    for dx, dy in DIRS:
        if dx == 0:
            continue
        peers = peers + jnp.where(there(dx, dy), 1, 0)

        @pl.when(there(dx, dy))
        def _():
            pl.semaphore_signal(barrier, inc=1, device_id=(s + dx, m + dy), device_id_type=MESH)

    loads = [
        pltpu.make_async_copy(src, dst, load.at[j])
        for j, (src, dst) in enumerate(
            ((f2_hbm, f2_flat), (f1_hbm, f1_flat), (v_hbm, v_ref), (c_hbm, c_ref)))
    ]
    for copy in loads:
        copy.start()
    for dx, dy in DIRS:
        (_, nx), (tx, _) = spans(-dx, size_x, 2)
        (_, ny), (ty, _) = spans(-dy, size_y, 2)

        @pl.when(jnp.logical_not(there(dx, dy)))
        def _():
            vp[tx : tx + nx, ty : ty + ny] = jnp.zeros((nx, ny, CIN, size_z), BF16)

    loads[0].wait()
    split_rows(f2_flat, f2_ref)
    build_order(s2)
    ordered = f2_ref.shape[1] == 27 * C1
    if ordered:
        f2_ref[...] = dot(f2_ref[...], s2[...])[:, : 27 * C1].astype(BF16)
    loads[1].wait()
    split_rows(f1_flat, f1_ref)
    turn_v = one_hot_rows(CIN, size_y)
    loads[2].wait()

    def centre(x, carry):
        value = v_ref[:, x].astype(F32).reshape(CIN * size_y, size_z).astype(BF16)
        value = dot(turn_v, value)
        vf[x + 2, 2 * CIN : (2 + size_y) * CIN] = value
        for y in range(size_y):
            vp[x + 2, y + 2] = value[CIN * y : CIN * (y + 1)].astype(BF16)
        return carry

    lax.fori_loop(0, size_x, centre, 0)
    pl.semaphore_wait(barrier, peers)

    def copy_1(k):
        return pltpu.make_async_remote_copy(
            src_ref=f1_ref, dst_ref=all1.at[m], send_sem=send_1.at[k], recv_sem=recv_1.at[k],
            device_id=(s, lax.rem(m + k, n_samp)), device_id_type=MESH)

    def copy_2(peer):
        return pltpu.make_async_remote_copy(
            src_ref=f2_ref, dst_ref=all2.at[s], send_sem=send_2, recv_sem=recv_2.at[s],
            device_id=(peer, other), device_id_type=MESH)

    def await_2(peer):
        pltpu.make_async_copy(all2.at[peer], all2.at[peer], recv_2.at[peer]).wait()

    def halo(src, dst, width, send, recv, slot, dx, dy):
        (sx, nx), (tx, _) = spans(dx, size_x, width)
        (sy, ny), (ty, _) = spans(dy, size_y, width)
        return pltpu.make_async_remote_copy(
            src_ref=src.at[pl.ds(sx + width, nx), pl.ds(sy + width, ny)], dst_ref=dst.at[pl.ds(tx, nx), pl.ds(ty, ny)],
            send_sem=send.at[slot], recv_sem=recv.at[slot],
            device_id=(jnp.clip(s + dx, 0, n_space - 1), jnp.clip(m + dy, 0, n_samp - 1)),
            device_id_type=MESH)

    vol = [halo(vp, vp, 2, send_v, recv_v, j, dx, dy) for j, (dx, dy) in enumerate(DIRS)]
    @each_other_far
    def _(peer):
        copy_2(peer).start()

    for k in range(1, n_samp):
        copy_1(k).start()
    for copy, (dx, dy) in zip(vol, DIRS):
        @pl.when(there(dx, dy))
        def _():
            copy.start()

    all1[m] = f1_ref[...]
    all2[s] = f2_ref[...]
    last = size_z - 1
    high_y = size_y + 2

    def lanes(rows):
        return lax.broadcasted_iota(jnp.int32, (rows, size_z), 1)

    width1 = CIN * (size_y + 4)
    build_selectors(s1, q2, width1)
    turn[...] = one_hot_rows(C2, size_y)
    loads[3].wait()

    def turn_c(x, carry):
        value = c_ref[:, x].astype(F32).reshape(C2 * size_y, size_z).astype(BF16)
        cp[x] = dot(turn[...], value).astype(BF16)
        return carry

    lax.fori_loop(0, size_x, turn_c, 0)

    r = lax.broadcasted_iota(jnp.int32, (C2 * size_y, C2 * size_y), 0)
    q = lax.broadcasted_iota(jnp.int32, (C2 * size_y, C2 * size_y), 1)
    from_row = (r % size_y) * C2 + r // size_y
    perm[...] = jnp.where(q == from_row, 1.0, 0.0).astype(BF16)
    acc1[...] = jnp.zeros_like(acc1)
    acc2[...] = jnp.zeros_like(acc2)

    def arrive(width):
        for copy, (dx, dy) in zip(vol, DIRS):
            if abs(dx) != width:
                continue

            @pl.when(there(-dx, -dy))
            def _():
                copy.wait_recv()

    for k in range(1, n_samp):
        copy_1(k).wait_recv()
    base1 = dot(gather_rows(all1, rows1, wide1), s1[...])
    for y in range(high_y):
        row = base1 if y == 0 else pltpu.roll(base1, CIN * y, axis=1)
        a1[C1 * y : C1 * (y + 1)] = row[:, : 9 * width1].astype(BF16)

    lane_v = lanes(width1)
    lane_h = lanes(C1 * high_y)
    lane_b = lanes(C2 * 4)
    first_row = jnp.where(m > 0, 1.0, 0.0)
    last_row = jnp.where(m < n_samp - 1, 1.0, 0.0)

    def lift(x, rows):
        for y in rows:
            vf[x, CIN * y : CIN * (y + 1)] = vp[x, y].astype(F32)
        value = vf[x]
        before, after = shifted(value, lane_v, last)
        vrows[0, x] = before.astype(BF16)
        vrows[1, x] = value.astype(BF16)
        vrows[2, x] = after.astype(BF16)

    def vwin(x):
        return jnp.concatenate([vrows[kz, x + kx] for kz in range(3) for kx in range(3)], axis=0)

    def layer1(x):
        p = dot(a1[...], vwin(x))
        slope = jnp.where(p > 0, 1.0, SLOPE)
        if x == 0:
            slope = slope * jnp.where(s > 0, 1.0, 0.0)
        if x == size_x + 1:
            slope = slope * jnp.where(s < n_space - 1, 1.0, 0.0)
        slope = jnp.concatenate(
            [slope[:C1] * first_row, slope[C1 : C1 * (high_y - 1)], slope[C1 * (high_y - 1) :] * last_row], axis=0)
        slope1[x] = slope
        h = p * slope
        before, after = shifted(h, lane_h, last)
        hid[0, x] = before.astype(BF16)
        hid[1, x] = h.astype(BF16)
        hid[2, x] = after.astype(BF16)

    edge_rows = (0, 1, size_y + 2, size_y + 3)
    arrive(0)
    for x in range(2, size_x + 2):
        lift(x, edge_rows)
    for x in range(2, size_x):
        layer1(x)
    arrive(1)
    for x in (0, 1, size_x + 2, size_x + 3):
        lift(x, range(size_y + 4))
    for x in (0, 1, size_x, size_x + 1):
        layer1(x)

    each_other_far(await_2)
    base2 = gather_rows(all2, rows2, wide2)
    base2 = base2.astype(F32) if ordered else dot(base2, s2[...])[:, : 27 * C1]
    base2 = jnp.concatenate([base2, jnp.zeros((C2, 896 - 27 * C1), F32)], axis=1)
    for y in range(4):
        row = base2 if y == 0 else pltpu.roll(base2, 9 * C1 * y, axis=1)
        a2[C2 * y : C2 * (y + 1)] = row[:, : 54 * C1].astype(BF16)

    for x in range(size_x):
        for half in range(size_y // 4):
            rows = slice(128 * half, 128 * half + 128)
            win = jnp.concatenate(
                [hid[kz, x + kx, 64 * half + C1 * y : 64 * half + C1 * (y + 1)]
                 for y in range(6) for kz in range(3) for kx in range(3)], axis=0)
            p = dot(a2[...], win)
            slope = jnp.where(p > 0, 1.0, SLOPE)
            act[x, rows] = (p * slope).astype(BF16)
            b = (cp[x, rows].astype(F32) * slope).astype(BF16)
            before, after = shifted(b.astype(F32), lane_b, last)
            back[0, x, rows] = after.astype(BF16)
            back[1, x, rows] = b
            back[2, x, rows] = before.astype(BF16)

    for x in range(size_x):
        moved, windows = [], []
        for y in range(0, size_y, 2):
            moved.append(jnp.concatenate([back[kz, x, C2 * y : C2 * y + 64] for kz in range(3)], axis=0))
            windows.append(jnp.concatenate([hid[1, x + kx, C1 * y : C1 * y + 64] for kx in range(3)], axis=0))
        acc2[...] += dot_nt(jnp.concatenate(moved, axis=1), jnp.concatenate(windows, axis=1))

    shares = []
    for kz in range(3):
        low = jnp.concatenate([acc2[64 * kz : 64 * kz + C2], jnp.zeros((C2, 64), F32)], axis=1)
        high = jnp.concatenate([acc2[64 * kz + C2 : 64 * kz + 64], jnp.zeros((C2, 64), F32)], axis=1)
        shares.append(low + pltpu.roll(high, 256 - C1, axis=1))
    scatter_rows(pick(jnp.concatenate(shares, axis=1), q2[...]), rows2, wide2, grad2)

    def spread_2(peer):
        pltpu.make_async_remote_copy(
            src_ref=grad2.at[peer], dst_ref=part2.at[s], send_sem=send_a2, recv_sem=recv_a2,
            device_id=(peer, other), device_id_type=MESH).start()

    each_other_far(spread_2)
    spread_2(s)

    tall = jnp.concatenate([base2[:, :512], jnp.zeros((128 - C2, 512), F32)], axis=0).T
    lane_t = lax.broadcasted_iota(jnp.int32, (C1, 128), 1)
    for kx in range(3):
        for kz in range(3):
            tile = 0.0
            for y in range(3):
                first = C1 * (9 * (2 - y) + 3 * kz + kx)
                piece = tall[first : first + C1]
                tile = tile + (piece if y == 0 else pltpu.roll(piece, C2 * y, axis=1))
            turns = [tile] + [pltpu.roll(tile, C2 * r, axis=1) for r in range(1, 4)]
            for y in range(6):
                turned = turns[(y + 2) % 4]
                if y < 2:
                    turned = jnp.where(lane_t < C2 * (y + 2), turned, 0.0)
                elif y > 3:
                    turned = jnp.where(lane_t >= C2 * (y - 2), turned, 0.0)
                first = C1 * (6 * kx + y)
                a3[first : first + C1, 128 * kz : 128 * kz + 128] = turned.astype(BF16)

    span = C1 * 6
    for x in range(size_x):
        halves = []
        for half in range(size_y // 4):
            win = jnp.concatenate([back[kz, x, 128 * half : 128 * half + 128] for kz in range(3)], axis=0)
            halves.append(dot(a3[...], win))
        for kx in range(3):
            low, high = (d[span * kx : span * (kx + 1)] for d in halves)
            share = jnp.concatenate([low[:64], low[64:] + high[:32], high[32:]], axis=0)
            if x == 0 or kx == 2:
                dhid[x + kx] = share
            else:
                dhid[x + kx] += share
    for x in range(0, size_x + 2, 2):
        pair = [(dhid[x + k] * slope1[x + k]).astype(BF16) for k in range(2)]
        acc1[:, : 9 * width1] += dot_nt(
            jnp.concatenate(pair, axis=1), jnp.concatenate([vwin(x), vwin(x + 1)], axis=1))

    total1 = acc1[:C1]
    for y in range(1, high_y):
        total1 = total1 + pltpu.roll(acc1[C1 * y : C1 * (y + 1)], acc1.shape[1] - CIN * y, axis=1)
    scatter_rows(pick(total1, s1[...]), rows1, wide1, grad1)

    everyone = n_space * n_samp
    me = s * n_samp + m

    def to_one(ps, pm):
        pltpu.make_async_remote_copy(
            src_ref=grad1.at[pm], dst_ref=part1.at[me], send_sem=send_a1, recv_sem=recv_a1,
            device_id=(ps, pm), device_id_type=MESH).start()

    @each_other_far
    def _(peer):
        for j in range(n_samp):
            to_one(peer, lax.rem(m + n_samp - 1 - j, n_samp))

    for k in range(1, n_samp):
        to_one(s, lax.rem(m + k, n_samp))

    def send_act(x, carry):
        value = dot(perm[...], act[x])
        act_ref[:, x] = value.reshape(C2, size_y, size_z).astype(BF16)
        return carry

    lax.fori_loop(0, size_x, send_act, 0)
    part1[me] = grad1[m]
    pltpu.make_async_copy(part2, part2, recv_a2).wait()
    mine2[...] = jnp.sum(part2[...], axis=0)
    for k in range(n_samp - 1, 0, -1):
        pltpu.make_async_remote_copy(
            src_ref=mine2, dst_ref=full2.at[m], send_sem=send_b2, recv_sem=recv_b2,
            device_id=(s, lax.rem(m + k, n_samp)), device_id_type=MESH).start()
    full2[m] = mine2[...]
    rest = full2.at[pl.ds(0, n_samp - 1)]
    for k in range(1, n_samp):
        copy_1(k).wait_send()
    for copy, (dx, dy) in zip(vol, DIRS):
        @pl.when(there(dx, dy))
        def _():
            copy.wait_send()
    sent = all2.at[pl.ds(0, n_space - 1)]
    pltpu.make_async_copy(sent, sent, send_2).wait()
    pltpu.make_async_copy(part2, part2, send_a2).wait()
    pltpu.make_async_copy(rest, rest, send_b2).wait()
    pltpu.make_async_copy(rest, rest, recv_b2).wait()
    o2_ref[...] = jnp.sum(full2[...], axis=0)
    others = part1.at[pl.ds(0, everyone - 1)]
    pltpu.make_async_copy(others, others, send_a1).wait()
    pltpu.make_async_copy(others, others, recv_a1).wait()
    o1_ref[...] = jnp.sum(part1[...], axis=0)


def store_kernel(scale, act, o1, o2, act_out, o1_out, o2_out, flat1, flat2, done):
    pieces = done.shape[0] - 2
    step = C2 // pieces
    copies = [
        pltpu.make_async_copy(act.at[pl.ds(step * j, step)], act_out.at[pl.ds(step * j, step)], done.at[j + 2])
        for j in range(pieces)
    ]
    copies.append(pltpu.make_async_copy(flat1, o1_out, done.at[0]))
    copies.append(pltpu.make_async_copy(flat2, o2_out, done.at[1]))
    for copy in copies[:pieces]:
        copy.start()
    flat2[...] = flatten(o2[...] * scale)
    copies[-1].start()
    flat1[...] = flatten(o1[...] * scale)
    copies[-2].start()
    for copy in copies:
        copy.wait()


VMEM = pl.BlockSpec(memory_space=pltpu.VMEM)
HBM = pl.BlockSpec(memory_space=pltpu.HBM)


def on_device(n_space, n_samp, volume, filters_one, filters_two, cotangent):
    _, size_x, size_y, size_z = volume.shape
    len1 = filters_one.shape[0]
    len2 = filters_two.shape[0]
    unit1 = math.gcd(len1, 27 * CIN)
    unit2 = math.gcd(len2, 27 * C1)
    piece1 = (len1 // unit1, unit1)
    piece2 = (len2 // unit2, unit2)
    high_y = size_y + 2
    width1 = CIN * (size_y + 4)
    scale = 1.0 / math.sqrt(float(size_x * n_space * size_y * n_samp * size_z))
    samp, space = pltpu.SemaphoreType.DMA((n_samp,)), pltpu.SemaphoreType.DMA((n_space,))
    sides, one = pltpu.SemaphoreType.DMA((8,)), pltpu.SemaphoreType.DMA
    activation, out1, out2 = pl.pallas_call(
        functools.partial(fused_kernel, n_space, n_samp),
        out_shape=[
            jax.ShapeDtypeStruct((C2, size_x, size_y, size_z), BF16),
            jax.ShapeDtypeStruct(piece1, F32),
            jax.ShapeDtypeStruct(piece2, F32),
        ],
        in_specs=[HBM] * 4,
        out_specs=[VMEM] * 3,
        scratch_shapes=[
            pltpu.VMEM(volume.shape, BF16),
            pltpu.VMEM(cotangent.shape, BF16),
            pltpu.VMEM((len1,), BF16),
            pltpu.VMEM((len2,), BF16),
            pltpu.VMEM(piece1, BF16),
            pltpu.VMEM(piece2, BF16),
            pltpu.SemaphoreType.DMA((4,)),
            pltpu.VMEM((size_x + 4, size_y + 4, CIN, size_z), BF16),
            pltpu.VMEM((size_x, C2 * size_y, size_z), BF16),
            pltpu.VMEM((n_samp, *piece1), BF16),
            pltpu.VMEM((n_space, *piece2), BF16),
            pltpu.VMEM((C2 * size_y, C2 * size_y), BF16),
            pltpu.VMEM((C1 * high_y, 9 * width1), BF16),
            pltpu.VMEM((C2 * 4, 9 * C1 * 6), BF16),
            pltpu.VMEM((18 * C1, 12 * C2), BF16),
            pltpu.VMEM((size_x + 2, C1 * high_y, size_z), F32),
            pltpu.VMEM((3, size_x + 2, C1 * high_y, size_z), BF16),
            pltpu.VMEM((3, size_x, C2 * size_y, size_z), BF16),
            pltpu.VMEM((size_x + 2, C1 * high_y, size_z), F32),
            pltpu.VMEM((C2 * size_y, C2 * size_y), BF16),
            pltpu.VMEM((C1 * high_y, 512), F32),
            pltpu.VMEM((192, 192), F32),
            pltpu.VMEM((size_x, C2 * size_y, size_z), BF16),
            pltpu.VMEM((27 * CIN, 512), BF16),
            pltpu.VMEM((27 * C1, 512), BF16),
            pltpu.VMEM((27 * C1, 768), BF16),
            pltpu.VMEM((n_samp * piece1[0], piece1[1]), F32),
            pltpu.VMEM((C1, 27 * CIN), F32),
            pltpu.VMEM((n_space * piece2[0], piece2[1]), F32),
            pltpu.VMEM((C2, 27 * C1), F32),
            pltpu.VMEM((size_x + 4, width1, size_z), F32),
            pltpu.VMEM((3, size_x + 4, width1, size_z), BF16),
            pltpu.VMEM((n_samp, *piece1), F32),
            pltpu.VMEM((n_space, *piece2), F32),
            pltpu.VMEM((n_space * n_samp, *piece1), F32),
            pltpu.VMEM((n_space, *piece2), F32),
            pltpu.VMEM((n_samp, *piece2), F32),
            pltpu.VMEM(piece2, F32),
            sides, sides, samp, samp, one, space,
            one, one, one, one, one, one,
        ],
        compiler_params=pltpu.CompilerParams(
            collective_id=0, has_side_effects=True, vmem_limit_bytes=48 * 2**20),
    )(*(pltpu.with_memory_space_constraint(x, pltpu.HBM)
        for x in (volume, cotangent, filters_one, filters_two)))
    return pl.pallas_call(
        functools.partial(store_kernel, scale),
        out_shape=[
            jax.ShapeDtypeStruct(activation.shape, BF16),
            jax.ShapeDtypeStruct((len1,), F32),
            jax.ShapeDtypeStruct((len2,), F32),
        ],
        in_specs=[VMEM] * 3,
        out_specs=[HBM] * 3,
        scratch_shapes=[pltpu.VMEM((len1,), F32), pltpu.VMEM((len2,), F32), pltpu.SemaphoreType.DMA((3,))],
        compiler_params=pltpu.CompilerParams(vmem_limit_bytes=2**20),
    )(activation, out1, out2)


def solution(mesh):
    in_specs = (
        P(None, "space", "samp", None),
        P("samp"),
        P("space"),
        P(None, "space", "samp", None),
    )
    out_specs = (P(None, "space", "samp", None), P("samp"), P("space"))
    return jax.shard_map(
        functools.partial(on_device, mesh.shape["space"], mesh.shape["samp"]),
        mesh=mesh, in_specs=in_specs, out_specs=out_specs, check_vma=False,
    )
```

```python
import functools
import math

import jax
import jax.numpy as jnp
from jax import lax
from jax.experimental import pallas as pl
from jax.experimental.pallas import tpu as pltpu
from jax.sharding import PartitionSpec as P

CIN = 4
C1 = 16
C2 = 32
SLOPE = 0.3
MESH = pl.DeviceIdType.MESH
F32 = jnp.float32
BF16 = jnp.bfloat16
DIRS = [(dx, dy) for dx in (-1, 0, 1) for dy in (-1, 0, 1) if (dx, dy) != (0, 0)]


def spans(delta, size, width):
    if delta == 1:
        return (size - width, width), (0, width)
    if delta == -1:
        return (0, width), (size + width, width)
    return (0, size), (width, size)


def leaky(values):
    return jnp.where(values > 0, values, SLOPE * values)


def shifted(values, lane, last):
    before = jnp.where(lane == 0, 0.0, pltpu.roll(values, 1, axis=1))
    after = jnp.where(lane == last, 0.0, pltpu.roll(values, last, axis=1))
    return before, after


def dot(a, b):
    return lax.dot_general(a, b, (((1,), (0,)), ((), ())), preferred_element_type=F32)


def dot_nt(a, b):
    return lax.dot_general(a, b, (((1,), (1,)), ((), ())), preferred_element_type=F32)


def one_hot(rows, source):
    row = lax.broadcasted_iota(jnp.int32, (rows, source.shape[1]), 0)
    return jnp.where(row == source, 1.0, 0.0).astype(BF16)


def one_hot_rows(chans, size_y):
    r = lax.broadcasted_iota(jnp.int32, (chans * size_y, chans * size_y), 0)
    q = lax.broadcasted_iota(jnp.int32, (chans * size_y, chans * size_y), 1)
    return jnp.where(q == (r % chans) * size_y + r // chans, 1.0, 0.0).astype(BF16)


def build_selectors(s1, q2, width1):
    lane = lax.broadcasted_iota(jnp.int32, (1, s1.shape[1]), 1)
    group, rest = lax.div(lane, width1), lax.rem(lane, width1)
    kz, kx, ky, i = lax.div(group, 3), lax.rem(group, 3), lax.div(rest, CIN), lax.rem(rest, CIN)
    s1[...] = one_hot(27 * CIN, jnp.where((group < 9) & (ky < 3), i * 27 + kx * 9 + ky * 3 + kz, -9))
    lane = lax.broadcasted_iota(jnp.int32, (1, 256), 1)
    kx, ky, i = lane >> 6, (lane >> 4) & 3, lane & 15
    source = jnp.where((kx < 3) & (ky < 3), i * 27 + kx * 9 + ky * 3, -9)
    for kz in range(3):
        q2[:, 256 * kz : 256 * kz + 256] = one_hot(27 * C1, source + kz)


def build_order(s2):
    lane = lax.broadcasted_iota(jnp.int32, (1, s2.shape[1]), 1)
    tap, i = lane >> 4, lane & 15
    ky, kz, kx = lax.div(tap, 9), lax.rem(lax.div(tap, 3), 3), lax.rem(tap, 3)
    s2[...] = one_hot(27 * C1, jnp.where(tap < 27, i * 27 + kx * 9 + ky * 3 + kz, -9))


def split_rows(flat_ref, rows_ref):
    rows, unit = rows_ref.shape
    flat = flat_ref[...].astype(F32).reshape(1, rows * unit)
    rows_ref[...] = jnp.concatenate(
        [flat[:, unit * k : unit * (k + 1)] for k in range(rows)], axis=0).astype(BF16)


def flatten(rows):
    return jnp.concatenate([rows[k : k + 1] for k in range(rows.shape[0])], axis=1).reshape(rows.size)


def gather_rows(all_ref, rows_ref, wide_ref):
    owners, count, unit = all_ref.shape
    for j in range(owners):
        rows_ref[count * j : count * (j + 1)] = all_ref[j].astype(F32)
    split = wide_ref.shape[1] // unit
    if split == 1:
        return rows_ref[...]
    for k in range(split):
        wide_ref[:, unit * k : unit * (k + 1)] = rows_ref[pl.ds(k, wide_ref.shape[0], stride=split)]
    return wide_ref[...]


def scatter_rows(value, rows_ref, wide_ref, out_ref):
    owners, count, unit = out_ref.shape
    split = value.shape[1] // unit
    if split == 1:
        for j in range(owners):
            out_ref[j] = value[count * j : count * (j + 1)]
        return
    wide_ref[...] = value
    for k in range(split):
        rows_ref[pl.ds(k, value.shape[0], stride=split)] = wide_ref[:, unit * k : unit * (k + 1)]
    for j in range(owners):
        out_ref[j] = rows_ref[count * j : count * (j + 1)]


def split3(g):
    high = g.astype(BF16)
    rest = g - high.astype(F32)
    mid = rest.astype(BF16)
    low = (rest - mid.astype(F32)).astype(BF16)
    return jnp.concatenate([high, mid, low], axis=0)


def pick(g, selector):
    rows = g.shape[0]
    r = dot_nt(split3(g), selector)
    return r[:rows] + r[rows : 2 * rows] + r[2 * rows :]


def fused_kernel(
    n_space, n_samp, v_hbm, c_hbm, f1_hbm, f2_hbm, act_ref, o1_ref, o2_ref,
    v_ref, c_ref, f1_flat, f2_flat, f1_ref, f2_ref, load,
    vp, cp, all1, all2,
    turn, a1, a2, a3, dhid, hid, back, slope1, perm, acc1, acc2, act,
    s1, s2, q2, rows1, wide1, rows2, wide2, vf, vrows,
    grad1, grad2, part1, part2, full2, mine2,
    send_v, recv_v, send_1, recv_1, send_2, recv_2,
    send_a1, recv_a1, send_a2, recv_a2, send_b2, recv_b2,
):
    s = lax.axis_index("space")
    m = lax.axis_index("samp")
    size_x, size_y, size_z = v_ref.shape[1:]
    other = m + 1 - 2 * lax.rem(m, 2)
    chips = n_samp // 2
    turn_sign = 1 - 2 * ((2 * s) // n_space)

    def far(k):
        return lax.rem(2 * n_space + s - turn_sign * k, n_space)

    def across(j):
        return lax.rem(other + 2 * j, n_samp)

    def each_other_far(body):
        if n_space <= 16:
            for k in range(1, n_space):
                body(far(k))
            return

        def step(k, carry):
            body(far(k))
            return carry

        lax.fori_loop(1, n_space, step, 0)

    def there(dx, dy):
        return (s + dx >= 0) & (s + dx < n_space) & (m + dy >= 0) & (m + dy < n_samp)

    barrier = pltpu.get_barrier_semaphore()
    peers = n_samp - 1 + n_space - 1
    @each_other_far
    def _(peer):
        pl.semaphore_signal(barrier, inc=1, device_id=(peer, other), device_id_type=MESH)

    for k in range(1, n_samp):
        pl.semaphore_signal(barrier, inc=1, device_id=(s, lax.rem(m + k, n_samp)), device_id_type=MESH)

    for dx, dy in DIRS:
        if dx == 0:
            continue
        peers = peers + jnp.where(there(dx, dy), 1, 0)

        @pl.when(there(dx, dy))
        def _():
            pl.semaphore_signal(barrier, inc=1, device_id=(s + dx, m + dy), device_id_type=MESH)

    loads = [
        pltpu.make_async_copy(src, dst, load.at[j])
        for j, (src, dst) in enumerate(
            ((f2_hbm, f2_flat), (f1_hbm, f1_flat), (v_hbm, v_ref), (c_hbm, c_ref)))
    ]
    for copy in loads:
        copy.start()
    for dx, dy in DIRS:
        (_, nx), (tx, _) = spans(-dx, size_x, 2)
        (_, ny), (ty, _) = spans(-dy, size_y, 2)

        @pl.when(jnp.logical_not(there(dx, dy)))
        def _():
            vp[tx : tx + nx, ty : ty + ny] = jnp.zeros((nx, ny, CIN, size_z), BF16)

    loads[0].wait()
    split_rows(f2_flat, f2_ref)
    build_order(s2)
    ordered = f2_ref.shape[1] == 27 * C1
    if ordered:
        f2_ref[...] = dot(f2_ref[...], s2[...])[:, : 27 * C1].astype(BF16)
    loads[1].wait()
    split_rows(f1_flat, f1_ref)
    turn_v = one_hot_rows(CIN, size_y)
    loads[2].wait()

    def centre(x, carry):
        value = v_ref[:, x].astype(F32).reshape(CIN * size_y, size_z).astype(BF16)
        value = dot(turn_v, value)
        vf[x + 2, 2 * CIN : (2 + size_y) * CIN] = value
        for y in range(size_y):
            vp[x + 2, y + 2] = value[CIN * y : CIN * (y + 1)].astype(BF16)
        return carry

    lax.fori_loop(0, size_x, centre, 0)
    pl.semaphore_wait(barrier, peers)

    def copy_1(k):
        return pltpu.make_async_remote_copy(
            src_ref=f1_ref, dst_ref=all1.at[m], send_sem=send_1.at[k], recv_sem=recv_1.at[k],
            device_id=(s, lax.rem(m + k, n_samp)), device_id_type=MESH)

    def copy_2(peer):
        return pltpu.make_async_remote_copy(
            src_ref=f2_ref, dst_ref=all2.at[s], send_sem=send_2, recv_sem=recv_2.at[s],
            device_id=(peer, other), device_id_type=MESH)

    def await_2(peer):
        pltpu.make_async_copy(all2.at[peer], all2.at[peer], recv_2.at[peer]).wait()

    def halo(src, dst, width, send, recv, slot, dx, dy):
        (sx, nx), (tx, _) = spans(dx, size_x, width)
        (sy, ny), (ty, _) = spans(dy, size_y, width)
        return pltpu.make_async_remote_copy(
            src_ref=src.at[pl.ds(sx + width, nx), pl.ds(sy + width, ny)], dst_ref=dst.at[pl.ds(tx, nx), pl.ds(ty, ny)],
            send_sem=send.at[slot], recv_sem=recv.at[slot],
            device_id=(jnp.clip(s + dx, 0, n_space - 1), jnp.clip(m + dy, 0, n_samp - 1)),
            device_id_type=MESH)

    vol = [halo(vp, vp, 2, send_v, recv_v, j, dx, dy) for j, (dx, dy) in enumerate(DIRS)]
    @each_other_far
    def _(peer):
        copy_2(peer).start()

    for k in range(1, n_samp):
        copy_1(k).start()
    for copy, (dx, dy) in zip(vol, DIRS):
        @pl.when(there(dx, dy))
        def _():
            copy.start()

    all1[m] = f1_ref[...]
    all2[s] = f2_ref[...]
    last = size_z - 1
    high_y = size_y + 2

    def lanes(rows):
        return lax.broadcasted_iota(jnp.int32, (rows, size_z), 1)

    width1 = CIN * (size_y + 4)
    build_selectors(s1, q2, width1)
    turn[...] = one_hot_rows(C2, size_y)
    loads[3].wait()

    def turn_c(x, carry):
        value = c_ref[:, x].astype(F32).reshape(C2 * size_y, size_z).astype(BF16)
        cp[x] = dot(turn[...], value).astype(BF16)
        return carry

    lax.fori_loop(0, size_x, turn_c, 0)

    acc1[...] = jnp.zeros_like(acc1)
    acc2[...] = jnp.zeros_like(acc2)

    def arrive(width):
        for copy, (dx, dy) in zip(vol, DIRS):
            if abs(dx) != width:
                continue

            @pl.when(there(-dx, -dy))
            def _():
                copy.wait_recv()

    for k in range(1, n_samp):
        copy_1(k).wait_recv()
    base1 = dot(gather_rows(all1, rows1, wide1).astype(BF16), s1[...])
    for y in range(high_y):
        row = base1 if y == 0 else pltpu.roll(base1, CIN * y, axis=1)
        a1[C1 * y : C1 * (y + 1)] = row[:, : 9 * width1].astype(BF16)

    lane_v = lanes(width1)
    lane_h = lanes(C1 * high_y)
    lane_b = lanes(C2 * 4)
    first_row = jnp.where(m > 0, 1.0, 0.0)
    last_row = jnp.where(m < n_samp - 1, 1.0, 0.0)

    def lift(x, rows):
        for y in rows:
            vf[x, CIN * y : CIN * (y + 1)] = vp[x, y].astype(F32)
        value = vf[x]
        before, after = shifted(value, lane_v, last)
        vrows[0, x] = before.astype(BF16)
        vrows[1, x] = value.astype(BF16)
        vrows[2, x] = after.astype(BF16)

    def vwin(x):
        return jnp.concatenate([vrows[kz, x + kx] for kz in range(3) for kx in range(3)], axis=0)

    def layer1(x):
        p = dot(a1[...], vwin(x))
        slope = jnp.where(p > 0, 1.0, SLOPE)
        if x == 0:
            slope = slope * jnp.where(s > 0, 1.0, 0.0)
        if x == size_x + 1:
            slope = slope * jnp.where(s < n_space - 1, 1.0, 0.0)
        slope = jnp.concatenate(
            [slope[:C1] * first_row, slope[C1 : C1 * (high_y - 1)], slope[C1 * (high_y - 1) :] * last_row], axis=0)
        slope1[x] = slope
        h = p * slope
        before, after = shifted(h, lane_h, last)
        hid[0, x] = before.astype(BF16)
        hid[1, x] = h.astype(BF16)
        hid[2, x] = after.astype(BF16)

    edge_rows = (0, 1, size_y + 2, size_y + 3)
    arrive(0)
    for x in range(2, size_x + 2):
        lift(x, edge_rows)
    for x in range(2, size_x):
        layer1(x)
    arrive(1)
    for x in (0, 1, size_x + 2, size_x + 3):
        lift(x, range(size_y + 4))
    for x in (0, 1, size_x, size_x + 1):
        layer1(x)

    each_other_far(await_2)
    base2 = gather_rows(all2, rows2, wide2)
    base2 = base2 if ordered else dot(base2.astype(BF16), s2[...])[:, : 27 * C1]
    base2 = jnp.concatenate([base2, jnp.zeros((C2, 896 - 27 * C1), F32)], axis=1)
    for y in range(4):
        row = base2 if y == 0 else pltpu.roll(base2, 9 * C1 * y, axis=1)
        a2[C2 * y : C2 * (y + 1)] = row[:, : 54 * C1].astype(BF16)

    for x in range(size_x):
        for half in range(size_y // 4):
            rows = slice(128 * half, 128 * half + 128)
            win = jnp.concatenate(
                [hid[kz, x + kx, 64 * half + C1 * y : 64 * half + C1 * (y + 1)]
                 for y in range(6) for kz in range(3) for kx in range(3)], axis=0)
            p = dot(a2[...], win)
            slope = jnp.where(p > 0, 1.0, SLOPE)
            act[x, rows] = (p * slope).astype(BF16)
            b = (cp[x, rows].astype(F32) * slope).astype(BF16)
            before, after = shifted(b.astype(F32), lane_b, last)
            back[0, x, rows] = after.astype(BF16)
            back[1, x, rows] = b
            back[2, x, rows] = before.astype(BF16)

    for x in range(size_x):
        moved, windows = [], []
        for y in range(0, size_y, 2):
            moved.append(jnp.concatenate([back[kz, x, C2 * y : C2 * y + 64] for kz in range(3)], axis=0))
            windows.append(jnp.concatenate([hid[1, x + kx, C1 * y : C1 * y + 64] for kx in range(3)], axis=0))
        acc2[...] += dot_nt(jnp.concatenate(moved, axis=1), jnp.concatenate(windows, axis=1))

    shares = []
    for kz in range(3):
        low = jnp.concatenate([acc2[64 * kz : 64 * kz + C2], jnp.zeros((C2, 64), F32)], axis=1)
        high = jnp.concatenate([acc2[64 * kz + C2 : 64 * kz + 64], jnp.zeros((C2, 64), F32)], axis=1)
        shares.append(low + pltpu.roll(high, 256 - C1, axis=1))
    scatter_rows(pick(jnp.concatenate(shares, axis=1), q2[...]), rows2, wide2, grad2)

    def spread_2(peer):
        pltpu.make_async_remote_copy(
            src_ref=grad2.at[peer], dst_ref=part2.at[s], send_sem=send_a2, recv_sem=recv_a2,
            device_id=(peer, other), device_id_type=MESH).start()

    each_other_far(spread_2)
    spread_2(s)

    tall = jnp.concatenate([base2[:, :512], jnp.zeros((128 - C2, 512), F32)], axis=0).T
    lane_t = lax.broadcasted_iota(jnp.int32, (C1, 128), 1)
    for kx in range(3):
        for kz in range(3):
            tile = 0.0
            for y in range(3):
                first = C1 * (9 * (2 - y) + 3 * kz + kx)
                piece = tall[first : first + C1]
                tile = tile + (piece if y == 0 else pltpu.roll(piece, C2 * y, axis=1))
            turns = [tile] + [pltpu.roll(tile, C2 * r, axis=1) for r in range(1, 4)]
            for y in range(6):
                turned = turns[(y + 2) % 4]
                if y < 2:
                    turned = jnp.where(lane_t < C2 * (y + 2), turned, 0.0)
                elif y > 3:
                    turned = jnp.where(lane_t >= C2 * (y - 2), turned, 0.0)
                first = C1 * (6 * kx + y)
                a3[first : first + C1, 128 * kz : 128 * kz + 128] = turned.astype(BF16)

    span = C1 * 6
    for x in range(size_x):
        halves = []
        for half in range(size_y // 4):
            win = jnp.concatenate([back[kz, x, 128 * half : 128 * half + 128] for kz in range(3)], axis=0)
            halves.append(dot(a3[...], win))
        for kx in range(3):
            low, high = (d[span * kx : span * (kx + 1)] for d in halves)
            share = jnp.concatenate([low[:64], low[64:] + high[:32], high[32:]], axis=0)
            if x == 0 or kx == 2:
                dhid[x + kx] = share
            else:
                dhid[x + kx] += share
    for x in range(0, size_x + 2, 2):
        pair = [(dhid[x + k] * slope1[x + k]).astype(BF16) for k in range(2)]
        share = dot_nt(jnp.concatenate(pair, axis=1), jnp.concatenate([vwin(x), vwin(x + 1)], axis=1))
        if x == 0:
            acc1[:, : 9 * width1] = share
        else:
            acc1[:, : 9 * width1] += share

    total1 = acc1[:C1]
    for y in range(1, high_y):
        total1 = total1 + pltpu.roll(acc1[C1 * y : C1 * (y + 1)], acc1.shape[1] - CIN * y, axis=1)
    scatter_rows(pick(total1, s1[...]), rows1, wide1, grad1)

    everyone = n_space * n_samp
    me = s * n_samp + m

    def to_one(ps, pm):
        pltpu.make_async_remote_copy(
            src_ref=grad1.at[pm], dst_ref=part1.at[me], send_sem=send_a1, recv_sem=recv_a1,
            device_id=(ps, pm), device_id_type=MESH).start()

    for start in (0, 1):
        @each_other_far
        def _(peer):
            for j in reversed(range(start, n_samp, 2)):
                to_one(peer, lax.rem(m + j, n_samp))

    for k in range(1, n_samp):
        to_one(s, lax.rem(m + k, n_samp))

    r = lax.broadcasted_iota(jnp.int32, (C2 * size_y, C2 * size_y), 0)
    q = lax.broadcasted_iota(jnp.int32, (C2 * size_y, C2 * size_y), 1)
    from_row = (r % size_y) * C2 + r // size_y
    perm[...] = jnp.where(q == from_row, 1.0, 0.0).astype(BF16)

    def send_act(x, carry):
        value = dot(perm[...], act[x])
        act_ref[:, x] = value.reshape(C2, size_y, size_z).astype(BF16)
        return carry

    lax.fori_loop(0, size_x, send_act, 0)
    part1[me] = grad1[m]
    pltpu.make_async_copy(part2, part2, recv_a2).wait()
    mine2[...] = jnp.sum(part2[...], axis=0)
    for k in range(n_samp - 1, 0, -1):
        pltpu.make_async_remote_copy(
            src_ref=mine2, dst_ref=full2.at[m], send_sem=send_b2, recv_sem=recv_b2,
            device_id=(s, lax.rem(m + k, n_samp)), device_id_type=MESH).start()
    full2[m] = mine2[...]
    rest = full2.at[pl.ds(0, n_samp - 1)]
    for k in range(1, n_samp):
        copy_1(k).wait_send()
    for copy, (dx, dy) in zip(vol, DIRS):
        @pl.when(there(dx, dy))
        def _():
            copy.wait_send()
    sent = all2.at[pl.ds(0, n_space - 1)]
    pltpu.make_async_copy(sent, sent, send_2).wait()
    pltpu.make_async_copy(part2, part2, send_a2).wait()
    pltpu.make_async_copy(rest, rest, send_b2).wait()
    pltpu.make_async_copy(rest, rest, recv_b2).wait()
    o2_ref[...] = jnp.sum(full2[...], axis=0)
    others = part1.at[pl.ds(0, everyone - 1)]
    pltpu.make_async_copy(others, others, send_a1).wait()
    pltpu.make_async_copy(others, others, recv_a1).wait()
    o1_ref[...] = jnp.sum(part1[...], axis=0)


def store_kernel(scale, act, o1, o2, act_out, o1_out, o2_out, flat1, flat2, done):
    pieces = done.shape[0] - 2
    step = C2 // pieces
    copies = [
        pltpu.make_async_copy(act.at[pl.ds(step * j, step)], act_out.at[pl.ds(step * j, step)], done.at[j + 2])
        for j in range(pieces)
    ]
    copies.append(pltpu.make_async_copy(flat1, o1_out, done.at[0]))
    copies.append(pltpu.make_async_copy(flat2, o2_out, done.at[1]))
    for copy in copies[:pieces]:
        copy.start()
    flat2[...] = flatten(o2[...] * scale)
    copies[-1].start()
    flat1[...] = flatten(o1[...] * scale)
    copies[-2].start()
    for copy in copies:
        copy.wait()


VMEM = pl.BlockSpec(memory_space=pltpu.VMEM)
HBM = pl.BlockSpec(memory_space=pltpu.HBM)


def on_device(n_space, n_samp, volume, filters_one, filters_two, cotangent):
    _, size_x, size_y, size_z = volume.shape
    len1 = filters_one.shape[0]
    len2 = filters_two.shape[0]
    unit1 = math.gcd(len1, 27 * CIN)
    unit2 = math.gcd(len2, 27 * C1)
    piece1 = (len1 // unit1, unit1)
    piece2 = (len2 // unit2, unit2)
    high_y = size_y + 2
    width1 = CIN * (size_y + 4)
    scale = 1.0 / math.sqrt(float(size_x * n_space * size_y * n_samp * size_z))
    samp, space = pltpu.SemaphoreType.DMA((n_samp,)), pltpu.SemaphoreType.DMA((n_space,))
    sides, one = pltpu.SemaphoreType.DMA((8,)), pltpu.SemaphoreType.DMA
    activation, out1, out2 = pl.pallas_call(
        functools.partial(fused_kernel, n_space, n_samp),
        out_shape=[
            jax.ShapeDtypeStruct((C2, size_x, size_y, size_z), BF16),
            jax.ShapeDtypeStruct(piece1, F32),
            jax.ShapeDtypeStruct(piece2, F32),
        ],
        in_specs=[HBM] * 4,
        out_specs=[VMEM] * 3,
        scratch_shapes=[
            pltpu.VMEM(volume.shape, BF16),
            pltpu.VMEM(cotangent.shape, BF16),
            pltpu.VMEM((len1,), BF16),
            pltpu.VMEM((len2,), BF16),
            pltpu.VMEM(piece1, BF16),
            pltpu.VMEM(piece2, BF16),
            pltpu.SemaphoreType.DMA((4,)),
            pltpu.VMEM((size_x + 4, size_y + 4, CIN, size_z), BF16),
            pltpu.VMEM((size_x, C2 * size_y, size_z), BF16),
            pltpu.VMEM((n_samp, *piece1), BF16),
            pltpu.VMEM((n_space, *piece2), BF16),
            pltpu.VMEM((C2 * size_y, C2 * size_y), BF16),
            pltpu.VMEM((C1 * high_y, 9 * width1), BF16),
            pltpu.VMEM((C2 * 4, 9 * C1 * 6), BF16),
            pltpu.VMEM((18 * C1, 12 * C2), BF16),
            pltpu.VMEM((size_x + 2, C1 * high_y, size_z), F32),
            pltpu.VMEM((3, size_x + 2, C1 * high_y, size_z), BF16),
            pltpu.VMEM((3, size_x, C2 * size_y, size_z), BF16),
            pltpu.VMEM((size_x + 2, C1 * high_y, size_z), F32),
            pltpu.VMEM((C2 * size_y, C2 * size_y), BF16),
            pltpu.VMEM((C1 * high_y, 512), F32),
            pltpu.VMEM((192, 192), F32),
            pltpu.VMEM((size_x, C2 * size_y, size_z), BF16),
            pltpu.VMEM((27 * CIN, 512), BF16),
            pltpu.VMEM((27 * C1, 512), BF16),
            pltpu.VMEM((27 * C1, 768), BF16),
            pltpu.VMEM((n_samp * piece1[0], piece1[1]), F32),
            pltpu.VMEM((C1, 27 * CIN), F32),
            pltpu.VMEM((n_space * piece2[0], piece2[1]), F32),
            pltpu.VMEM((C2, 27 * C1), F32),
            pltpu.VMEM((size_x + 4, width1, size_z), F32),
            pltpu.VMEM((3, size_x + 4, width1, size_z), BF16),
            pltpu.VMEM((n_samp, *piece1), F32),
            pltpu.VMEM((n_space, *piece2), F32),
            pltpu.VMEM((n_space * n_samp, *piece1), F32),
            pltpu.VMEM((n_space, *piece2), F32),
            pltpu.VMEM((n_samp, *piece2), F32),
            pltpu.VMEM(piece2, F32),
            sides, sides, samp, samp, one, space,
            one, one, one, one, one, one,
        ],
        compiler_params=pltpu.CompilerParams(
            collective_id=0, has_side_effects=True, vmem_limit_bytes=48 * 2**20),
    )(*(pltpu.with_memory_space_constraint(x, pltpu.HBM)
        for x in (volume, cotangent, filters_one, filters_two)))
    return pl.pallas_call(
        functools.partial(store_kernel, scale),
        out_shape=[
            jax.ShapeDtypeStruct(activation.shape, BF16),
            jax.ShapeDtypeStruct((len1,), F32),
            jax.ShapeDtypeStruct((len2,), F32),
        ],
        in_specs=[VMEM] * 3,
        out_specs=[HBM] * 3,
        scratch_shapes=[pltpu.VMEM((len1,), F32), pltpu.VMEM((len2,), F32), pltpu.SemaphoreType.DMA((3,))],
        compiler_params=pltpu.CompilerParams(vmem_limit_bytes=2**20),
    )(activation, out1, out2)


def solution(mesh):
    in_specs = (
        P(None, "space", "samp", None),
        P("samp"),
        P("space"),
        P(None, "space", "samp", None),
    )
    out_specs = (P(None, "space", "samp", None), P("samp"), P("space"))
    return jax.shard_map(
        functools.partial(on_device, mesh.shape["space"], mesh.shape["samp"]),
        mesh=mesh, in_specs=in_specs, out_specs=out_specs, check_vma=False,
    )
```
